512 devices in a mesh: dp: 4 (over x), ctx: 32 (over y_lo, z, core), tp: 4 (over y_hi).
Axes of the slice: x: 4, y: 8 (y_hi: 4, y_lo: 2; y = y_hi * 2 + y_lo), z: 8, core: 2. Of those that a mesh axis runs over, the one named last changes fastest.
Arguments:
- hyena_features: bfloat16 [3, 32768, 4096], P(None, ('dp', 'ctx'), 'tp'), parts along dimension 1, may hold values from -6 to 6
- short_filter: float32 [3, 3, 4096], P(None, None, 'tp'), may hold values from -3.5 to 3.5
- long_filter: float32 [128, 4096], P(None, 'tp'), may hold values from -0.5 to 0.5
- att_query: bfloat16 [32768, 4096], P(('dp', 'ctx'), 'tp'), parts along dimension 0, may hold values from -10 to 10
- att_key: bfloat16 [32768, 4096], P(('dp', 'ctx'), 'tp'), parts along dimension 0, may hold values from -10 to 10
Outputs:
- hyena_mixed: bfloat16 [32768, 4096], P(('dp', 'ctx'), 'tp'), parts along dimension 0
- attended: bfloat16 [32768, 4096], P(('dp', 'ctx'), 'tp'), parts along dimension 0
The draws below stay inside these ranges and needn't reach their ends.
There are 4 independent parts, one for each index of `dp`. The reference program is written for one: setup_inputs(seed, part) draws one part's arguments, and reference() takes and returns one part's arrays. A program takes and returns all parts, laid end to end along the dimension named above; an argument that names none is the same for every part. Nothing has to cross between parts.
All inputs are finite; a program needn't handle non-finite values.
Results may differ from the reference program's by a relative error of at most 0.0063.
Values may be sent and summed in bfloat16 or wider, within the bound.
A program may use at most 64 MiB of HBM per device.

```python
import math
import jax
import jax.numpy as jnp
from jax import lax

CHANNELS = 4096
HEADS = 32
HEAD_DIM = 128
TAPS = 128
SHORT_TAPS = 3
WINDOW_BLOCKS = 4
TOK_DEV = 256
TOKENS = 8192
N_CTX = 32


def base_values(key, salt):
    shape = (TOKENS, HEADS * HEAD_DIM)
    return jnp.clip(jax.random.normal(jax.random.fold_in(key, salt), shape, jnp.float32), -6.0, 6.0)


def draw_att_query(key, part):
    base = base_values(key, 1)
    return base.astype(jnp.bfloat16)


def draw_att_key(key, part):
    base = base_values(key, 2)
    return base.astype(jnp.bfloat16)


def block_levels(own_key, shape, shards, smallest, largest):
    factor_of = 1.0
    for dim, blocks in shards:
        steps = jax.random.uniform(jax.random.fold_in(jax.random.fold_in(own_key, 6), dim), (blocks,), jnp.float32, smallest / len(shards), largest / len(shards))
        factor_of = factor_of * jnp.repeat(jnp.exp(steps), shape[dim] // blocks).reshape((-1,) + (1,) * (len(shape) - 1 - dim))
    return factor_of


def bell_draw(rng, extent, spread, most, cuts=(), kind=jnp.bfloat16):
    values = spread * jax.random.normal(rng, extent, jnp.float32)
    if cuts:
        values = values * block_levels(rng, extent, cuts, -0.22, 0.18)
    return jnp.clip(values, -most, most).astype(kind)


def setup_inputs(seed: int = 0, part: int = 0) -> dict:
    keys = jax.random.split(jax.random.key(seed), 6)
    part_splits = jax.random.split(jax.random.fold_in(keys[5], part), 6)
    return {
        "hyena_features": bell_draw(part_splits[0], (3, TOKENS, CHANNELS), 1.0, 6.0, ((1, 32), (2, 4))),
        "short_filter": bell_draw(keys[1], (3, SHORT_TAPS, CHANNELS), SHORT_TAPS ** -0.5, 3.5, ((2, 4),), jnp.float32),
        "long_filter": bell_draw(keys[2], (TAPS, CHANNELS), TAPS ** -0.5, 0.5, ((1, 4),), jnp.float32),
        "att_query": draw_att_query(jax.random.fold_in(jax.random.fold_in(keys[5], part), 71), part),
        "att_key": draw_att_key(jax.random.fold_in(jax.random.fold_in(keys[5], part), 71), part),
    }


def short_mix(rows, weights):
    return weights[0] * rows[2:] + weights[1] * rows[1:-1] + weights[2] * rows[:-2]

def attend_block(query_rows, window_keys, window_values, block_index):
    row_count = query_rows.shape[0]
    key_count = window_keys.shape[0]
    query_heads = query_rows.astype(jnp.float32).reshape(row_count, HEADS, HEAD_DIM)
    key_heads = window_keys.astype(jnp.float32).reshape(key_count, HEADS, HEAD_DIM)
    value_heads = window_values.astype(jnp.float32).reshape(key_count, HEADS, HEAD_DIM)
    scores = jnp.einsum('thd,shd->hts', query_heads, key_heads) * (1.0 / math.sqrt(HEAD_DIM))
    query_pos = block_index * row_count + jnp.arange(row_count, dtype=jnp.int32)[:, None]
    key_pos = (block_index - WINDOW_BLOCKS + 1) * row_count + jnp.arange(key_count, dtype=jnp.int32)[None, :]
    visible = (key_pos >= 0) & (key_pos <= query_pos)
    masked = jnp.where(visible[None], scores, -jnp.inf)
    row_peak = lax.optimization_barrier(jnp.max(masked, axis=-1, keepdims=True))
    weights = jnp.exp(masked - row_peak)
    row_total = lax.optimization_barrier(jnp.sum(weights, axis=-1))
    weights_b = weights.astype(jnp.bfloat16).astype(jnp.float32)
    mixed = jnp.einsum('hts,shd->thd', weights_b, value_heads)
    result = mixed / jnp.transpose(row_total)[:, :, None]
    return result.astype(jnp.bfloat16).reshape(row_count, HEADS * HEAD_DIM)

def reference(hyena_features, short_filter, long_filter, att_query, att_key):
    blank = jnp.zeros((2, CHANNELS), jnp.float32)

    def featurize(which):
        padded = jnp.concatenate([blank, hyena_features[which].astype(jnp.float32)], 0)
        return short_mix(padded, short_filter[which])
    q_mix = featurize(0)
    k_mix = featurize(1)
    v_mix = featurize(2)
    product = (k_mix * v_mix).astype(jnp.bfloat16)
    product = lax.optimization_barrier(product)
    padded_product = jnp.concatenate([jnp.zeros((TAPS - 1, CHANNELS), jnp.float32), product.astype(jnp.float32)], 0)

    def add_tap(tap, accum):
        return accum + long_filter[tap] * lax.dynamic_slice_in_dim(padded_product, TAPS - 1 - tap, TOKENS, 0)
    filtered = lax.fori_loop(0, TAPS, add_tap, jnp.zeros((TOKENS, CHANNELS), jnp.float32))
    hyena_mixed = (q_mix * filtered).astype(jnp.bfloat16)
    pad_rows = (WINDOW_BLOCKS - 1) * TOK_DEV
    empty_rows = jnp.zeros((pad_rows, HEADS * HEAD_DIM), jnp.bfloat16)
    padded_key = jnp.concatenate([empty_rows, att_key], 0)
    padded_value = jnp.concatenate([empty_rows, hyena_mixed], 0)

    def one_block(block_index):
        start = (block_index * TOK_DEV).astype(jnp.int32)
        query_rows = lax.dynamic_slice_in_dim(att_query, start, TOK_DEV, 0)
        window_keys = lax.dynamic_slice_in_dim(padded_key, start, WINDOW_BLOCKS * TOK_DEV, 0)
        window_values = lax.dynamic_slice_in_dim(padded_value, start, WINDOW_BLOCKS * TOK_DEV, 0)
        return attend_block(query_rows, window_keys, window_values, block_index)
    attended = lax.map(one_block, jnp.arange(N_CTX, dtype=jnp.int32)).reshape(TOKENS, HEADS * HEAD_DIM)
    return (hyena_mixed, attended)
```

```python
import math

import jax
import jax.numpy as jnp
from jax import lax
from jax.sharding import PartitionSpec as P

HEAD_DIM = 128
WINDOW_BLOCKS = 4


def shift_pairs(count, pairs):
    return [(s, t) for s, t in pairs if 0 <= s < count and 0 <= t < count]


def from_behind(value, axis, steps):
    count = lax.axis_size(axis)
    return lax.ppermute(
        value, axis, shift_pairs(count, [(s, s + steps) for s in range(count)])
    )


def window_blocks(block, axis):
    count = lax.axis_size(axis)
    two_back = lax.ppermute(block, axis, shift_pairs(count, [(s, s + 2) for s in range(count)]))
    sibling_own = lax.ppermute(
        block, axis, shift_pairs(count, [(s, s + 1) for s in range(0, count, 2)])
    )
    swapped = lax.ppermute(
        two_back,
        axis,
        shift_pairs(count, [(s, s ^ 1) for s in range(count)]),
    )
    forwarded = lax.ppermute(
        two_back, axis, shift_pairs(count, [(s, s + 1) for s in range(1, count, 2)])
    )
    odd = lax.rem(lax.axis_index(axis), 2) == 1
    one_back = jnp.where(odd, sibling_own, swapped)
    three_back = jnp.where(odd, swapped, forwarded)
    return [three_back, two_back, one_back]


def short_mix(rows, weights):
    return weights[0] * rows[2:] + weights[1] * rows[1:-1] + weights[2] * rows[:-2]


def attend_block(query_rows, window_keys, window_values, block_index):
    row_count = query_rows.shape[0]
    key_count = window_keys.shape[0]
    head_count = query_rows.shape[1] // HEAD_DIM
    query_heads = query_rows.reshape(row_count, head_count, HEAD_DIM)
    key_heads = window_keys.reshape(key_count, head_count, HEAD_DIM)
    value_heads = window_values.reshape(key_count, head_count, HEAD_DIM)
    scores = jnp.einsum(
        "thd,shd->hts", query_heads, key_heads, preferred_element_type=jnp.float32
    ) * (1.0 / math.sqrt(HEAD_DIM))
    query_pos = block_index * row_count + jnp.arange(row_count, dtype=jnp.int32)[:, None]
    key_pos = (block_index - WINDOW_BLOCKS + 1) * row_count + jnp.arange(
        key_count, dtype=jnp.int32
    )[None, :]
    visible = (key_pos >= 0) & (key_pos <= query_pos)
    masked = jnp.where(visible[None], scores, -jnp.inf)
    row_peak = jnp.max(masked, axis=-1, keepdims=True)
    weights = jnp.exp(masked - row_peak)
    row_total = jnp.sum(weights, axis=-1)
    mixed = jnp.einsum(
        "hts,shd->thd",
        weights.astype(jnp.bfloat16),
        value_heads,
        preferred_element_type=jnp.float32,
    )
    result = mixed / jnp.transpose(row_total)[:, :, None]
    return result.astype(jnp.bfloat16).reshape(row_count, head_count * HEAD_DIM)


def body(hyena_features, short_filter, long_filter, att_query, att_key):
    tap_count = long_filter.shape[0]
    channel_count = long_filter.shape[1]
    key_blocks = window_blocks(att_key, "ctx")
    q_raw = hyena_features[0]
    k_raw = hyena_features[1]
    v_raw = hyena_features[2]
    edge_rows = jnp.concatenate(
        [q_raw[-2:], k_raw[-(tap_count + 1) :], v_raw[-(tap_count + 1) :]], 0
    )
    received = from_behind(edge_rows, "ctx", 1)
    q_ext = jnp.concatenate([received[:2], q_raw], 0).astype(jnp.float32)
    k_ext = jnp.concatenate([received[2 : tap_count + 3], k_raw], 0).astype(jnp.float32)
    v_ext = jnp.concatenate([received[tap_count + 3 :], v_raw], 0).astype(jnp.float32)
    q_mix = short_mix(q_ext, short_filter[0])
    product_ext = (short_mix(k_ext, short_filter[1]) * short_mix(v_ext, short_filter[2])).astype(
        jnp.bfloat16
    )
    product_ext = lax.optimization_barrier(product_ext)
    kernel = long_filter[::-1][:, None, :]
    filtered = lax.conv_general_dilated(
        product_ext.astype(jnp.float32)[None],
        kernel,
        (1,),
        "VALID",
        dimension_numbers=("NWC", "WIO", "NWC"),
        feature_group_count=channel_count,
        precision=lax.Precision.HIGHEST,
    )[0]
    hyena_mixed = (q_mix * filtered).astype(jnp.bfloat16)
    value_blocks = window_blocks(hyena_mixed, "ctx")
    window_k = jnp.concatenate(key_blocks + [att_key], 0)
    window_v = jnp.concatenate(value_blocks + [hyena_mixed], 0)
    attended = attend_block(att_query, window_k, window_v, lax.axis_index("ctx"))
    return (hyena_mixed, attended)


def solution(mesh):
    return jax.shard_map(
        body,
        mesh=mesh,
        in_specs=(
            P(None, ("dp", "ctx"), "tp"),
            P(None, None, "tp"),
            P(None, "tp"),
            P(("dp", "ctx"), "tp"),
            P(("dp", "ctx"), "tp"),
        ),
        out_specs=(P(("dp", "ctx"), "tp"), P(("dp", "ctx"), "tp")),
        check_vma=False,
    )
```

```python
import math

import jax
import jax.numpy as jnp
from jax import lax
from jax.sharding import PartitionSpec as P

HEAD_DIM = 128
WINDOW_BLOCKS = 4


def shift_pairs(count, pairs):
    return [(s, t) for s, t in pairs if 0 <= s < count and 0 <= t < count]


def from_behind(value, axis, steps):
    count = lax.axis_size(axis)
    return lax.ppermute(
        value, axis, shift_pairs(count, [(s, s + steps) for s in range(count)])
    )


def window_blocks(block, axis):
    count = lax.axis_size(axis)
    two_back = lax.ppermute(block, axis, shift_pairs(count, [(s, s + 2) for s in range(count)]))
    sibling_own = lax.ppermute(
        block, axis, shift_pairs(count, [(s, s + 1) for s in range(0, count, 2)])
    )
    swapped = lax.ppermute(
        two_back,
        axis,
        shift_pairs(count, [(s, s ^ 1) for s in range(count)]),
    )
    forwarded = lax.ppermute(
        two_back, axis, shift_pairs(count, [(s, s + 1) for s in range(1, count, 2)])
    )
    odd = lax.rem(lax.axis_index(axis), 2) == 1
    one_back = jnp.where(odd, sibling_own, swapped)
    three_back = jnp.where(odd, swapped, forwarded)
    return [three_back, two_back, one_back]


def short_mix(rows, weights):
    return weights[0] * rows[2:] + weights[1] * rows[1:-1] + weights[2] * rows[:-2]


def attend_block(query_rows, window_keys, window_values, block_index):
    row_count = query_rows.shape[0]
    key_count = window_keys.shape[0]
    head_count = query_rows.shape[1] // HEAD_DIM
    query_heads = query_rows.reshape(row_count, head_count, HEAD_DIM)
    key_heads = window_keys.reshape(key_count, head_count, HEAD_DIM)
    value_heads = window_values.reshape(key_count, head_count, HEAD_DIM)
    scores = jnp.einsum(
        "thd,shd->hts", query_heads, key_heads, preferred_element_type=jnp.float32
    ) * (1.0 / math.sqrt(HEAD_DIM))
    query_pos = block_index * row_count + jnp.arange(row_count, dtype=jnp.int32)[:, None]
    key_pos = (block_index - WINDOW_BLOCKS + 1) * row_count + jnp.arange(
        key_count, dtype=jnp.int32
    )[None, :]
    visible = (key_pos >= 0) & (key_pos <= query_pos)
    masked = jnp.where(visible[None], scores, -jnp.inf)
    row_peak = jnp.max(masked, axis=-1, keepdims=True)
    weights = jnp.exp(masked - row_peak)
    row_total = jnp.sum(weights, axis=-1)
    mixed = jnp.einsum(
        "hts,shd->thd",
        weights.astype(jnp.bfloat16),
        value_heads,
        preferred_element_type=jnp.float32,
    )
    result = mixed / jnp.transpose(row_total)[:, :, None]
    return result.astype(jnp.bfloat16).reshape(row_count, head_count * HEAD_DIM)


def body(hyena_features, short_filter, long_filter, att_query, att_key):
    tap_count = long_filter.shape[0]
    channel_count = long_filter.shape[1]
    q_raw = hyena_features[0]
    k_raw = hyena_features[1]
    v_raw = hyena_features[2]
    row_count = q_raw.shape[0]
    tail = row_count - (tap_count - 1) - 2
    product_tail = (
        short_mix(k_raw[tail:].astype(jnp.float32), short_filter[1])
        * short_mix(v_raw[tail:].astype(jnp.float32), short_filter[2])
    ).astype(jnp.bfloat16)
    edge_rows = jnp.concatenate([q_raw[-2:], k_raw[-2:], v_raw[-2:], product_tail], 0)
    received = from_behind(edge_rows, "ctx", 1)
    received, key_rows = lax.optimization_barrier((received, att_key))
    key_blocks = window_blocks(key_rows, "ctx")
    q_ext = jnp.concatenate([received[0:2], q_raw], 0).astype(jnp.float32)
    k_ext = jnp.concatenate([received[2:4], k_raw], 0).astype(jnp.float32)
    v_ext = jnp.concatenate([received[4:6], v_raw], 0).astype(jnp.float32)
    q_mix = short_mix(q_ext, short_filter[0])
    product = (short_mix(k_ext, short_filter[1]) * short_mix(v_ext, short_filter[2])).astype(
        jnp.bfloat16
    )
    product_ext = jnp.concatenate([received[6:], product], 0)
    product_ext = lax.optimization_barrier(product_ext)
    kernel = long_filter[::-1][:, None, :]
    filtered = lax.conv_general_dilated(
        product_ext.astype(jnp.float32)[None],
        kernel,
        (1,),
        "VALID",
        dimension_numbers=("NWC", "WIO", "NWC"),
        feature_group_count=channel_count,
        precision=lax.Precision.HIGHEST,
    )[0]
    hyena_mixed = (q_mix * filtered).astype(jnp.bfloat16)
    value_blocks = window_blocks(hyena_mixed, "ctx")
    window_k = jnp.concatenate(key_blocks + [att_key], 0)
    window_v = jnp.concatenate(value_blocks + [hyena_mixed], 0)
    attended = attend_block(att_query, window_k, window_v, lax.axis_index("ctx"))
    return (hyena_mixed, attended)


def solution(mesh):
    return jax.shard_map(
        body,
        mesh=mesh,
        in_specs=(
            P(None, ("dp", "ctx"), "tp"),
            P(None, None, "tp"),
            P(None, "tp"),
            P(("dp", "ctx"), "tp"),
            P(("dp", "ctx"), "tp"),
        ),
        out_specs=(P(("dp", "ctx"), "tp"), P(("dp", "ctx"), "tp")),
        check_vma=False,
    )
```

```python
import functools
import math

import jax
import jax.numpy as jnp
from jax import lax
from jax.experimental import pallas as pl
from jax.experimental.pallas import tpu as pltpu
from jax.sharding import PartitionSpec as P

MESH = pl.DeviceIdType.MESH

HEAD_DIM = 128
WINDOW_BLOCKS = 4


def shift_pairs(count, pairs):
    return [(s, t) for s, t in pairs if 0 <= s < count and 0 <= t < count]


def from_behind(value, axis, steps):
    count = lax.axis_size(axis)
    return lax.ppermute(
        value, axis, shift_pairs(count, [(s, s + steps) for s in range(count)])
    )


def window_blocks(block, axis):
    count = lax.axis_size(axis)
    two_back = lax.ppermute(block, axis, shift_pairs(count, [(s, s + 2) for s in range(count)]))
    sibling_own = lax.ppermute(
        block, axis, shift_pairs(count, [(s, s + 1) for s in range(0, count, 2)])
    )
    swapped = lax.ppermute(
        two_back,
        axis,
        shift_pairs(count, [(s, s ^ 1) for s in range(count)]),
    )
    forwarded = lax.ppermute(
        two_back, axis, shift_pairs(count, [(s, s + 1) for s in range(1, count, 2)])
    )
    odd = lax.rem(lax.axis_index(axis), 2) == 1
    one_back = jnp.where(odd, sibling_own, swapped)
    three_back = jnp.where(odd, swapped, forwarded)
    return [three_back, two_back, one_back]


def attend_exchange_kernel(
    count, q_ref, k3_ref, k2_ref, k1_ref, k0_ref, v_ref, out_ref,
    slots, weights, totals, acc, send_sems, recv_sems,
):
    me = lax.axis_index("ctx")
    odd = lax.rem(me, 2) == 1
    rows, width = q_ref.shape
    heads = width // HEAD_DIM
    scale = 1.0 / math.sqrt(HEAD_DIM)

    @pl.when(me < 3)
    def _():
        for slot, first in ((0, 3), (1, 2), (2, 1)):
            @pl.when(me < first)
            def _():
                slots[slot] = jnp.zeros((rows, width), slots.dtype)

    barrier = pltpu.get_barrier_semaphore()
    for step in (-2, -1, 1, 2):
        peer = me + step

        @pl.when((peer >= 0) & (peer < count))
        def _():
            pl.semaphore_signal(barrier, inc=1, device_id={"ctx": peer}, device_id_type=MESH)

    neighbours = (
        (me >= 2).astype(jnp.int32) + (me >= 1).astype(jnp.int32)
        + (me + 1 < count).astype(jnp.int32) + (me + 2 < count).astype(jnp.int32)
    )
    pl.semaphore_wait(barrier, neighbours)

    def send(src, slot, peer, sem):
        return pltpu.make_async_remote_copy(
            src_ref=src, dst_ref=slots.at[slot], send_sem=send_sems.at[sem],
            recv_sem=recv_sems.at[slot], device_id={"ctx": peer}, device_id_type=MESH,
        )

    def incoming(slot):
        return pltpu.make_async_remote_copy(
            src_ref=v_ref, dst_ref=slots.at[slot], send_sem=send_sems.at[0],
            recv_sem=recv_sems.at[slot], device_id={"ctx": me}, device_id_type=MESH,
        )

    far = send(v_ref, 1, me + 2, 0)
    near = send(v_ref, 2, me + 1, 1)

    @pl.when(me + 2 < count)
    def _():
        far.start()

    @pl.when(jnp.logical_not(odd))
    def _():
        near.start()

    def score_head(h, carry):
        cols = pl.ds(pl.multiple_of(h * HEAD_DIM, HEAD_DIM), HEAD_DIM)
        q = q_ref[:, cols]
        parts = []
        for b, k_ref in enumerate((k3_ref, k2_ref, k1_ref, k0_ref)):
            s = lax.dot_general(
                q, k_ref[:, cols], (((1,), (1,)), ((), ())), preferred_element_type=jnp.float32
            ) * scale
            t = lax.broadcasted_iota(jnp.int32, (rows, rows), 0)
            u = lax.broadcasted_iota(jnp.int32, (rows, rows), 1)
            if b == 3:
                visible = u <= t
            else:
                visible = jnp.broadcast_to(me - 3 + b >= 0, (rows, rows))
            parts.append(jnp.where(visible, s, -jnp.inf))
        masked = jnp.concatenate(parts, axis=1)
        peak = jnp.max(masked, axis=1, keepdims=True)
        w = jnp.exp(masked - peak)
        totals[h] = jnp.sum(w, axis=1, keepdims=True)
        weights[h] = w.astype(jnp.bfloat16)
        return carry

    lax.fori_loop(0, heads, score_head, 0)

    def accumulate(block, v_src, first):
        def one_head(h, carry):
            cols = pl.ds(pl.multiple_of(h * HEAD_DIM, HEAD_DIM), HEAD_DIM)
            w = weights[h, :, pl.ds(block * rows, rows)]
            part = jnp.dot(w, v_src[:, cols], preferred_element_type=jnp.float32)
            if first:
                acc[:, cols] = part
            else:
                acc[:, cols] = acc[:, cols] + part
            return carry

        lax.fori_loop(0, heads, one_head, 0)

    accumulate(3, v_ref, True)

    @pl.when(me >= 2)
    def _():
        incoming(1).wait_recv()

    relay_near = send(slots.at[1], 2, me - 1, 2)
    relay_far = send(slots.at[1], 0, me + 1, 3)

    @pl.when(me >= 2)
    def _():
        @pl.when(odd)
        def _():
            relay_near.start()

        @pl.when(jnp.logical_or(jnp.logical_not(odd), me + 1 < count))
        def _():
            relay_far.start()

    accumulate(1, slots.at[1], False)

    @pl.when(me >= 1)
    def _():
        incoming(2).wait_recv()

    accumulate(2, slots.at[2], False)

    @pl.when(me >= 3)
    def _():
        incoming(0).wait_recv()

    accumulate(0, slots.at[0], False)

    def finish(h, carry):
        cols = pl.ds(pl.multiple_of(h * HEAD_DIM, HEAD_DIM), HEAD_DIM)
        out_ref[:, cols] = (acc[:, cols] / totals[h]).astype(out_ref.dtype)
        return carry

    lax.fori_loop(0, heads, finish, 0)

    @pl.when(me + 2 < count)
    def _():
        far.wait_send()

    @pl.when(jnp.logical_not(odd))
    def _():
        near.wait_send()

    @pl.when((me >= 2) & odd)
    def _():
        relay_near.wait_send()

    @pl.when((me >= 2) & jnp.logical_or(jnp.logical_not(odd), me + 1 < count))
    def _():
        relay_far.wait_send()


def attend_exchange(query, key_blocks, values):
    count = lax.axis_size("ctx")
    rows, width = query.shape
    heads = width // HEAD_DIM
    vmem = pl.BlockSpec(memory_space=pltpu.VMEM)
    return pl.pallas_call(
        functools.partial(attend_exchange_kernel, count),
        out_shape=jax.ShapeDtypeStruct((rows, width), jnp.bfloat16),
        in_specs=[vmem] * 6,
        out_specs=vmem,
        scratch_shapes=[
            pltpu.VMEM((3, rows, width), jnp.bfloat16),
            pltpu.VMEM((heads, rows, WINDOW_BLOCKS * rows), jnp.bfloat16),
            pltpu.VMEM((heads, rows, 1), jnp.float32),
            pltpu.VMEM((rows, width), jnp.float32),
            pltpu.SemaphoreType.DMA((4,)),
            pltpu.SemaphoreType.DMA((3,)),
        ],
        compiler_params=pltpu.CompilerParams(
            collective_id=0, has_side_effects=True, vmem_limit_bytes=48 * 1024 * 1024
        ),
    )(query, *key_blocks, values)


def short_mix(rows, weights):
    return weights[0] * rows[2:] + weights[1] * rows[1:-1] + weights[2] * rows[:-2]


def attend_block(query_rows, window_keys, window_values, block_index):
    row_count = query_rows.shape[0]
    key_count = window_keys.shape[0]
    head_count = query_rows.shape[1] // HEAD_DIM
    query_heads = query_rows.reshape(row_count, head_count, HEAD_DIM)
    key_heads = window_keys.reshape(key_count, head_count, HEAD_DIM)
    value_heads = window_values.reshape(key_count, head_count, HEAD_DIM)
    scores = jnp.einsum(
        "thd,shd->hts", query_heads, key_heads, preferred_element_type=jnp.float32
    ) * (1.0 / math.sqrt(HEAD_DIM))
    query_pos = block_index * row_count + jnp.arange(row_count, dtype=jnp.int32)[:, None]
    key_pos = (block_index - WINDOW_BLOCKS + 1) * row_count + jnp.arange(
        key_count, dtype=jnp.int32
    )[None, :]
    visible = (key_pos >= 0) & (key_pos <= query_pos)
    masked = jnp.where(visible[None], scores, -jnp.inf)
    row_peak = jnp.max(masked, axis=-1, keepdims=True)
    weights = jnp.exp(masked - row_peak)
    row_total = jnp.sum(weights, axis=-1)
    mixed = jnp.einsum(
        "hts,shd->thd",
        weights.astype(jnp.bfloat16),
        value_heads,
        preferred_element_type=jnp.float32,
    )
    result = mixed / jnp.transpose(row_total)[:, :, None]
    return result.astype(jnp.bfloat16).reshape(row_count, head_count * HEAD_DIM)


def body(hyena_features, short_filter, long_filter, att_query, att_key):
    tap_count = long_filter.shape[0]
    channel_count = long_filter.shape[1]
    q_raw = hyena_features[0]
    k_raw = hyena_features[1]
    v_raw = hyena_features[2]
    row_count = q_raw.shape[0]
    tail = row_count - (tap_count - 1) - 2
    product_tail = (
        short_mix(k_raw[tail:].astype(jnp.float32), short_filter[1])
        * short_mix(v_raw[tail:].astype(jnp.float32), short_filter[2])
    ).astype(jnp.bfloat16)
    edge_rows = jnp.concatenate([q_raw[-2:], k_raw[-2:], v_raw[-2:], product_tail], 0)
    received = from_behind(edge_rows, "ctx", 1)
    received, key_rows = lax.optimization_barrier((received, att_key))
    key_blocks = window_blocks(key_rows, "ctx")
    q_ext = jnp.concatenate([received[0:2], q_raw], 0).astype(jnp.float32)
    k_ext = jnp.concatenate([received[2:4], k_raw], 0).astype(jnp.float32)
    v_ext = jnp.concatenate([received[4:6], v_raw], 0).astype(jnp.float32)
    q_mix = short_mix(q_ext, short_filter[0])
    product = (short_mix(k_ext, short_filter[1]) * short_mix(v_ext, short_filter[2])).astype(
        jnp.bfloat16
    )
    product_ext = jnp.concatenate([received[6:], product], 0)
    product_ext = lax.optimization_barrier(product_ext)
    kernel = long_filter[::-1][:, None, :]
    filtered = lax.conv_general_dilated(
        product_ext.astype(jnp.float32)[None],
        kernel,
        (1,),
        "VALID",
        dimension_numbers=("NWC", "WIO", "NWC"),
        feature_group_count=channel_count,
        precision=lax.Precision.HIGHEST,
    )[0]
    hyena_mixed = (q_mix * filtered).astype(jnp.bfloat16)
    attended = attend_exchange(att_query, key_blocks + [att_key], hyena_mixed)
    return (hyena_mixed, attended)


def solution(mesh):
    return jax.shard_map(
        body,
        mesh=mesh,
        in_specs=(
            P(None, ("dp", "ctx"), "tp"),
            P(None, None, "tp"),
            P(None, "tp"),
            P(("dp", "ctx"), "tp"),
            P(("dp", "ctx"), "tp"),
        ),
        out_specs=(P(("dp", "ctx"), "tp"), P(("dp", "ctx"), "tp")),
        check_vma=False,
    )
```

```python
import functools
import math

import jax
import jax.numpy as jnp
from jax import lax
from jax.experimental import pallas as pl
from jax.experimental.pallas import tpu as pltpu
from jax.sharding import PartitionSpec as P

MESH = pl.DeviceIdType.MESH

HEAD_DIM = 128
WINDOW_BLOCKS = 4


def attend_exchange_kernel(
    count, q_ref, kw_ref, k0_ref, v_ref, out_ref,
    slots, weights, totals, acc, send_sems, recv_sems,
):
    me = lax.axis_index("ctx")
    odd = lax.rem(me, 2) == 1
    rows, width = q_ref.shape
    heads = width // HEAD_DIM
    scale = 1.0 / math.sqrt(HEAD_DIM)

    @pl.when(me < 3)
    def _():
        for slot, first in ((0, 3), (1, 2), (2, 1)):
            @pl.when(me < first)
            def _():
                slots[slot] = jnp.zeros((rows, width), slots.dtype)

    barrier = pltpu.get_barrier_semaphore()
    for step in (-2, -1, 1, 2):
        peer = me + step

        @pl.when((peer >= 0) & (peer < count))
        def _():
            pl.semaphore_signal(barrier, inc=1, device_id={"ctx": peer}, device_id_type=MESH)

    neighbours = (
        (me >= 2).astype(jnp.int32) + (me >= 1).astype(jnp.int32)
        + (me + 1 < count).astype(jnp.int32) + (me + 2 < count).astype(jnp.int32)
    )
    pl.semaphore_wait(barrier, neighbours)

    def send(src, slot, peer, sem):
        return pltpu.make_async_remote_copy(
            src_ref=src, dst_ref=slots.at[slot], send_sem=send_sems.at[sem],
            recv_sem=recv_sems.at[slot], device_id={"ctx": peer}, device_id_type=MESH,
        )

    def incoming(slot):
        return pltpu.make_async_remote_copy(
            src_ref=v_ref, dst_ref=slots.at[slot], send_sem=send_sems.at[0],
            recv_sem=recv_sems.at[slot], device_id={"ctx": me}, device_id_type=MESH,
        )

    far = send(v_ref, 1, me + 2, 0)
    near = send(v_ref, 2, me + 1, 1)

    @pl.when(me + 2 < count)
    def _():
        far.start()

    @pl.when(jnp.logical_not(odd))
    def _():
        near.start()

    def score_head(h, carry):
        cols = pl.ds(pl.multiple_of(h * HEAD_DIM, HEAD_DIM), HEAD_DIM)
        q = q_ref[:, cols]
        parts = []
        for b, k_ref in enumerate((kw_ref.at[0], kw_ref.at[1], kw_ref.at[2], k0_ref)):
            s = lax.dot_general(
                q, k_ref[:, cols], (((1,), (1,)), ((), ())), preferred_element_type=jnp.float32
            ) * scale
            t = lax.broadcasted_iota(jnp.int32, (rows, rows), 0)
            u = lax.broadcasted_iota(jnp.int32, (rows, rows), 1)
            if b == 3:
                visible = u <= t
            else:
                visible = jnp.broadcast_to(me - 3 + b >= 0, (rows, rows))
            parts.append(jnp.where(visible, s, -jnp.inf))
        masked = jnp.concatenate(parts, axis=1)
        peak = jnp.max(masked, axis=1, keepdims=True)
        w = jnp.exp(masked - peak)
        totals[h] = jnp.sum(w, axis=1, keepdims=True)
        weights[h] = w.astype(jnp.bfloat16)
        return carry

    lax.fori_loop(0, heads, score_head, 0)

    def accumulate(block, v_src, first):
        def one_head(h, carry):
            cols = pl.ds(pl.multiple_of(h * HEAD_DIM, HEAD_DIM), HEAD_DIM)
            w = weights[h, :, pl.ds(block * rows, rows)]
            part = jnp.dot(w, v_src[:, cols], preferred_element_type=jnp.float32)
            if first:
                acc[:, cols] = part
            else:
                acc[:, cols] = acc[:, cols] + part
            return carry

        lax.fori_loop(0, heads, one_head, 0)

    accumulate(3, v_ref, True)

    @pl.when(me >= 2)
    def _():
        incoming(1).wait_recv()

    relay_near = send(slots.at[1], 2, me - 1, 2)
    relay_far = send(slots.at[1], 0, me + 1, 3)

    @pl.when(me >= 2)
    def _():
        @pl.when(odd)
        def _():
            relay_near.start()

        @pl.when(jnp.logical_or(jnp.logical_not(odd), me + 1 < count))
        def _():
            relay_far.start()

    accumulate(1, slots.at[1], False)

    @pl.when(me >= 1)
    def _():
        incoming(2).wait_recv()

    accumulate(2, slots.at[2], False)

    @pl.when(me >= 3)
    def _():
        incoming(0).wait_recv()

    accumulate(0, slots.at[0], False)

    def finish(h, carry):
        cols = pl.ds(pl.multiple_of(h * HEAD_DIM, HEAD_DIM), HEAD_DIM)
        out_ref[:, cols] = (acc[:, cols] / totals[h]).astype(out_ref.dtype)
        return carry

    lax.fori_loop(0, heads, finish, 0)

    @pl.when(me + 2 < count)
    def _():
        far.wait_send()

    @pl.when(jnp.logical_not(odd))
    def _():
        near.wait_send()

    @pl.when((me >= 2) & odd)
    def _():
        relay_near.wait_send()

    @pl.when((me >= 2) & jnp.logical_or(jnp.logical_not(odd), me + 1 < count))
    def _():
        relay_far.wait_send()


def attend_exchange(query, key_stack, keys, values):
    count = lax.axis_size("ctx")
    rows, width = query.shape
    heads = width // HEAD_DIM
    vmem = pl.BlockSpec(memory_space=pltpu.VMEM)
    return pl.pallas_call(
        functools.partial(attend_exchange_kernel, count),
        out_shape=jax.ShapeDtypeStruct((rows, width), jnp.bfloat16),
        in_specs=[vmem] * 4,
        out_specs=vmem,
        scratch_shapes=[
            pltpu.VMEM((3, rows, width), jnp.bfloat16),
            pltpu.VMEM((heads, rows, WINDOW_BLOCKS * rows), jnp.bfloat16),
            pltpu.VMEM((heads, rows, 1), jnp.float32),
            pltpu.VMEM((rows, width), jnp.float32),
            pltpu.SemaphoreType.DMA((4,)),
            pltpu.SemaphoreType.DMA((3,)),
        ],
        compiler_params=pltpu.CompilerParams(
            collective_id=0, has_side_effects=True, vmem_limit_bytes=48 * 1024 * 1024
        ),
    )(query, key_stack, keys, values)


def key_exchange_kernel(
    count, edge_ref, k_ref, edge_out, k_out, edge_slot, slots, send_sems, recv_sems
):
    me = lax.axis_index("ctx")
    odd = lax.rem(me, 2) == 1
    rows, width = k_ref.shape

    @pl.when(me < 3)
    def _():
        for slot, first in ((0, 3), (1, 2), (2, 1)):
            @pl.when(me < first)
            def _():
                slots[slot] = jnp.zeros((rows, width), slots.dtype)

    @pl.when(me == 0)
    def _():
        edge_slot[...] = jnp.zeros(edge_slot.shape, edge_slot.dtype)

    barrier = pltpu.get_barrier_semaphore()
    for step in (-2, -1, 1, 2):
        peer = me + step

        @pl.when((peer >= 0) & (peer < count))
        def _():
            pl.semaphore_signal(barrier, inc=1, device_id={"ctx": peer}, device_id_type=MESH)

    neighbours = (
        (me >= 2).astype(jnp.int32) + (me >= 1).astype(jnp.int32)
        + (me + 1 < count).astype(jnp.int32) + (me + 2 < count).astype(jnp.int32)
    )
    pl.semaphore_wait(barrier, neighbours)

    def send(src, slot, peer, sem):
        return pltpu.make_async_remote_copy(
            src_ref=src, dst_ref=slots.at[slot], send_sem=send_sems.at[sem],
            recv_sem=recv_sems.at[slot], device_id={"ctx": peer}, device_id_type=MESH,
        )

    edge = pltpu.make_async_remote_copy(
        src_ref=edge_ref, dst_ref=edge_slot, send_sem=send_sems.at[4],
        recv_sem=recv_sems.at[3], device_id={"ctx": me + 1}, device_id_type=MESH,
    )
    edge_in = pltpu.make_async_remote_copy(
        src_ref=edge_ref, dst_ref=edge_slot, send_sem=send_sems.at[4],
        recv_sem=recv_sems.at[3], device_id={"ctx": me}, device_id_type=MESH,
    )

    @pl.when(me + 1 < count)
    def _():
        edge.start()

    far = send(k_ref, 1, me + 2, 0)
    near = send(k_ref, 2, me + 1, 1)

    @pl.when(me + 2 < count)
    def _():
        far.start()

    @pl.when(jnp.logical_not(odd))
    def _():
        near.start()

    @pl.when(me >= 1)
    def _():
        edge_in.wait_recv()

    edge_out[...] = edge_slot[...]

    def incoming(slot):
        return pltpu.make_async_remote_copy(
            src_ref=k_ref, dst_ref=slots.at[slot], send_sem=send_sems.at[0],
            recv_sem=recv_sems.at[slot], device_id={"ctx": me}, device_id_type=MESH,
        )

    @pl.when(me >= 2)
    def _():
        incoming(1).wait_recv()

    relay_near = send(slots.at[1], 2, me - 1, 2)
    relay_far = send(slots.at[1], 0, me + 1, 3)

    @pl.when(me >= 2)
    def _():
        @pl.when(odd)
        def _():
            relay_near.start()

        @pl.when(jnp.logical_or(jnp.logical_not(odd), me + 1 < count))
        def _():
            relay_far.start()

    k_out[1] = slots[1]

    @pl.when(me >= 1)
    def _():
        incoming(2).wait_recv()

    k_out[2] = slots[2]

    @pl.when(me >= 3)
    def _():
        incoming(0).wait_recv()

    k_out[0] = slots[0]

    @pl.when(me + 1 < count)
    def _():
        edge.wait_send()

    @pl.when(me + 2 < count)
    def _():
        far.wait_send()

    @pl.when(jnp.logical_not(odd))
    def _():
        near.wait_send()

    @pl.when((me >= 2) & odd)
    def _():
        relay_near.wait_send()

    @pl.when((me >= 2) & jnp.logical_or(jnp.logical_not(odd), me + 1 < count))
    def _():
        relay_far.wait_send()


def key_exchange(edge_rows, keys):
    count = lax.axis_size("ctx")
    rows, width = keys.shape
    vmem = pl.BlockSpec(memory_space=pltpu.VMEM)
    return pl.pallas_call(
        functools.partial(key_exchange_kernel, count),
        out_shape=(
            jax.ShapeDtypeStruct(edge_rows.shape, edge_rows.dtype),
            jax.ShapeDtypeStruct((3, rows, width), keys.dtype),
        ),
        in_specs=[vmem] * 2,
        out_specs=(vmem, vmem),
        scratch_shapes=[
            pltpu.VMEM(edge_rows.shape, edge_rows.dtype),
            pltpu.VMEM((3, rows, width), keys.dtype),
            pltpu.SemaphoreType.DMA((5,)),
            pltpu.SemaphoreType.DMA((4,)),
        ],
        compiler_params=pltpu.CompilerParams(
            collective_id=1, has_side_effects=True, vmem_limit_bytes=32 * 1024 * 1024
        ),
    )(edge_rows, keys)


def short_mix(rows, weights):
    return weights[0] * rows[2:] + weights[1] * rows[1:-1] + weights[2] * rows[:-2]


def body(hyena_features, short_filter, long_filter, att_query, att_key):
    tap_count = long_filter.shape[0]
    channel_count = long_filter.shape[1]
    q_raw = hyena_features[0]
    k_raw = hyena_features[1]
    v_raw = hyena_features[2]
    row_count = q_raw.shape[0]
    tail = row_count - (tap_count - 1) - 2
    product_tail = (
        short_mix(k_raw[tail:].astype(jnp.float32), short_filter[1])
        * short_mix(v_raw[tail:].astype(jnp.float32), short_filter[2])
    ).astype(jnp.bfloat16)
    edge_rows = jnp.concatenate([q_raw[-2:], k_raw[-2:], v_raw[-2:], product_tail], 0)
    pad = (-edge_rows.shape[0]) % 16
    edge_rows = jnp.concatenate([edge_rows, jnp.zeros((pad, channel_count), edge_rows.dtype)], 0)
    received, key_stack = key_exchange(edge_rows, att_key)
    received = received[: edge_rows.shape[0] - pad]
    q_ext = jnp.concatenate([received[0:2], q_raw], 0).astype(jnp.float32)
    k_ext = jnp.concatenate([received[2:4], k_raw], 0).astype(jnp.float32)
    v_ext = jnp.concatenate([received[4:6], v_raw], 0).astype(jnp.float32)
    q_mix = short_mix(q_ext, short_filter[0])
    product = (short_mix(k_ext, short_filter[1]) * short_mix(v_ext, short_filter[2])).astype(
        jnp.bfloat16
    )
    product_ext = jnp.concatenate([received[6:], product], 0)
    product_ext = lax.optimization_barrier(product_ext)
    kernel = long_filter[::-1][:, None, :]
    filtered = lax.conv_general_dilated(
        product_ext.astype(jnp.float32)[None],
        kernel,
        (1,),
        "VALID",
        dimension_numbers=("NWC", "WIO", "NWC"),
        feature_group_count=channel_count,
        precision=lax.Precision.HIGHEST,
    )[0]
    hyena_mixed = (q_mix * filtered).astype(jnp.bfloat16)
    attended = attend_exchange(att_query, key_stack, att_key, hyena_mixed)
    return (hyena_mixed, attended)


def solution(mesh):
    return jax.shard_map(
        body,
        mesh=mesh,
        in_specs=(
            P(None, ("dp", "ctx"), "tp"),
            P(None, None, "tp"),
            P(None, "tp"),
            P(("dp", "ctx"), "tp"),
            P(("dp", "ctx"), "tp"),
        ),
        out_specs=(P(("dp", "ctx"), "tp"), P(("dp", "ctx"), "tp")),
        check_vma=False,
    )
```

```python
import functools
import math

import jax
import jax.numpy as jnp
from jax import lax
from jax.experimental import pallas as pl
from jax.experimental.pallas import tpu as pltpu
from jax.sharding import PartitionSpec as P

MESH = pl.DeviceIdType.MESH

HEAD_DIM = 128
WINDOW_BLOCKS = 4


def attend_exchange_kernel(
    count, q_ref, kw_ref, k0_ref, v_ref, out_ref,
    slots, weights, totals, acc, send_sems, recv_sems,
):
    me = lax.axis_index("ctx")
    odd = lax.rem(me, 2) == 1
    rows, width = q_ref.shape
    heads = width // HEAD_DIM
    scale = 1.0 / math.sqrt(HEAD_DIM)

    @pl.when(me < 3)
    def _():
        for slot, first in ((0, 3), (1, 2), (2, 1)):
            @pl.when(me < first)
            def _():
                slots[slot] = jnp.zeros((rows, width), slots.dtype)

    barrier = pltpu.get_barrier_semaphore()
    for step in (-2, -1, 1, 2):
        peer = me + step

        @pl.when((peer >= 0) & (peer < count))
        def _():
            pl.semaphore_signal(barrier, inc=1, device_id={"ctx": peer}, device_id_type=MESH)

    neighbours = (
        (me >= 2).astype(jnp.int32) + (me >= 1).astype(jnp.int32)
        + (me + 1 < count).astype(jnp.int32) + (me + 2 < count).astype(jnp.int32)
    )
    pl.semaphore_wait(barrier, neighbours)

    def send(src, slot, peer, sem):
        return pltpu.make_async_remote_copy(
            src_ref=src, dst_ref=slots.at[slot], send_sem=send_sems.at[sem],
            recv_sem=recv_sems.at[slot], device_id={"ctx": peer}, device_id_type=MESH,
        )

    def incoming(slot):
        return pltpu.make_async_remote_copy(
            src_ref=v_ref, dst_ref=slots.at[slot], send_sem=send_sems.at[0],
            recv_sem=recv_sems.at[slot], device_id={"ctx": me}, device_id_type=MESH,
        )

    far = send(v_ref, 1, me + 2, 0)
    near = send(v_ref, 2, me + 1, 1)

    @pl.when(me + 2 < count)
    def _():
        far.start()

    @pl.when(jnp.logical_not(odd))
    def _():
        near.start()

    def score_head(h, carry):
        cols = pl.ds(pl.multiple_of(h * HEAD_DIM, HEAD_DIM), HEAD_DIM)
        q = q_ref[:, cols]
        parts = []
        for b, k_ref in enumerate((kw_ref.at[0], kw_ref.at[1], kw_ref.at[2], k0_ref)):
            s = lax.dot_general(
                q, k_ref[:, cols], (((1,), (1,)), ((), ())), preferred_element_type=jnp.float32
            ) * scale
            t = lax.broadcasted_iota(jnp.int32, (rows, rows), 0)
            u = lax.broadcasted_iota(jnp.int32, (rows, rows), 1)
            if b == 3:
                visible = u <= t
            else:
                visible = jnp.broadcast_to(me - 3 + b >= 0, (rows, rows))
            parts.append(jnp.where(visible, s, -jnp.inf))
        masked = jnp.concatenate(parts, axis=1)
        peak = jnp.max(masked, axis=1, keepdims=True)
        w = jnp.exp(masked - peak)
        totals[h] = jnp.sum(w, axis=1, keepdims=True)
        weights[h] = w.astype(jnp.bfloat16)
        return carry

    lax.fori_loop(0, heads, score_head, 0)

    def accumulate(block, v_src, first):
        def one_head(h, carry):
            cols = pl.ds(pl.multiple_of(h * HEAD_DIM, HEAD_DIM), HEAD_DIM)
            w = weights[h, :, pl.ds(block * rows, rows)]
            part = jnp.dot(w, v_src[:, cols], preferred_element_type=jnp.float32)
            if first:
                acc[:, cols] = part
            else:
                acc[:, cols] = acc[:, cols] + part
            return carry

        lax.fori_loop(0, heads, one_head, 0)

    accumulate(3, v_ref, True)

    @pl.when(me >= 2)
    def _():
        incoming(1).wait_recv()

    relay_near = send(slots.at[1], 2, me - 1, 2)
    relay_far = send(slots.at[1], 0, me + 1, 3)

    @pl.when(me >= 2)
    def _():
        @pl.when(odd)
        def _():
            relay_near.start()

        @pl.when(jnp.logical_or(jnp.logical_not(odd), me + 1 < count))
        def _():
            relay_far.start()

    accumulate(1, slots.at[1], False)

    @pl.when(me >= 1)
    def _():
        incoming(2).wait_recv()

    accumulate(2, slots.at[2], False)

    @pl.when(me >= 3)
    def _():
        incoming(0).wait_recv()

    accumulate(0, slots.at[0], False)

    def finish(h, carry):
        cols = pl.ds(pl.multiple_of(h * HEAD_DIM, HEAD_DIM), HEAD_DIM)
        out_ref[:, cols] = (acc[:, cols] / totals[h]).astype(out_ref.dtype)
        return carry

    lax.fori_loop(0, heads, finish, 0)

    @pl.when(me + 2 < count)
    def _():
        far.wait_send()

    @pl.when(jnp.logical_not(odd))
    def _():
        near.wait_send()

    @pl.when((me >= 2) & odd)
    def _():
        relay_near.wait_send()

    @pl.when((me >= 2) & jnp.logical_or(jnp.logical_not(odd), me + 1 < count))
    def _():
        relay_far.wait_send()


def attend_exchange(query, key_stack, keys, values):
    count = lax.axis_size("ctx")
    rows, width = query.shape
    heads = width // HEAD_DIM
    vmem = pl.BlockSpec(memory_space=pltpu.VMEM)
    return pl.pallas_call(
        functools.partial(attend_exchange_kernel, count),
        out_shape=jax.ShapeDtypeStruct((rows, width), jnp.bfloat16),
        in_specs=[vmem] * 4,
        out_specs=vmem,
        scratch_shapes=[
            pltpu.VMEM((3, rows, width), jnp.bfloat16),
            pltpu.VMEM((heads, rows, WINDOW_BLOCKS * rows), jnp.bfloat16),
            pltpu.VMEM((heads, rows, 1), jnp.float32),
            pltpu.VMEM((rows, width), jnp.float32),
            pltpu.SemaphoreType.DMA((4,)),
            pltpu.SemaphoreType.DMA((3,)),
        ],
        compiler_params=pltpu.CompilerParams(
            collective_id=0, has_side_effects=True, vmem_limit_bytes=48 * 1024 * 1024
        ),
    )(query, key_stack, keys, values)


def hyena_key_kernel(
    count, edge_ref, k_ref, feats_ref, sf_ref, lf_ref, qmix_ref, prod_ref,
    hm_out, k_out, edge_slot, slots, ext, shifted, filtered, send_sems, recv_sems,
):
    me = lax.axis_index("ctx")
    odd = lax.rem(me, 2) == 1
    rows, width = k_ref.shape
    taps = lf_ref.shape[0]

    @pl.when(me < 3)
    def _():
        for slot, first in ((0, 3), (1, 2), (2, 1)):
            @pl.when(me < first)
            def _():
                slots[slot] = jnp.zeros((rows, width), slots.dtype)

    @pl.when(me == 0)
    def _():
        edge_slot[...] = jnp.zeros(edge_slot.shape, edge_slot.dtype)

    barrier = pltpu.get_barrier_semaphore()
    for step in (-2, -1, 1, 2):
        peer = me + step

        @pl.when((peer >= 0) & (peer < count))
        def _():
            pl.semaphore_signal(barrier, inc=1, device_id={"ctx": peer}, device_id_type=MESH)

    neighbours = (
        (me >= 2).astype(jnp.int32) + (me >= 1).astype(jnp.int32)
        + (me + 1 < count).astype(jnp.int32) + (me + 2 < count).astype(jnp.int32)
    )
    pl.semaphore_wait(barrier, neighbours)

    def send(src, slot, peer, sem):
        return pltpu.make_async_remote_copy(
            src_ref=src, dst_ref=slots.at[slot], send_sem=send_sems.at[sem],
            recv_sem=recv_sems.at[slot], device_id={"ctx": peer}, device_id_type=MESH,
        )

    edge = pltpu.make_async_remote_copy(
        src_ref=edge_ref, dst_ref=edge_slot, send_sem=send_sems.at[4],
        recv_sem=recv_sems.at[3], device_id={"ctx": me + 1}, device_id_type=MESH,
    )
    edge_in = pltpu.make_async_remote_copy(
        src_ref=edge_ref, dst_ref=edge_slot, send_sem=send_sems.at[4],
        recv_sem=recv_sems.at[3], device_id={"ctx": me}, device_id_type=MESH,
    )

    @pl.when(me + 1 < count)
    def _():
        edge.start()

    far = send(k_ref, 1, me + 2, 0)
    near = send(k_ref, 2, me + 1, 1)

    @pl.when(me + 2 < count)
    def _():
        far.start()

    @pl.when(jnp.logical_not(odd))
    def _():
        near.start()

    @pl.when(me >= 1)
    def _():
        edge_in.wait_recv()

    ext[pl.ds(0, taps), :] = edge_slot[pl.ds(0, taps), :].astype(jnp.float32)
    ext[pl.ds(taps, rows), :] = prod_ref[...].astype(jnp.float32)

    def prev(i):
        return edge_slot[pl.ds(taps + i, 1), :].astype(jnp.float32)

    def own(which, i):
        return feats_ref[which, pl.ds(i, 1), :].astype(jnp.float32)

    def mixed(which, r):
        w = sf_ref[which]
        older = [prev(2 * which), prev(2 * which + 1)] + [own(which, 0), own(which, 1)]
        return (w[0:1] * older[r + 2] + w[1:2] * older[r + 1]) + w[2:3] * older[r]

    for r in range(2):
        product = (mixed(1, r) * mixed(2, r)).astype(jnp.bfloat16).astype(jnp.float32)
        ext[pl.ds(taps + r, 1), :] = product

    def chunk(c, carry):
        cols = pl.ds(pl.multiple_of(c * 128, 128), 128)
        for b in range(8):
            shifted[b, pl.ds(8, rows + taps - 8), :] = ext[pl.ds(8 - b, rows + taps - 8), cols]
        acc = jnp.zeros((rows, 128), jnp.float32)
        for a in range(taps // 8):
            for b in range(8):
                j = 8 * a + b
                acc = acc + lf_ref[pl.ds(j, 1), cols] * shifted[b, pl.ds(taps - 8 * a, rows), :]
        filtered[:, cols] = acc
        hm_out[:, cols] = (qmix_ref[:, cols] * acc).astype(hm_out.dtype)
        return carry

    lax.fori_loop(0, width // 128, chunk, 0)
    for r in range(2):
        hm_out[pl.ds(r, 1), :] = (mixed(0, r) * filtered[pl.ds(r, 1), :]).astype(hm_out.dtype)

    def incoming(slot):
        return pltpu.make_async_remote_copy(
            src_ref=k_ref, dst_ref=slots.at[slot], send_sem=send_sems.at[0],
            recv_sem=recv_sems.at[slot], device_id={"ctx": me}, device_id_type=MESH,
        )

    @pl.when(me >= 2)
    def _():
        incoming(1).wait_recv()

    relay_near = send(slots.at[1], 2, me - 1, 2)
    relay_far = send(slots.at[1], 0, me + 1, 3)

    @pl.when(me >= 2)
    def _():
        @pl.when(odd)
        def _():
            relay_near.start()

        @pl.when(jnp.logical_or(jnp.logical_not(odd), me + 1 < count))
        def _():
            relay_far.start()

    k_out[1] = slots[1]

    @pl.when(me >= 1)
    def _():
        incoming(2).wait_recv()

    k_out[2] = slots[2]

    @pl.when(me >= 3)
    def _():
        incoming(0).wait_recv()

    k_out[0] = slots[0]

    @pl.when(me + 1 < count)
    def _():
        edge.wait_send()

    @pl.when(me + 2 < count)
    def _():
        far.wait_send()

    @pl.when(jnp.logical_not(odd))
    def _():
        near.wait_send()

    @pl.when((me >= 2) & odd)
    def _():
        relay_near.wait_send()

    @pl.when((me >= 2) & jnp.logical_or(jnp.logical_not(odd), me + 1 < count))
    def _():
        relay_far.wait_send()


def hyena_key_exchange(edge_rows, keys, feats, short_filter, long_filter, q_mix, product):
    count = lax.axis_size("ctx")
    rows, width = keys.shape
    taps = long_filter.shape[0]
    vmem = pl.BlockSpec(memory_space=pltpu.VMEM)
    return pl.pallas_call(
        functools.partial(hyena_key_kernel, count),
        out_shape=(
            jax.ShapeDtypeStruct((rows, width), jnp.bfloat16),
            jax.ShapeDtypeStruct((3, rows, width), keys.dtype),
        ),
        in_specs=[vmem] * 7,
        out_specs=(vmem, vmem),
        scratch_shapes=[
            pltpu.VMEM(edge_rows.shape, edge_rows.dtype),
            pltpu.VMEM((3, rows, width), keys.dtype),
            pltpu.VMEM((rows + taps, width), jnp.float32),
            pltpu.VMEM((8, rows + taps, 128), jnp.float32),
            pltpu.VMEM((rows, width), jnp.float32),
            pltpu.SemaphoreType.DMA((5,)),
            pltpu.SemaphoreType.DMA((4,)),
        ],
        compiler_params=pltpu.CompilerParams(
            collective_id=1, has_side_effects=True, vmem_limit_bytes=48 * 1024 * 1024
        ),
    )(edge_rows, keys, feats, short_filter, long_filter, q_mix, product)


def short_mix(rows, weights):
    return weights[0] * rows[2:] + weights[1] * rows[1:-1] + weights[2] * rows[:-2]


def body(hyena_features, short_filter, long_filter, att_query, att_key):
    tap_count = long_filter.shape[0]
    channel_count = long_filter.shape[1]
    q_raw = hyena_features[0]
    k_raw = hyena_features[1]
    v_raw = hyena_features[2]
    row_count = q_raw.shape[0]
    tail = row_count - (tap_count - 1) - 2
    product_tail = (
        short_mix(k_raw[tail:].astype(jnp.float32), short_filter[1])
        * short_mix(v_raw[tail:].astype(jnp.float32), short_filter[2])
    ).astype(jnp.bfloat16)
    edge_rows = jnp.concatenate(
        [jnp.zeros((1, channel_count), jnp.bfloat16), product_tail,
         q_raw[-2:], k_raw[-2:], v_raw[-2:]], 0
    )
    pad = (-edge_rows.shape[0]) % 16
    edge_rows = jnp.concatenate([edge_rows, jnp.zeros((pad, channel_count), edge_rows.dtype)], 0)
    blank = jnp.zeros((2, channel_count), jnp.float32)
    q_mix = short_mix(jnp.concatenate([blank, q_raw.astype(jnp.float32)], 0), short_filter[0])
    product = (
        short_mix(jnp.concatenate([blank, k_raw.astype(jnp.float32)], 0), short_filter[1])
        * short_mix(jnp.concatenate([blank, v_raw.astype(jnp.float32)], 0), short_filter[2])
    ).astype(jnp.bfloat16)
    hyena_mixed, key_stack = hyena_key_exchange(
        edge_rows, att_key, hyena_features, short_filter, long_filter, q_mix, product
    )
    attended = attend_exchange(att_query, key_stack, att_key, hyena_mixed)
    return (hyena_mixed, attended)


def solution(mesh):
    return jax.shard_map(
        body,
        mesh=mesh,
        in_specs=(
            P(None, ("dp", "ctx"), "tp"),
            P(None, None, "tp"),
            P(None, "tp"),
            P(("dp", "ctx"), "tp"),
            P(("dp", "ctx"), "tp"),
        ),
        out_specs=(P(("dp", "ctx"), "tp"), P(("dp", "ctx"), "tp")),
        check_vma=False,
    )
```

```python
import functools
import math

import jax
import jax.numpy as jnp
from jax import lax
from jax.experimental import pallas as pl
from jax.experimental.pallas import tpu as pltpu
from jax.sharding import PartitionSpec as P

MESH = pl.DeviceIdType.MESH

HEAD_DIM = 128
WINDOW_BLOCKS = 4


def fused_kernel(
    count, k_ref, feats_ref, sf_ref, lf_ref, q_ref,
    hm_out, out_ref,
    edge_stage, edge_send, edge_slot, kslots, vslots, vsrc, raw, qmix, ext, shifted,
    weights, totals, acc, send_sems, recv_sems, copy_sem,
):
    me = lax.axis_index("ctx")
    odd = lax.rem(me, 2) == 1
    even = jnp.logical_not(odd)
    rows, width = k_ref.shape
    taps = lf_ref.shape[0]
    heads = width // HEAD_DIM
    scale = 1.0 / math.sqrt(HEAD_DIM)

    @pl.when(me < 3)
    def _():
        for slot, first in ((0, 3), (1, 2), (2, 1)):
            @pl.when(me < first)
            def _():
                kslots[slot] = jnp.zeros((rows, width), kslots.dtype)
                vslots[slot] = jnp.zeros((rows, width), vslots.dtype)

    @pl.when(me == 0)
    def _():
        edge_slot[...] = jnp.zeros(edge_slot.shape, edge_slot.dtype)

    barrier = pltpu.get_barrier_semaphore()
    for step in (-2, -1, 1, 2):
        peer = me + step

        @pl.when((peer >= 0) & (peer < count))
        def _():
            pl.semaphore_signal(barrier, inc=1, device_id={"ctx": peer}, device_id_type=MESH)

    neighbours = (
        (me >= 2).astype(jnp.int32) + (me >= 1).astype(jnp.int32)
        + (me + 1 < count).astype(jnp.int32) + (me + 2 < count).astype(jnp.int32)
    )
    pl.semaphore_wait(barrier, neighbours)

    def route(slots, src, base_send, base_recv):
        def send(source, slot, peer, sem):
            return pltpu.make_async_remote_copy(
                src_ref=source, dst_ref=slots.at[slot], send_sem=send_sems.at[base_send + sem],
                recv_sem=recv_sems.at[base_recv + slot], device_id={"ctx": peer},
                device_id_type=MESH,
            )

        def incoming(slot):
            return pltpu.make_async_remote_copy(
                src_ref=src, dst_ref=slots.at[slot], send_sem=send_sems.at[base_send],
                recv_sem=recv_sems.at[base_recv + slot], device_id={"ctx": me},
                device_id_type=MESH,
            )

        far = send(src, 1, me + 2, 0)
        near = send(src, 2, me + 1, 1)
        relay_near = send(slots.at[1], 2, me - 1, 2)
        relay_far = send(slots.at[1], 0, me + 1, 3)
        return far, near, relay_near, relay_far, incoming

    def start_first(far, near):
        @pl.when(me + 2 < count)
        def _():
            far.start()

        @pl.when(even)
        def _():
            near.start()

    def start_relay(relay_near, relay_far, incoming):
        @pl.when(me >= 2)
        def _():
            incoming(1).wait_recv()

            @pl.when(odd)
            def _():
                relay_near.start()

            @pl.when(jnp.logical_or(even, me + 1 < count))
            def _():
                relay_far.start()

    def finish_sends(far, near, relay_near, relay_far):
        @pl.when(me + 2 < count)
        def _():
            far.wait_send()

        @pl.when(even)
        def _():
            near.wait_send()

        @pl.when((me >= 2) & odd)
        def _():
            relay_near.wait_send()

        @pl.when((me >= 2) & jnp.logical_or(even, me + 1 < count))
        def _():
            relay_far.wait_send()

    front = 8
    half = rows // 2
    for which in range(3):
        raw[which, pl.ds(0, front), :] = jnp.zeros((front, width), jnp.float32)
        raw[which, pl.ds(front, rows), :] = feats_ref[which].astype(jnp.float32)

    def mix(which, start, length):
        w = sf_ref[which]
        x = raw.at[which]
        return (
            w[0:1] * x[pl.ds(front + start, length), :]
            + w[1:2] * x[pl.ds(front + start - 1, length), :]
        ) + w[2:3] * x[pl.ds(front + start - 2, length), :]

    edge_stage[pl.ds(0, half), :] = (mix(1, half, half) * mix(2, half, half)).astype(
        edge_stage.dtype
    )
    for which in range(3):
        edge_stage[pl.ds(half + 16 * which, 16), :] = feats_ref[which, pl.ds(rows - 16, 16), :]
    staged = pltpu.make_async_copy(edge_stage, edge_send, copy_sem.at[1])
    staged.start()
    staged.wait()

    edge = pltpu.make_async_remote_copy(
        src_ref=edge_send, dst_ref=edge_slot, send_sem=send_sems.at[8],
        recv_sem=recv_sems.at[6], device_id={"ctx": me + 1}, device_id_type=MESH,
    )
    edge_in = pltpu.make_async_remote_copy(
        src_ref=edge_send, dst_ref=edge_slot, send_sem=send_sems.at[8],
        recv_sem=recv_sems.at[6], device_id={"ctx": me}, device_id_type=MESH,
    )

    @pl.when(me + 1 < count)
    def _():
        edge.start()

    k_far, k_near, k_relay_near, k_relay_far, k_incoming = route(kslots, k_ref, 0, 0)
    start_first(k_far, k_near)

    @pl.when(me >= 1)
    def _():
        edge_in.wait_recv()

    for which in range(3):
        older = edge_slot[pl.ds(half + 16 * which, 16), :].astype(jnp.float32)
        raw[which, pl.ds(0, front), :] = older[16 - front :]

    qmix[...] = mix(0, 0, rows)
    ext[pl.ds(0, taps), :] = edge_slot[pl.ds(0, taps), :].astype(jnp.float32)
    ext[pl.ds(taps, rows), :] = (mix(1, 0, rows) * mix(2, 0, rows)).astype(
        jnp.bfloat16
    ).astype(jnp.float32)

    def chunk(c, carry):
        cols = pl.ds(pl.multiple_of(c * 128, 128), 128)
        for b in range(8):
            shifted[b, pl.ds(8, rows + taps - 8), :] = ext[pl.ds(8 - b, rows + taps - 8), cols]
        total = jnp.zeros((rows, 128), jnp.float32)
        for a in range(taps // 8):
            for b in range(8):
                j = 8 * a + b
                total = total + lf_ref[pl.ds(j, 1), cols] * shifted[b, pl.ds(taps - 8 * a, rows), :]
        hm_out[:, cols] = (qmix[:, cols] * total).astype(hm_out.dtype)
        return carry

    lax.fori_loop(0, width // 128, chunk, 0)

    local = pltpu.make_async_copy(hm_out, vsrc, copy_sem.at[0])
    local.start()
    local.wait()

    v_far, v_near, v_relay_near, v_relay_far, v_incoming = route(vslots, vsrc, 4, 3)
    start_first(v_far, v_near)
    start_relay(k_relay_near, k_relay_far, k_incoming)

    @pl.when(me >= 1)
    def _():
        k_incoming(2).wait_recv()

    @pl.when(me >= 3)
    def _():
        k_incoming(0).wait_recv()

    def score_head(h, carry):
        cols = pl.ds(pl.multiple_of(h * HEAD_DIM, HEAD_DIM), HEAD_DIM)
        q = q_ref[:, cols]
        parts = []
        for b, keys in enumerate((kslots.at[0], kslots.at[1], kslots.at[2], k_ref)):
            s = lax.dot_general(
                q, keys[:, cols], (((1,), (1,)), ((), ())), preferred_element_type=jnp.float32
            ) * scale
            t = lax.broadcasted_iota(jnp.int32, (rows, rows), 0)
            u = lax.broadcasted_iota(jnp.int32, (rows, rows), 1)
            if b == 3:
                visible = u <= t
            else:
                visible = jnp.broadcast_to(me - 3 + b >= 0, (rows, rows))
            parts.append(jnp.where(visible, s, -jnp.inf))
        masked = jnp.concatenate(parts, axis=1)
        peak = jnp.max(masked, axis=1, keepdims=True)
        w = jnp.exp(masked - peak)
        totals[h] = jnp.sum(w, axis=1, keepdims=True)
        weights[h] = w.astype(jnp.bfloat16)
        return carry

    lax.fori_loop(0, heads, score_head, 0)

    def accumulate(block, v_src, first):
        def one_head(h, carry):
            cols = pl.ds(pl.multiple_of(h * HEAD_DIM, HEAD_DIM), HEAD_DIM)
            w = weights[h, :, pl.ds(block * rows, rows)]
            part = jnp.dot(w, v_src[:, cols], preferred_element_type=jnp.float32)
            if first:
                acc[:, cols] = part
            else:
                acc[:, cols] = acc[:, cols] + part
            return carry

        lax.fori_loop(0, heads, one_head, 0)

    accumulate(3, vsrc, True)
    start_relay(v_relay_near, v_relay_far, v_incoming)
    accumulate(1, vslots.at[1], False)

    @pl.when(me >= 1)
    def _():
        v_incoming(2).wait_recv()

    accumulate(2, vslots.at[2], False)

    @pl.when(me >= 3)
    def _():
        v_incoming(0).wait_recv()

    accumulate(0, vslots.at[0], False)

    def finish(h, carry):
        cols = pl.ds(pl.multiple_of(h * HEAD_DIM, HEAD_DIM), HEAD_DIM)
        out_ref[:, cols] = (acc[:, cols] / totals[h]).astype(out_ref.dtype)
        return carry

    lax.fori_loop(0, heads, finish, 0)

    @pl.when(me + 1 < count)
    def _():
        edge.wait_send()

    finish_sends(k_far, k_near, k_relay_near, k_relay_far)
    finish_sends(v_far, v_near, v_relay_near, v_relay_far)


def fused_call(keys, feats, short_filter, long_filter, query):
    count = lax.axis_size("ctx")
    rows, width = keys.shape
    taps = long_filter.shape[0]
    heads = width // HEAD_DIM
    edge_rows = rows // 2 + 48
    vmem = pl.BlockSpec(memory_space=pltpu.VMEM)
    return pl.pallas_call(
        functools.partial(fused_kernel, count),
        out_shape=(
            jax.ShapeDtypeStruct((rows, width), jnp.bfloat16),
            jax.ShapeDtypeStruct((rows, width), jnp.bfloat16),
        ),
        in_specs=[vmem] * 5,
        out_specs=(vmem, vmem),
        scratch_shapes=[
            pltpu.VMEM((edge_rows, width), jnp.bfloat16),
            pltpu.VMEM((edge_rows, width), jnp.bfloat16),
            pltpu.VMEM((edge_rows, width), jnp.bfloat16),
            pltpu.VMEM((3, rows, width), keys.dtype),
            pltpu.VMEM((3, rows, width), jnp.bfloat16),
            pltpu.VMEM((rows, width), jnp.bfloat16),
            pltpu.VMEM((3, rows + 8, width), jnp.float32),
            pltpu.VMEM((rows, width), jnp.float32),
            pltpu.VMEM((rows + taps, width), jnp.float32),
            pltpu.VMEM((8, rows + taps, 128), jnp.float32),
            pltpu.VMEM((heads, rows, WINDOW_BLOCKS * rows), jnp.bfloat16),
            pltpu.VMEM((heads, rows, 1), jnp.float32),
            pltpu.VMEM((rows, width), jnp.float32),
            pltpu.SemaphoreType.DMA((9,)),
            pltpu.SemaphoreType.DMA((7,)),
            pltpu.SemaphoreType.DMA((2,)),
        ],
        compiler_params=pltpu.CompilerParams(
            collective_id=0, has_side_effects=True, vmem_limit_bytes=60 * 1024 * 1024
        ),
    )(keys, feats, short_filter, long_filter, query)


def body(hyena_features, short_filter, long_filter, att_query, att_key):
    return fused_call(att_key, hyena_features, short_filter, long_filter, att_query)


def solution(mesh):
    return jax.shard_map(
        body,
        mesh=mesh,
        in_specs=(
            P(None, ("dp", "ctx"), "tp"),
            P(None, None, "tp"),
            P(None, "tp"),
            P(("dp", "ctx"), "tp"),
            P(("dp", "ctx"), "tp"),
        ),
        out_specs=(P(("dp", "ctx"), "tp"), P(("dp", "ctx"), "tp")),
        check_vma=False,
    )
```

```python
import functools
import math

import jax
import jax.numpy as jnp
from jax import lax
from jax.experimental import pallas as pl
from jax.experimental.pallas import tpu as pltpu
from jax.sharding import PartitionSpec as P

MESH = pl.DeviceIdType.MESH

HEAD_DIM = 128
WINDOW_BLOCKS = 4


def fused_kernel(
    count, k_ref, feats_ref, sf_ref, lf_ref, q_ref,
    hm_out, out_ref,
    edge_stage, edge_send, edge_slot, kslots, vslots, vsrc, vstage, raw, qmix, ext, shifted,
    weights, totals, acc, send_sems, recv_sems, copy_sem,
):
    me = lax.axis_index("ctx")
    odd = lax.rem(me, 2) == 1
    even = jnp.logical_not(odd)
    rows, width = k_ref.shape
    taps = lf_ref.shape[0]
    heads = width // HEAD_DIM
    scale = 1.0 / math.sqrt(HEAD_DIM)

    @pl.when(me < 3)
    def _():
        for slot, first in ((0, 3), (1, 2), (2, 1)):
            @pl.when(me < first)
            def _():
                kslots[slot] = jnp.zeros((rows, width), kslots.dtype)
                vslots[slot] = jnp.zeros((rows, width), vslots.dtype)

    @pl.when(me == 0)
    def _():
        edge_slot[...] = jnp.zeros(edge_slot.shape, edge_slot.dtype)

    barrier = pltpu.get_barrier_semaphore()
    for step in (-2, -1, 1, 2):
        peer = me + step

        @pl.when((peer >= 0) & (peer < count))
        def _():
            pl.semaphore_signal(barrier, inc=1, device_id={"ctx": peer}, device_id_type=MESH)

    neighbours = (
        (me >= 2).astype(jnp.int32) + (me >= 1).astype(jnp.int32)
        + (me + 1 < count).astype(jnp.int32) + (me + 2 < count).astype(jnp.int32)
    )
    pl.semaphore_wait(barrier, neighbours)

    def route(slots, src, base_send, base_recv):
        def send(source, slot, peer, sem):
            return pltpu.make_async_remote_copy(
                src_ref=source, dst_ref=slots.at[slot], send_sem=send_sems.at[base_send + sem],
                recv_sem=recv_sems.at[base_recv + slot], device_id={"ctx": peer},
                device_id_type=MESH,
            )

        def incoming(slot):
            return pltpu.make_async_remote_copy(
                src_ref=src, dst_ref=slots.at[slot], send_sem=send_sems.at[base_send],
                recv_sem=recv_sems.at[base_recv + slot], device_id={"ctx": me},
                device_id_type=MESH,
            )

        far = send(src, 1, me + 2, 0)
        near = send(src, 2, me + 1, 1)
        relay_near = send(slots.at[1], 2, me - 1, 2)
        relay_far = send(slots.at[1], 0, me + 1, 3)
        return far, near, relay_near, relay_far, incoming

    def start_first(far, near):
        @pl.when(me + 2 < count)
        def _():
            far.start()

        @pl.when(even)
        def _():
            near.start()

    def start_relay(relay_near, relay_far, incoming):
        @pl.when(me >= 2)
        def _():
            incoming(1).wait_recv()

            @pl.when(odd)
            def _():
                relay_near.start()

            @pl.when(jnp.logical_or(even, me + 1 < count))
            def _():
                relay_far.start()

    def finish_sends(far, near, relay_near, relay_far):
        @pl.when(me + 2 < count)
        def _():
            far.wait_send()

        @pl.when(even)
        def _():
            near.wait_send()

        @pl.when((me >= 2) & odd)
        def _():
            relay_near.wait_send()

        @pl.when((me >= 2) & jnp.logical_or(even, me + 1 < count))
        def _():
            relay_far.wait_send()

    front = 8
    half = rows // 2
    for which in range(3):
        raw[which, pl.ds(0, front), :] = jnp.zeros((front, width), jnp.float32)
        raw[which, pl.ds(front, rows), :] = feats_ref[which].astype(jnp.float32)

    def mix(which, start, length):
        w = sf_ref[which]
        x = raw.at[which]
        return (
            w[0:1] * x[pl.ds(front + start, length), :]
            + w[1:2] * x[pl.ds(front + start - 1, length), :]
        ) + w[2:3] * x[pl.ds(front + start - 2, length), :]

    edge_stage[pl.ds(0, half), :] = (mix(1, half, half) * mix(2, half, half)).astype(
        edge_stage.dtype
    )
    for which in range(3):
        edge_stage[pl.ds(half + 16 * which, 16), :] = feats_ref[which, pl.ds(rows - 16, 16), :]
    staged = pltpu.make_async_copy(edge_stage, edge_send, copy_sem.at[1])
    staged.start()
    staged.wait()

    edge = pltpu.make_async_remote_copy(
        src_ref=edge_send, dst_ref=edge_slot, send_sem=send_sems.at[8],
        recv_sem=recv_sems.at[6], device_id={"ctx": me + 1}, device_id_type=MESH,
    )
    edge_in = pltpu.make_async_remote_copy(
        src_ref=edge_send, dst_ref=edge_slot, send_sem=send_sems.at[8],
        recv_sem=recv_sems.at[6], device_id={"ctx": me}, device_id_type=MESH,
    )

    @pl.when(me + 1 < count)
    def _():
        edge.start()

    k_far, k_near, k_relay_near, k_relay_far, k_incoming = route(kslots, k_ref, 0, 0)
    start_first(k_far, k_near)

    @pl.when(me >= 1)
    def _():
        edge_in.wait_recv()

    for which in range(3):
        older = edge_slot[pl.ds(half + 16 * which, 16), :].astype(jnp.float32)
        raw[which, pl.ds(0, front), :] = older[16 - front :]

    qmix[...] = mix(0, 0, rows)
    ext[pl.ds(0, taps), :] = edge_slot[pl.ds(0, taps), :].astype(jnp.float32)
    ext[pl.ds(taps, rows), :] = (mix(1, 0, rows) * mix(2, 0, rows)).astype(
        jnp.bfloat16
    ).astype(jnp.float32)

    def chunk(c, carry):
        cols = pl.ds(pl.multiple_of(c * 128, 128), 128)
        for b in range(8):
            shifted[b, pl.ds(8, rows + taps - 8), :] = ext[pl.ds(8 - b, rows + taps - 8), cols]
        total = jnp.zeros((rows, 128), jnp.float32)
        for a in range(taps // 8):
            for b in range(8):
                j = 8 * a + b
                total = total + lf_ref[pl.ds(j, 1), cols] * shifted[b, pl.ds(taps - 8 * a, rows), :]
        gated = qmix[:, cols] * total
        hm_out[:, cols] = gated
        vsrc[:, cols] = gated.astype(vsrc.dtype)
        return carry

    lax.fori_loop(0, width // 128, chunk, 0)

    local = pltpu.make_async_copy(vsrc, vstage, copy_sem.at[0])
    local.start()
    local.wait()

    v_far, v_near, v_relay_near, v_relay_far, v_incoming = route(vslots, vstage, 4, 3)
    start_first(v_far, v_near)
    start_relay(k_relay_near, k_relay_far, k_incoming)

    @pl.when(me >= 1)
    def _():
        k_incoming(2).wait_recv()

    @pl.when(me >= 3)
    def _():
        k_incoming(0).wait_recv()

    def score_head(h, carry):
        cols = pl.ds(pl.multiple_of(h * HEAD_DIM, HEAD_DIM), HEAD_DIM)
        q = q_ref[:, cols]
        parts = []
        for b, keys in enumerate((kslots.at[0], kslots.at[1], kslots.at[2], k_ref)):
            s = lax.dot_general(
                q, keys[:, cols], (((1,), (1,)), ((), ())), preferred_element_type=jnp.float32
            ) * scale
            t = lax.broadcasted_iota(jnp.int32, (rows, rows), 0)
            u = lax.broadcasted_iota(jnp.int32, (rows, rows), 1)
            if b == 3:
                visible = u <= t
            else:
                visible = jnp.broadcast_to(me - 3 + b >= 0, (rows, rows))
            parts.append(jnp.where(visible, s, -jnp.inf))
        masked = jnp.concatenate(parts, axis=1)
        peak = jnp.max(masked, axis=1, keepdims=True)
        w = jnp.exp(masked - peak)
        totals[h] = jnp.sum(w, axis=1, keepdims=True)
        weights[h] = w.astype(jnp.bfloat16)
        return carry

    lax.fori_loop(0, heads, score_head, 0)

    def accumulate(block, v_src, first):
        def one_head(h, carry):
            cols = pl.ds(pl.multiple_of(h * HEAD_DIM, HEAD_DIM), HEAD_DIM)
            w = weights[h, :, pl.ds(block * rows, rows)]
            part = jnp.dot(w, v_src[:, cols], preferred_element_type=jnp.float32)
            if first:
                acc[:, cols] = part
            else:
                acc[:, cols] = acc[:, cols] + part
            return carry

        lax.fori_loop(0, heads, one_head, 0)

    accumulate(3, vstage, True)
    start_relay(v_relay_near, v_relay_far, v_incoming)
    accumulate(1, vslots.at[1], False)

    @pl.when(me >= 1)
    def _():
        v_incoming(2).wait_recv()

    accumulate(2, vslots.at[2], False)

    @pl.when(me >= 3)
    def _():
        v_incoming(0).wait_recv()

    accumulate(0, vslots.at[0], False)

    def finish(h, carry):
        cols = pl.ds(pl.multiple_of(h * HEAD_DIM, HEAD_DIM), HEAD_DIM)
        out_ref[:, cols] = acc[:, cols] / totals[h]
        return carry

    lax.fori_loop(0, heads, finish, 0)

    @pl.when(me + 1 < count)
    def _():
        edge.wait_send()

    finish_sends(k_far, k_near, k_relay_near, k_relay_far)
    finish_sends(v_far, v_near, v_relay_near, v_relay_far)


def fused_call(keys, feats, short_filter, long_filter, query):
    count = lax.axis_size("ctx")
    rows, width = keys.shape
    taps = long_filter.shape[0]
    heads = width // HEAD_DIM
    edge_rows = rows // 2 + 48
    vmem = pl.BlockSpec(memory_space=pltpu.VMEM)
    return pl.pallas_call(
        functools.partial(fused_kernel, count),
        out_shape=(
            jax.ShapeDtypeStruct((rows, width), jnp.float32),
            jax.ShapeDtypeStruct((rows, width), jnp.float32),
        ),
        in_specs=[vmem] * 5,
        out_specs=(vmem, vmem),
        scratch_shapes=[
            pltpu.VMEM((edge_rows, width), jnp.bfloat16),
            pltpu.VMEM((edge_rows, width), jnp.bfloat16),
            pltpu.VMEM((edge_rows, width), jnp.bfloat16),
            pltpu.VMEM((3, rows, width), keys.dtype),
            pltpu.VMEM((3, rows, width), jnp.bfloat16),
            pltpu.VMEM((rows, width), jnp.bfloat16),
            pltpu.VMEM((rows, width), jnp.bfloat16),
            pltpu.VMEM((3, rows + 8, width), jnp.float32),
            pltpu.VMEM((rows, width), jnp.float32),
            pltpu.VMEM((rows + taps, width), jnp.float32),
            pltpu.VMEM((8, rows + taps, 128), jnp.float32),
            pltpu.VMEM((heads, rows, WINDOW_BLOCKS * rows), jnp.bfloat16),
            pltpu.VMEM((heads, rows, 1), jnp.float32),
            pltpu.VMEM((rows, width), jnp.float32),
            pltpu.SemaphoreType.DMA((9,)),
            pltpu.SemaphoreType.DMA((7,)),
            pltpu.SemaphoreType.DMA((2,)),
        ],
        compiler_params=pltpu.CompilerParams(
            collective_id=0, has_side_effects=True, vmem_limit_bytes=60 * 1024 * 1024
        ),
    )(keys, feats, short_filter, long_filter, query)


def body(hyena_features, short_filter, long_filter, att_query, att_key):
    gated, attended = fused_call(att_key, hyena_features, short_filter, long_filter, att_query)
    return gated.astype(jnp.bfloat16), attended.astype(jnp.bfloat16)


def solution(mesh):
    return jax.shard_map(
        body,
        mesh=mesh,
        in_specs=(
            P(None, ("dp", "ctx"), "tp"),
            P(None, None, "tp"),
            P(None, "tp"),
            P(("dp", "ctx"), "tp"),
            P(("dp", "ctx"), "tp"),
        ),
        out_specs=(P(("dp", "ctx"), "tp"), P(("dp", "ctx"), "tp")),
        check_vma=False,
    )
```

```python
import functools
import math

import jax
import jax.numpy as jnp
from jax import lax
from jax.experimental import pallas as pl
from jax.experimental.pallas import tpu as pltpu
from jax.sharding import PartitionSpec as P

MESH = pl.DeviceIdType.MESH

HEAD_DIM = 128
WINDOW_BLOCKS = 4


class SplitCopy:
    def __init__(self, source, target, send_sem, recv_sem, peer):
        half = source.shape[0] // 2
        self.whole = pltpu.make_async_remote_copy(
            src_ref=source, dst_ref=target, send_sem=send_sem, recv_sem=recv_sem,
            device_id={"ctx": peer}, device_id_type=MESH,
        )
        self.parts = [
            pltpu.make_async_remote_copy(
                src_ref=source.at[pl.ds(start, half)], dst_ref=target.at[pl.ds(start, half)],
                send_sem=send_sem, recv_sem=recv_sem, device_id={"ctx": peer},
                device_id_type=MESH,
            )
            for start in (0, half)
        ]

    def start(self):
        for part in self.parts:
            part.start()

    def wait_send(self):
        self.whole.wait_send()


def fused_kernel(
    count, k_ref, feats_ref, sf_ref, lf_ref, q_ref,
    hm_out, out_ref,
    edge_stage, edge_send, edge_slot, kslots, vslots, vsrc, vstage, raw, qmix, ext, shifted,
    weights, totals, acc, send_sems, recv_sems, copy_sem,
):
    me = lax.axis_index("ctx")
    odd = lax.rem(me, 2) == 1
    even = jnp.logical_not(odd)
    rows, width = k_ref.shape
    taps = lf_ref.shape[0]
    heads = width // HEAD_DIM
    scale = 1.0 / math.sqrt(HEAD_DIM)

    @pl.when(me < 3)
    def _():
        for slot, first in ((0, 3), (1, 2), (2, 1)):
            @pl.when(me < first)
            def _():
                kslots[slot] = jnp.zeros((rows, width), kslots.dtype)
                vslots[slot] = jnp.zeros((rows, width), vslots.dtype)

    @pl.when(me == 0)
    def _():
        edge_slot[...] = jnp.zeros(edge_slot.shape, edge_slot.dtype)

    barrier = pltpu.get_barrier_semaphore()
    for step in (-2, -1, 1, 2):
        peer = me + step

        @pl.when((peer >= 0) & (peer < count))
        def _():
            pl.semaphore_signal(barrier, inc=1, device_id={"ctx": peer}, device_id_type=MESH)

    neighbours = (
        (me >= 2).astype(jnp.int32) + (me >= 1).astype(jnp.int32)
        + (me + 1 < count).astype(jnp.int32) + (me + 2 < count).astype(jnp.int32)
    )
    pl.semaphore_wait(barrier, neighbours)

    def route(slots, src, base_send, base_recv):
        def send(source, slot, peer, sem):
            return SplitCopy(
                source, slots.at[slot], send_sems.at[base_send + sem],
                recv_sems.at[base_recv + slot], peer,
            )

        def incoming(slot):
            return pltpu.make_async_remote_copy(
                src_ref=src, dst_ref=slots.at[slot], send_sem=send_sems.at[base_send],
                recv_sem=recv_sems.at[base_recv + slot], device_id={"ctx": me},
                device_id_type=MESH,
            )

        far = send(src, 1, me + 2, 0)
        near = send(src, 2, me + 1, 1)
        relay_near = send(slots.at[1], 2, me - 1, 2)
        relay_far = send(slots.at[1], 0, me + 1, 3)
        return far, near, relay_near, relay_far, incoming

    def start_first(far, near):
        @pl.when(me + 2 < count)
        def _():
            far.start()

        @pl.when(even)
        def _():
            near.start()

    def start_relay(relay_near, relay_far, incoming):
        @pl.when(me >= 2)
        def _():
            incoming(1).wait_recv()

            @pl.when(odd)
            def _():
                relay_near.start()

            @pl.when(jnp.logical_or(even, me + 1 < count))
            def _():
                relay_far.start()

    def finish_sends(far, near, relay_near, relay_far):
        @pl.when(me + 2 < count)
        def _():
            far.wait_send()

        @pl.when(even)
        def _():
            near.wait_send()

        @pl.when((me >= 2) & odd)
        def _():
            relay_near.wait_send()

        @pl.when((me >= 2) & jnp.logical_or(even, me + 1 < count))
        def _():
            relay_far.wait_send()

    front = 8
    half = rows // 2
    for which in range(3):
        raw[which, pl.ds(0, front), :] = jnp.zeros((front, width), jnp.float32)
        raw[which, pl.ds(front, rows), :] = feats_ref[which].astype(jnp.float32)

    def mix(which, start, length):
        w = sf_ref[which]
        x = raw.at[which]
        return (
            w[0:1] * x[pl.ds(front + start, length), :]
            + w[1:2] * x[pl.ds(front + start - 1, length), :]
        ) + w[2:3] * x[pl.ds(front + start - 2, length), :]

    edge_stage[pl.ds(0, half), :] = (mix(1, half, half) * mix(2, half, half)).astype(
        edge_stage.dtype
    )
    for which in range(3):
        edge_stage[pl.ds(half + 16 * which, 16), :] = feats_ref[which, pl.ds(rows - 16, 16), :]
    staged = pltpu.make_async_copy(edge_stage, edge_send, copy_sem.at[1])
    staged.start()
    staged.wait()

    edge = pltpu.make_async_remote_copy(
        src_ref=edge_send, dst_ref=edge_slot, send_sem=send_sems.at[8],
        recv_sem=recv_sems.at[6], device_id={"ctx": me + 1}, device_id_type=MESH,
    )
    edge_in = pltpu.make_async_remote_copy(
        src_ref=edge_send, dst_ref=edge_slot, send_sem=send_sems.at[8],
        recv_sem=recv_sems.at[6], device_id={"ctx": me}, device_id_type=MESH,
    )

    @pl.when(me + 1 < count)
    def _():
        edge.start()

    k_far, k_near, k_relay_near, k_relay_far, k_incoming = route(kslots, k_ref, 0, 0)
    start_first(k_far, k_near)

    @pl.when(me >= 1)
    def _():
        edge_in.wait_recv()

    for which in range(3):
        older = edge_slot[pl.ds(half + 16 * which, 16), :].astype(jnp.float32)
        raw[which, pl.ds(0, front), :] = older[16 - front :]

    qmix[...] = mix(0, 0, rows)
    ext[pl.ds(0, taps), :] = edge_slot[pl.ds(0, taps), :].astype(jnp.float32)
    ext[pl.ds(taps, rows), :] = (mix(1, 0, rows) * mix(2, 0, rows)).astype(
        jnp.bfloat16
    ).astype(jnp.float32)

    def chunk(c, carry):
        cols = pl.ds(pl.multiple_of(c * 128, 128), 128)
        for b in range(8):
            shifted[b, pl.ds(8, rows + taps - 8), :] = ext[pl.ds(8 - b, rows + taps - 8), cols]
        total = jnp.zeros((rows, 128), jnp.float32)
        for a in range(taps // 8):
            for b in range(8):
                j = 8 * a + b
                total = total + lf_ref[pl.ds(j, 1), cols] * shifted[b, pl.ds(taps - 8 * a, rows), :]
        gated = qmix[:, cols] * total
        hm_out[:, cols] = gated
        vsrc[:, cols] = gated.astype(vsrc.dtype)
        return carry

    lax.fori_loop(0, width // 128, chunk, 0)

    local = pltpu.make_async_copy(vsrc, vstage, copy_sem.at[0])
    local.start()
    local.wait()

    v_far, v_near, v_relay_near, v_relay_far, v_incoming = route(vslots, vstage, 4, 3)
    start_first(v_far, v_near)
    start_relay(k_relay_near, k_relay_far, k_incoming)

    @pl.when(me >= 1)
    def _():
        k_incoming(2).wait_recv()

    @pl.when(me >= 3)
    def _():
        k_incoming(0).wait_recv()

    def score_head(h, carry):
        cols = pl.ds(pl.multiple_of(h * HEAD_DIM, HEAD_DIM), HEAD_DIM)
        q = q_ref[:, cols]
        parts = []
        for b, keys in enumerate((kslots.at[0], kslots.at[1], kslots.at[2], k_ref)):
            s = lax.dot_general(
                q, keys[:, cols], (((1,), (1,)), ((), ())), preferred_element_type=jnp.float32
            ) * scale
            t = lax.broadcasted_iota(jnp.int32, (rows, rows), 0)
            u = lax.broadcasted_iota(jnp.int32, (rows, rows), 1)
            if b == 3:
                visible = u <= t
            else:
                visible = jnp.broadcast_to(me - 3 + b >= 0, (rows, rows))
            parts.append(jnp.where(visible, s, -jnp.inf))
        masked = jnp.concatenate(parts, axis=1)
        peak = jnp.max(masked, axis=1, keepdims=True)
        w = jnp.exp(masked - peak)
        totals[h] = jnp.sum(w, axis=1, keepdims=True)
        weights[h] = w.astype(jnp.bfloat16)
        return carry

    lax.fori_loop(0, heads, score_head, 0)

    def accumulate(block, v_src, first):
        def one_head(h, carry):
            cols = pl.ds(pl.multiple_of(h * HEAD_DIM, HEAD_DIM), HEAD_DIM)
            w = weights[h, :, pl.ds(block * rows, rows)]
            part = jnp.dot(w, v_src[:, cols], preferred_element_type=jnp.float32)
            if first:
                acc[:, cols] = part
            else:
                acc[:, cols] = acc[:, cols] + part
            return carry

        lax.fori_loop(0, heads, one_head, 0)

    accumulate(3, vstage, True)
    start_relay(v_relay_near, v_relay_far, v_incoming)
    accumulate(1, vslots.at[1], False)

    @pl.when(me >= 1)
    def _():
        v_incoming(2).wait_recv()

    accumulate(2, vslots.at[2], False)

    @pl.when(me >= 3)
    def _():
        v_incoming(0).wait_recv()

    accumulate(0, vslots.at[0], False)

    def finish(h, carry):
        cols = pl.ds(pl.multiple_of(h * HEAD_DIM, HEAD_DIM), HEAD_DIM)
        out_ref[:, cols] = acc[:, cols] / totals[h]
        return carry

    lax.fori_loop(0, heads, finish, 0)

    @pl.when(me + 1 < count)
    def _():
        edge.wait_send()

    finish_sends(k_far, k_near, k_relay_near, k_relay_far)
    finish_sends(v_far, v_near, v_relay_near, v_relay_far)


def fused_call(keys, feats, short_filter, long_filter, query):
    count = lax.axis_size("ctx")
    rows, width = keys.shape
    taps = long_filter.shape[0]
    heads = width // HEAD_DIM
    edge_rows = rows // 2 + 48
    vmem = pl.BlockSpec(memory_space=pltpu.VMEM)
    return pl.pallas_call(
        functools.partial(fused_kernel, count),
        out_shape=(
            jax.ShapeDtypeStruct((rows, width), jnp.float32),
            jax.ShapeDtypeStruct((rows, width), jnp.float32),
        ),
        in_specs=[vmem] * 5,
        out_specs=(vmem, vmem),
        scratch_shapes=[
            pltpu.VMEM((edge_rows, width), jnp.bfloat16),
            pltpu.VMEM((edge_rows, width), jnp.bfloat16),
            pltpu.VMEM((edge_rows, width), jnp.bfloat16),
            pltpu.VMEM((3, rows, width), keys.dtype),
            pltpu.VMEM((3, rows, width), jnp.bfloat16),
            pltpu.VMEM((rows, width), jnp.bfloat16),
            pltpu.VMEM((rows, width), jnp.bfloat16),
            pltpu.VMEM((3, rows + 8, width), jnp.float32),
            pltpu.VMEM((rows, width), jnp.float32),
            pltpu.VMEM((rows + taps, width), jnp.float32),
            pltpu.VMEM((8, rows + taps, 128), jnp.float32),
            pltpu.VMEM((heads, rows, WINDOW_BLOCKS * rows), jnp.bfloat16),
            pltpu.VMEM((heads, rows, 1), jnp.float32),
            pltpu.VMEM((rows, width), jnp.float32),
            pltpu.SemaphoreType.DMA((9,)),
            pltpu.SemaphoreType.DMA((7,)),
            pltpu.SemaphoreType.DMA((2,)),
        ],
        compiler_params=pltpu.CompilerParams(
            collective_id=0, has_side_effects=True, vmem_limit_bytes=60 * 1024 * 1024
        ),
    )(keys, feats, short_filter, long_filter, query)


def body(hyena_features, short_filter, long_filter, att_query, att_key):
    gated, attended = fused_call(att_key, hyena_features, short_filter, long_filter, att_query)
    return gated.astype(jnp.bfloat16), attended.astype(jnp.bfloat16)


def solution(mesh):
    return jax.shard_map(
        body,
        mesh=mesh,
        in_specs=(
            P(None, ("dp", "ctx"), "tp"),
            P(None, None, "tp"),
            P(None, "tp"),
            P(("dp", "ctx"), "tp"),
            P(("dp", "ctx"), "tp"),
        ),
        out_specs=(P(("dp", "ctx"), "tp"), P(("dp", "ctx"), "tp")),
        check_vma=False,
    )
```

```python
import functools
import math

import jax
import jax.numpy as jnp
from jax import lax
from jax.experimental import pallas as pl
from jax.experimental.pallas import tpu as pltpu
from jax.sharding import PartitionSpec as P

MESH = pl.DeviceIdType.MESH

HEAD_DIM = 128
WINDOW_BLOCKS = 4


def fused_kernel(
    count, k_ref, feats_ref, sf_ref, lf_ref, q_ref,
    hm_out, out_ref,
    edge_stage, edge_send, edge_slot, kslots, vslots, vsrc, vstage, raw, qmix, ext, shifted,
    weights, totals, acc, send_sems, recv_sems, copy_sem,
):
    me = lax.axis_index("ctx")
    odd = lax.rem(me, 2) == 1
    even = jnp.logical_not(odd)
    rows, width = k_ref.shape
    taps = lf_ref.shape[0]
    heads = width // HEAD_DIM
    scale = 1.0 / math.sqrt(HEAD_DIM)

    @pl.when(me < 3)
    def _():
        for slot, first in ((0, 3), (1, 2), (2, 1)):
            @pl.when(me < first)
            def _():
                kslots[slot] = jnp.zeros((rows, width), kslots.dtype)
                vslots[slot] = jnp.zeros((rows, width), vslots.dtype)

    @pl.when(me == 0)
    def _():
        edge_slot[...] = jnp.zeros(edge_slot.shape, edge_slot.dtype)

    barrier = pltpu.get_barrier_semaphore()
    for step in (-2, -1, 1, 2):
        peer = me + step

        @pl.when((peer >= 0) & (peer < count))
        def _():
            pl.semaphore_signal(barrier, inc=1, device_id={"ctx": peer}, device_id_type=MESH)

    neighbours = (
        (me >= 2).astype(jnp.int32) + (me >= 1).astype(jnp.int32)
        + (me + 1 < count).astype(jnp.int32) + (me + 2 < count).astype(jnp.int32)
    )
    pl.semaphore_wait(barrier, neighbours)

    def route(slots, src, base_send, base_recv):
        def send(source, slot, peer, sem):
            return pltpu.make_async_remote_copy(
                src_ref=source, dst_ref=slots.at[slot], send_sem=send_sems.at[base_send + sem],
                recv_sem=recv_sems.at[base_recv + slot], device_id={"ctx": peer},
                device_id_type=MESH,
            )

        def incoming(slot):
            return pltpu.make_async_remote_copy(
                src_ref=src, dst_ref=slots.at[slot], send_sem=send_sems.at[base_send],
                recv_sem=recv_sems.at[base_recv + slot], device_id={"ctx": me},
                device_id_type=MESH,
            )

        far = send(src, 1, me + 2, 0)
        near = send(src, 2, me + 1, 1)
        relay_near = send(slots.at[1], 2, me - 1, 2)
        relay_far = send(slots.at[1], 0, me + 1, 3)
        return far, near, relay_near, relay_far, incoming

    def start_first(far, near):
        @pl.when(me + 2 < count)
        def _():
            far.start()

        @pl.when(even)
        def _():
            near.start()

    def start_relay(relay_near, relay_far, incoming):
        @pl.when(me >= 2)
        def _():
            incoming(1).wait_recv()

            @pl.when(odd)
            def _():
                relay_near.start()

            @pl.when(jnp.logical_or(even, me + 1 < count))
            def _():
                relay_far.start()

    def finish_sends(far, near, relay_near, relay_far):
        @pl.when(me + 2 < count)
        def _():
            far.wait_send()

        @pl.when(even)
        def _():
            near.wait_send()

        @pl.when((me >= 2) & odd)
        def _():
            relay_near.wait_send()

        @pl.when((me >= 2) & jnp.logical_or(even, me + 1 < count))
        def _():
            relay_far.wait_send()

    front = 8
    half = rows // 2
    for which in range(3):
        raw[which, pl.ds(0, front), :] = jnp.zeros((front, width), jnp.float32)
        raw[which, pl.ds(front, rows), :] = feats_ref[which].astype(jnp.float32)

    def mix(which, start, length):
        w = sf_ref[which]
        x = raw.at[which]
        return (
            w[0:1] * x[pl.ds(front + start, length), :]
            + w[1:2] * x[pl.ds(front + start - 1, length), :]
        ) + w[2:3] * x[pl.ds(front + start - 2, length), :]

    edge_stage[pl.ds(0, half), :] = (mix(1, half, half) * mix(2, half, half)).astype(
        edge_stage.dtype
    )
    for which in range(3):
        edge_stage[pl.ds(half + 16 * which, 16), :] = feats_ref[which, pl.ds(rows - 16, 16), :]
    staged = pltpu.make_async_copy(edge_stage, edge_send, copy_sem.at[1])
    staged.start()
    staged.wait()

    edge = pltpu.make_async_remote_copy(
        src_ref=edge_send, dst_ref=edge_slot, send_sem=send_sems.at[8],
        recv_sem=recv_sems.at[6], device_id={"ctx": me + 1}, device_id_type=MESH,
    )
    edge_in = pltpu.make_async_remote_copy(
        src_ref=edge_send, dst_ref=edge_slot, send_sem=send_sems.at[8],
        recv_sem=recv_sems.at[6], device_id={"ctx": me}, device_id_type=MESH,
    )

    @pl.when(me + 1 < count)
    def _():
        edge.start()

    k_far, k_near, k_relay_near, k_relay_far, k_incoming = route(kslots, k_ref, 0, 0)
    start_first(k_far, k_near)

    @pl.when(me >= 1)
    def _():
        edge_in.wait_recv()

    for which in range(3):
        older = edge_slot[pl.ds(half + 16 * which, 16), :].astype(jnp.float32)
        raw[which, pl.ds(0, front), :] = older[16 - front :]

    qmix[...] = mix(0, 0, rows)
    ext[pl.ds(0, taps), :] = edge_slot[pl.ds(0, taps), :].astype(jnp.float32)
    ext[pl.ds(taps, rows), :] = (mix(1, 0, rows) * mix(2, 0, rows)).astype(
        jnp.bfloat16
    ).astype(jnp.float32)

    def chunk(c, carry):
        cols = pl.ds(pl.multiple_of(c * 128, 128), 128)
        for b in range(8):
            shifted[b, pl.ds(8, rows + taps - 8), :] = ext[pl.ds(8 - b, rows + taps - 8), cols]
        total = jnp.zeros((rows, 128), jnp.float32)
        for a in range(taps // 8):
            for b in range(8):
                j = 8 * a + b
                total = total + lf_ref[pl.ds(j, 1), cols] * shifted[b, pl.ds(taps - 8 * a, rows), :]
        gated = qmix[:, cols] * total
        hm_out[:, cols] = gated
        vsrc[:, cols] = gated.astype(vsrc.dtype)
        return carry

    lax.fori_loop(0, width // 128, chunk, 0)

    local = pltpu.make_async_copy(vsrc, vstage, copy_sem.at[0])
    local.start()
    local.wait()

    v_far, v_near, v_relay_near, v_relay_far, v_incoming = route(vslots, vstage, 4, 3)
    start_first(v_far, v_near)
    start_relay(k_relay_near, k_relay_far, k_incoming)

    @pl.when(me >= 1)
    def _():
        k_incoming(2).wait_recv()

    @pl.when(me >= 3)
    def _():
        k_incoming(0).wait_recv()

    def score_head(h, carry):
        cols = pl.ds(pl.multiple_of(h * HEAD_DIM, HEAD_DIM), HEAD_DIM)
        q = q_ref[:, cols]
        parts = []
        for b, keys in enumerate((kslots.at[0], kslots.at[1], kslots.at[2], k_ref)):
            s = lax.dot_general(
                q, keys[:, cols], (((1,), (1,)), ((), ())), preferred_element_type=jnp.float32
            ) * scale
            t = lax.broadcasted_iota(jnp.int32, (rows, rows), 0)
            u = lax.broadcasted_iota(jnp.int32, (rows, rows), 1)
            if b == 3:
                visible = u <= t
            else:
                visible = jnp.broadcast_to(me - 3 + b >= 0, (rows, rows))
            parts.append(jnp.where(visible, s, -jnp.inf))
        masked = jnp.concatenate(parts, axis=1)
        peak = jnp.max(masked, axis=1, keepdims=True)
        w = jnp.exp(masked - peak)
        totals[h] = jnp.sum(w, axis=1, keepdims=True)
        weights[h] = w.astype(jnp.bfloat16)
        return carry

    lax.fori_loop(0, heads, score_head, 0)

    def accumulate(block, v_src, first):
        def one_head(h, carry):
            cols = pl.ds(pl.multiple_of(h * HEAD_DIM, HEAD_DIM), HEAD_DIM)
            w = weights[h, :, pl.ds(block * rows, rows)]
            part = jnp.dot(w, v_src[:, cols], preferred_element_type=jnp.float32)
            if first:
                acc[:, cols] = part
            else:
                acc[:, cols] = acc[:, cols] + part
            return carry

        lax.fori_loop(0, heads, one_head, 0)

    accumulate(3, vstage, True)
    start_relay(v_relay_near, v_relay_far, v_incoming)
    accumulate(1, vslots.at[1], False)

    @pl.when(me >= 1)
    def _():
        v_incoming(2).wait_recv()

    accumulate(2, vslots.at[2], False)

    @pl.when(me >= 3)
    def _():
        v_incoming(0).wait_recv()

    accumulate(0, vslots.at[0], False)

    def finish(h, carry):
        cols = pl.ds(pl.multiple_of(h * HEAD_DIM, HEAD_DIM), HEAD_DIM)
        out_ref[:, cols] = acc[:, cols] / totals[h]
        return carry

    lax.fori_loop(0, heads, finish, 0)

    @pl.when(me + 1 < count)
    def _():
        edge.wait_send()

    finish_sends(k_far, k_near, k_relay_near, k_relay_far)
    finish_sends(v_far, v_near, v_relay_near, v_relay_far)


def fused_call(keys, feats, short_filter, long_filter, query):
    count = lax.axis_size("ctx")
    rows, width = keys.shape
    taps = long_filter.shape[0]
    heads = width // HEAD_DIM
    edge_rows = rows // 2 + 48
    vmem = pl.BlockSpec(memory_space=pltpu.VMEM)
    return pl.pallas_call(
        functools.partial(fused_kernel, count),
        out_shape=(
            jax.ShapeDtypeStruct((rows, width), jnp.float32),
            jax.ShapeDtypeStruct((rows, width), jnp.float32),
        ),
        in_specs=[vmem] * 5,
        out_specs=(vmem, vmem),
        scratch_shapes=[
            pltpu.VMEM((edge_rows, width), jnp.bfloat16),
            pltpu.VMEM((edge_rows, width), jnp.bfloat16),
            pltpu.VMEM((edge_rows, width), jnp.bfloat16),
            pltpu.VMEM((3, rows, width), keys.dtype),
            pltpu.VMEM((3, rows, width), jnp.bfloat16),
            pltpu.VMEM((rows, width), jnp.bfloat16),
            pltpu.VMEM((rows, width), jnp.bfloat16),
            pltpu.VMEM((3, rows + 8, width), jnp.float32),
            pltpu.VMEM((rows, width), jnp.float32),
            pltpu.VMEM((rows + taps, width), jnp.float32),
            pltpu.VMEM((8, rows + taps, 128), jnp.float32),
            pltpu.VMEM((heads, rows, WINDOW_BLOCKS * rows), jnp.bfloat16),
            pltpu.VMEM((heads, rows, 1), jnp.float32),
            pltpu.VMEM((rows, width), jnp.float32),
            pltpu.SemaphoreType.DMA((9,)),
            pltpu.SemaphoreType.DMA((7,)),
            pltpu.SemaphoreType.DMA((2,)),
        ],
        compiler_params=pltpu.CompilerParams(
            collective_id=0, has_side_effects=True, vmem_limit_bytes=60 * 1024 * 1024
        ),
    )(keys, feats, short_filter, long_filter, query)


def round_kernel(gated_ref, attended_ref, hm_out, out_ref):
    hm_out[...] = gated_ref[...].astype(hm_out.dtype)
    out_ref[...] = attended_ref[...].astype(out_ref.dtype)


def round_outputs(gated, attended):
    vmem = pl.BlockSpec(memory_space=pltpu.VMEM)
    return pl.pallas_call(
        round_kernel,
        out_shape=(
            jax.ShapeDtypeStruct(gated.shape, jnp.bfloat16),
            jax.ShapeDtypeStruct(attended.shape, jnp.bfloat16),
        ),
        in_specs=[vmem] * 2,
        out_specs=(vmem, vmem),
    )(gated, attended)


def body(hyena_features, short_filter, long_filter, att_query, att_key):
    gated, attended = fused_call(att_key, hyena_features, short_filter, long_filter, att_query)
    return round_outputs(gated, attended)


def solution(mesh):
    return jax.shard_map(
        body,
        mesh=mesh,
        in_specs=(
            P(None, ("dp", "ctx"), "tp"),
            P(None, None, "tp"),
            P(None, "tp"),
            P(("dp", "ctx"), "tp"),
            P(("dp", "ctx"), "tp"),
        ),
        out_specs=(P(("dp", "ctx"), "tp"), P(("dp", "ctx"), "tp")),
        check_vma=False,
    )
```

```python
import functools
import math

import jax
import jax.numpy as jnp
from jax import lax
from jax.experimental import pallas as pl
from jax.experimental.pallas import tpu as pltpu
from jax.sharding import PartitionSpec as P

MESH = pl.DeviceIdType.MESH

HEAD_DIM = 128
WINDOW_BLOCKS = 4


def fused_kernel(
    count, k_ref, feats_ref, sf_ref, lf_ref, q_ref,
    hm_out, out_ref,
    edge_stage, edge_send, edge_slot, kslots, vslots, vsrc, vstage, raw, qmix, ext, shifted,
    weights, totals, acc, send_sems, recv_sems, copy_sem,
):
    me = lax.axis_index("ctx")
    odd = lax.rem(me, 2) == 1
    even = jnp.logical_not(odd)
    rows, width = k_ref.shape
    taps = lf_ref.shape[0]
    heads = width // HEAD_DIM
    scale = 1.0 / math.sqrt(HEAD_DIM)

    @pl.when(me < 3)
    def _():
        for slot, first in ((0, 3), (1, 2), (2, 1)):
            @pl.when(me < first)
            def _():
                kslots[slot] = jnp.zeros((rows, width), kslots.dtype)
                vslots[slot] = jnp.zeros((rows, width), vslots.dtype)

    @pl.when(me == 0)
    def _():
        edge_slot[...] = jnp.zeros(edge_slot.shape, edge_slot.dtype)

    barrier = pltpu.get_barrier_semaphore()
    for step in (-2, -1, 1, 2):
        peer = me + step

        @pl.when((peer >= 0) & (peer < count))
        def _():
            pl.semaphore_signal(barrier, inc=1, device_id={"ctx": peer}, device_id_type=MESH)

    neighbours = (
        (me >= 2).astype(jnp.int32) + (me >= 1).astype(jnp.int32)
        + (me + 1 < count).astype(jnp.int32) + (me + 2 < count).astype(jnp.int32)
    )
    pl.semaphore_wait(barrier, neighbours)

    def route(slots, src, base_send, base_recv):
        def send(source, slot, peer, sem):
            return pltpu.make_async_remote_copy(
                src_ref=source, dst_ref=slots.at[slot], send_sem=send_sems.at[base_send + sem],
                recv_sem=recv_sems.at[base_recv + slot], device_id={"ctx": peer},
                device_id_type=MESH,
            )

        def incoming(slot):
            return pltpu.make_async_remote_copy(
                src_ref=src, dst_ref=slots.at[slot], send_sem=send_sems.at[base_send],
                recv_sem=recv_sems.at[base_recv + slot], device_id={"ctx": me},
                device_id_type=MESH,
            )

        far = send(src, 1, me + 2, 0)
        near = send(src, 2, me + 1, 1)
        relay_near = send(slots.at[1], 2, me - 1, 2)
        relay_far = send(slots.at[1], 0, me + 1, 3)
        return far, near, relay_near, relay_far, incoming

    def start_first(far, near):
        @pl.when(me + 2 < count)
        def _():
            far.start()

        @pl.when(even)
        def _():
            near.start()

    def start_relay(relay_near, relay_far, incoming):
        @pl.when(me >= 2)
        def _():
            incoming(1).wait_recv()

            @pl.when(odd)
            def _():
                relay_near.start()

            @pl.when(jnp.logical_or(even, me + 1 < count))
            def _():
                relay_far.start()

    def finish_sends(far, near, relay_near, relay_far):
        @pl.when(me + 2 < count)
        def _():
            far.wait_send()

        @pl.when(even)
        def _():
            near.wait_send()

        @pl.when((me >= 2) & odd)
        def _():
            relay_near.wait_send()

        @pl.when((me >= 2) & jnp.logical_or(even, me + 1 < count))
        def _():
            relay_far.wait_send()

    front = 8
    half = rows // 2
    for which in range(3):
        raw[which, pl.ds(0, front), :] = jnp.zeros((front, width), jnp.float32)
        raw[which, pl.ds(front, rows), :] = feats_ref[which].astype(jnp.float32)

    def mix(which, start, length):
        w = sf_ref[which]
        x = raw.at[which]
        return (
            w[0:1] * x[pl.ds(front + start, length), :]
            + w[1:2] * x[pl.ds(front + start - 1, length), :]
        ) + w[2:3] * x[pl.ds(front + start - 2, length), :]

    edge_stage[pl.ds(0, half), :] = (mix(1, half, half) * mix(2, half, half)).astype(
        edge_stage.dtype
    )
    line = lax.broadcasted_iota(jnp.int32, (16, width), 0)
    packed = jnp.zeros((16, width), jnp.float32)
    for which in range(3):
        last = feats_ref[which, pl.ds(rows - 16, 16), :].astype(jnp.float32)
        for r in range(2):
            packed = jnp.where(line == 2 * which + r, last[14 + r : 15 + r], packed)
    edge_stage[pl.ds(half, 16), :] = packed.astype(edge_stage.dtype)
    staged = pltpu.make_async_copy(edge_stage, edge_send, copy_sem.at[1])
    staged.start()
    staged.wait()

    edge = pltpu.make_async_remote_copy(
        src_ref=edge_send, dst_ref=edge_slot, send_sem=send_sems.at[8],
        recv_sem=recv_sems.at[6], device_id={"ctx": me + 1}, device_id_type=MESH,
    )
    edge_in = pltpu.make_async_remote_copy(
        src_ref=edge_send, dst_ref=edge_slot, send_sem=send_sems.at[8],
        recv_sem=recv_sems.at[6], device_id={"ctx": me}, device_id_type=MESH,
    )

    @pl.when(me + 1 < count)
    def _():
        edge.start()

    k_far, k_near, k_relay_near, k_relay_far, k_incoming = route(kslots, k_ref, 0, 0)
    start_first(k_far, k_near)

    @pl.when(me >= 1)
    def _():
        edge_in.wait_recv()

    older = edge_slot[pl.ds(half, 16), :].astype(jnp.float32)
    line = lax.broadcasted_iota(jnp.int32, (front, width), 0)
    for which in range(3):
        tile = jnp.zeros((front, width), jnp.float32)
        for r in range(2):
            tile = jnp.where(line == front - 2 + r, older[2 * which + r : 2 * which + r + 1], tile)
        raw[which, pl.ds(0, front), :] = tile

    qmix[...] = mix(0, 0, rows)
    ext[pl.ds(0, taps), :] = edge_slot[pl.ds(0, taps), :].astype(jnp.float32)
    ext[pl.ds(taps, rows), :] = (mix(1, 0, rows) * mix(2, 0, rows)).astype(
        jnp.bfloat16
    ).astype(jnp.float32)

    def chunk(c, carry):
        cols = pl.ds(pl.multiple_of(c * 128, 128), 128)
        for b in range(8):
            shifted[b, pl.ds(8, rows + taps - 8), :] = ext[pl.ds(8 - b, rows + taps - 8), cols]
        total = jnp.zeros((rows, 128), jnp.float32)
        for a in range(taps // 8):
            for b in range(8):
                j = 8 * a + b
                total = total + lf_ref[pl.ds(j, 1), cols] * shifted[b, pl.ds(taps - 8 * a, rows), :]
        gated = (qmix[:, cols] * total).astype(vsrc.dtype)
        hm_out[:, cols] = gated
        vsrc[:, cols] = gated
        return carry

    lax.fori_loop(0, width // 128, chunk, 0)

    local = pltpu.make_async_copy(vsrc, vstage, copy_sem.at[0])
    local.start()
    local.wait()

    v_far, v_near, v_relay_near, v_relay_far, v_incoming = route(vslots, vstage, 4, 3)
    start_first(v_far, v_near)
    start_relay(k_relay_near, k_relay_far, k_incoming)

    @pl.when(me >= 1)
    def _():
        k_incoming(2).wait_recv()

    @pl.when(me >= 3)
    def _():
        k_incoming(0).wait_recv()

    def score_head(h, carry):
        cols = pl.ds(pl.multiple_of(h * HEAD_DIM, HEAD_DIM), HEAD_DIM)
        q = q_ref[:, cols]
        parts = []
        for b, keys in enumerate((kslots.at[0], kslots.at[1], kslots.at[2], k_ref)):
            s = lax.dot_general(
                q, keys[:, cols], (((1,), (1,)), ((), ())), preferred_element_type=jnp.float32
            ) * scale
            t = lax.broadcasted_iota(jnp.int32, (rows, rows), 0)
            u = lax.broadcasted_iota(jnp.int32, (rows, rows), 1)
            if b == 3:
                visible = u <= t
            else:
                visible = jnp.broadcast_to(me - 3 + b >= 0, (rows, rows))
            parts.append(jnp.where(visible, s, -jnp.inf))
        masked = jnp.concatenate(parts, axis=1)
        peak = jnp.max(masked, axis=1, keepdims=True)
        w = jnp.exp(masked - peak)
        totals[h] = jnp.sum(w, axis=1, keepdims=True)
        weights[h] = w.astype(jnp.bfloat16)
        return carry

    lax.fori_loop(0, heads, score_head, 0)

    def accumulate(block, v_src, first):
        def one_head(h, carry):
            cols = pl.ds(pl.multiple_of(h * HEAD_DIM, HEAD_DIM), HEAD_DIM)
            w = weights[h, :, pl.ds(block * rows, rows)]
            part = jnp.dot(w, v_src[:, cols], preferred_element_type=jnp.float32)
            if first:
                acc[:, cols] = part
            else:
                acc[:, cols] = acc[:, cols] + part
            return carry

        lax.fori_loop(0, heads, one_head, 0)

    accumulate(3, vstage, True)
    start_relay(v_relay_near, v_relay_far, v_incoming)
    accumulate(1, vslots.at[1], False)

    @pl.when(me >= 1)
    def _():
        v_incoming(2).wait_recv()

    accumulate(2, vslots.at[2], False)

    @pl.when(me >= 3)
    def _():
        v_incoming(0).wait_recv()

    accumulate(0, vslots.at[0], False)

    def finish(h, carry):
        cols = pl.ds(pl.multiple_of(h * HEAD_DIM, HEAD_DIM), HEAD_DIM)
        out_ref[:, cols] = (acc[:, cols] / totals[h]).astype(out_ref.dtype)
        return carry

    lax.fori_loop(0, heads, finish, 0)

    @pl.when(me + 1 < count)
    def _():
        edge.wait_send()

    finish_sends(k_far, k_near, k_relay_near, k_relay_far)
    finish_sends(v_far, v_near, v_relay_near, v_relay_far)


def fused_call(keys, feats, short_filter, long_filter, query):
    count = lax.axis_size("ctx")
    rows, width = keys.shape
    taps = long_filter.shape[0]
    heads = width // HEAD_DIM
    edge_rows = rows // 2 + 16
    vmem = pl.BlockSpec(memory_space=pltpu.VMEM)
    return pl.pallas_call(
        functools.partial(fused_kernel, count),
        out_shape=(
            jax.ShapeDtypeStruct((rows, width), jnp.bfloat16),
            jax.ShapeDtypeStruct((rows, width), jnp.bfloat16),
        ),
        in_specs=[vmem] * 5,
        out_specs=(vmem, vmem),
        scratch_shapes=[
            pltpu.VMEM((edge_rows, width), jnp.bfloat16),
            pltpu.VMEM((edge_rows, width), jnp.bfloat16),
            pltpu.VMEM((edge_rows, width), jnp.bfloat16),
            pltpu.VMEM((3, rows, width), keys.dtype),
            pltpu.VMEM((3, rows, width), jnp.bfloat16),
            pltpu.VMEM((rows, width), jnp.bfloat16),
            pltpu.VMEM((rows, width), jnp.bfloat16),
            pltpu.VMEM((3, rows + 8, width), jnp.float32),
            pltpu.VMEM((rows, width), jnp.float32),
            pltpu.VMEM((rows + taps, width), jnp.float32),
            pltpu.VMEM((8, rows + taps, 128), jnp.float32),
            pltpu.VMEM((heads, rows, WINDOW_BLOCKS * rows), jnp.bfloat16),
            pltpu.VMEM((heads, rows, 1), jnp.float32),
            pltpu.VMEM((rows, width), jnp.float32),
            pltpu.SemaphoreType.DMA((9,)),
            pltpu.SemaphoreType.DMA((7,)),
            pltpu.SemaphoreType.DMA((2,)),
        ],
        compiler_params=pltpu.CompilerParams(
            collective_id=0, has_side_effects=True, vmem_limit_bytes=60 * 1024 * 1024
        ),
    )(keys, feats, short_filter, long_filter, query)


def round_kernel(gated_ref, attended_ref, hm_out, out_ref):
    hm_out[...] = gated_ref[...]
    out_ref[...] = attended_ref[...]


def round_outputs(gated, attended):
    vmem = pl.BlockSpec(memory_space=pltpu.VMEM)
    return pl.pallas_call(
        round_kernel,
        out_shape=(
            jax.ShapeDtypeStruct(gated.shape, jnp.bfloat16),
            jax.ShapeDtypeStruct(attended.shape, jnp.bfloat16),
        ),
        in_specs=[vmem] * 2,
        out_specs=(vmem, vmem),
    )(gated, attended)


def body(hyena_features, short_filter, long_filter, att_query, att_key):
    gated, attended = fused_call(att_key, hyena_features, short_filter, long_filter, att_query)
    return round_outputs(gated, attended)


def solution(mesh):
    return jax.shard_map(
        body,
        mesh=mesh,
        in_specs=(
            P(None, ("dp", "ctx"), "tp"),
            P(None, None, "tp"),
            P(None, "tp"),
            P(("dp", "ctx"), "tp"),
            P(("dp", "ctx"), "tp"),
        ),
        out_specs=(P(("dp", "ctx"), "tp"), P(("dp", "ctx"), "tp")),
        check_vma=False,
    )
```

```python
import functools
import math

import jax
import jax.numpy as jnp
from jax import lax
from jax.experimental import pallas as pl
from jax.experimental.pallas import tpu as pltpu
from jax.sharding import PartitionSpec as P

MESH = pl.DeviceIdType.MESH

HEAD_DIM = 128
WINDOW_BLOCKS = 4


def fused_kernel(
    count, k_ref, feats_ref, sf_ref, lf_ref, q_ref,
    hm_out, out_ref,
    edge_stage, edge_send, edge_slot, kslots, vslots, vsrc, vstage, raw, qmix, ext, shifted,
    weights, totals, acc, send_sems, recv_sems, copy_sem,
):
    me = lax.axis_index("ctx")
    odd = lax.rem(me, 2) == 1
    even = jnp.logical_not(odd)
    rows, width = k_ref.shape
    taps = lf_ref.shape[0]
    heads = width // HEAD_DIM
    scale = 1.0 / math.sqrt(HEAD_DIM)

    @pl.when(me < 3)
    def _():
        for slot, first in ((0, 3), (1, 2), (2, 1)):
            @pl.when(me < first)
            def _():
                kslots[slot] = jnp.zeros((rows, width), kslots.dtype)
                vslots[slot] = jnp.zeros((rows, width), vslots.dtype)

    @pl.when(me == 0)
    def _():
        edge_slot[...] = jnp.zeros(edge_slot.shape, edge_slot.dtype)

    barrier = pltpu.get_barrier_semaphore()
    for step in (-2, -1, 1, 2):
        peer = me + step

        @pl.when((peer >= 0) & (peer < count))
        def _():
            pl.semaphore_signal(barrier, inc=1, device_id={"ctx": peer}, device_id_type=MESH)

    neighbours = (
        (me >= 2).astype(jnp.int32) + (me >= 1).astype(jnp.int32)
        + (me + 1 < count).astype(jnp.int32) + (me + 2 < count).astype(jnp.int32)
    )
    pl.semaphore_wait(barrier, neighbours)

    def route(slots, src, base_send, base_recv):
        def send(source, slot, peer, sem):
            return pltpu.make_async_remote_copy(
                src_ref=source, dst_ref=slots.at[slot], send_sem=send_sems.at[base_send + sem],
                recv_sem=recv_sems.at[base_recv + slot], device_id={"ctx": peer},
                device_id_type=MESH,
            )

        def incoming(slot):
            return pltpu.make_async_remote_copy(
                src_ref=src, dst_ref=slots.at[slot], send_sem=send_sems.at[base_send],
                recv_sem=recv_sems.at[base_recv + slot], device_id={"ctx": me},
                device_id_type=MESH,
            )

        far = send(src, 1, me + 2, 0)
        near = send(src, 2, me + 1, 1)
        relay_near = send(slots.at[1], 2, me - 1, 2)
        relay_far = send(slots.at[1], 0, me + 1, 3)
        return far, near, relay_near, relay_far, incoming

    def start_first(far, near):
        @pl.when(me + 2 < count)
        def _():
            far.start()

        @pl.when(even)
        def _():
            near.start()

    def start_relay(relay_near, relay_far, incoming):
        @pl.when(me >= 2)
        def _():
            incoming(1).wait_recv()

            @pl.when(odd)
            def _():
                relay_near.start()

            @pl.when(jnp.logical_or(even, me + 1 < count))
            def _():
                relay_far.start()

    def finish_sends(far, near, relay_near, relay_far):
        @pl.when(me + 2 < count)
        def _():
            far.wait_send()

        @pl.when(even)
        def _():
            near.wait_send()

        @pl.when((me >= 2) & odd)
        def _():
            relay_near.wait_send()

        @pl.when((me >= 2) & jnp.logical_or(even, me + 1 < count))
        def _():
            relay_far.wait_send()

    k_far, k_near, k_relay_near, k_relay_far, k_incoming = route(kslots, k_ref, 0, 0)
    start_first(k_far, k_near)

    front = 8
    half = rows // 2
    for which in range(3):
        raw[which, pl.ds(0, front), :] = jnp.zeros((front, width), jnp.float32)
        raw[which, pl.ds(front, rows), :] = feats_ref[which].astype(jnp.float32)

    def mix(which, start, length):
        w = sf_ref[which]
        x = raw.at[which]
        return (
            w[0:1] * x[pl.ds(front + start, length), :]
            + w[1:2] * x[pl.ds(front + start - 1, length), :]
        ) + w[2:3] * x[pl.ds(front + start - 2, length), :]

    edge_stage[pl.ds(0, half), :] = (mix(1, half, half) * mix(2, half, half)).astype(
        edge_stage.dtype
    )
    line = lax.broadcasted_iota(jnp.int32, (16, width), 0)
    packed = jnp.zeros((16, width), jnp.float32)
    for which in range(3):
        last = feats_ref[which, pl.ds(rows - 16, 16), :].astype(jnp.float32)
        for r in range(2):
            packed = jnp.where(line == 2 * which + r, last[14 + r : 15 + r], packed)
    edge_stage[pl.ds(half, 16), :] = packed.astype(edge_stage.dtype)
    staged = pltpu.make_async_copy(edge_stage, edge_send, copy_sem.at[1])
    staged.start()
    staged.wait()

    edge = pltpu.make_async_remote_copy(
        src_ref=edge_send, dst_ref=edge_slot, send_sem=send_sems.at[8],
        recv_sem=recv_sems.at[6], device_id={"ctx": me + 1}, device_id_type=MESH,
    )
    edge_in = pltpu.make_async_remote_copy(
        src_ref=edge_send, dst_ref=edge_slot, send_sem=send_sems.at[8],
        recv_sem=recv_sems.at[6], device_id={"ctx": me}, device_id_type=MESH,
    )

    @pl.when(me + 1 < count)
    def _():
        edge.start()

    @pl.when(me >= 1)
    def _():
        edge_in.wait_recv()

    older = edge_slot[pl.ds(half, 16), :].astype(jnp.float32)
    line = lax.broadcasted_iota(jnp.int32, (front, width), 0)
    for which in range(3):
        tile = jnp.zeros((front, width), jnp.float32)
        for r in range(2):
            tile = jnp.where(line == front - 2 + r, older[2 * which + r : 2 * which + r + 1], tile)
        raw[which, pl.ds(0, front), :] = tile

    qmix[...] = mix(0, 0, rows)
    ext[pl.ds(0, taps), :] = edge_slot[pl.ds(0, taps), :].astype(jnp.float32)
    ext[pl.ds(taps, rows), :] = (mix(1, 0, rows) * mix(2, 0, rows)).astype(
        jnp.bfloat16
    ).astype(jnp.float32)

    def chunk(c, carry):
        cols = pl.ds(pl.multiple_of(c * 128, 128), 128)
        for b in range(8):
            shifted[b, pl.ds(8, rows + taps - 8), :] = ext[pl.ds(8 - b, rows + taps - 8), cols]
        total = jnp.zeros((rows, 128), jnp.float32)
        for a in range(taps // 8):
            for b in range(8):
                j = 8 * a + b
                total = total + lf_ref[pl.ds(j, 1), cols] * shifted[b, pl.ds(taps - 8 * a, rows), :]
        gated = (qmix[:, cols] * total).astype(vsrc.dtype)
        hm_out[:, cols] = gated
        vsrc[:, cols] = gated
        return carry

    chunks = width // 128
    lax.fori_loop(0, chunks // 2, chunk, 0)
    start_relay(k_relay_near, k_relay_far, k_incoming)
    lax.fori_loop(chunks // 2, chunks, chunk, 0)

    local = pltpu.make_async_copy(vsrc, vstage, copy_sem.at[0])
    local.start()
    local.wait()

    v_far, v_near, v_relay_near, v_relay_far, v_incoming = route(vslots, vstage, 4, 3)
    start_first(v_far, v_near)

    @pl.when(me >= 1)
    def _():
        k_incoming(2).wait_recv()

    @pl.when(me >= 3)
    def _():
        k_incoming(0).wait_recv()

    def score_head(h, carry):
        cols = pl.ds(pl.multiple_of(h * HEAD_DIM, HEAD_DIM), HEAD_DIM)
        q = q_ref[:, cols]
        parts = []
        for b, keys in enumerate((kslots.at[0], kslots.at[1], kslots.at[2], k_ref)):
            s = lax.dot_general(
                q, keys[:, cols], (((1,), (1,)), ((), ())), preferred_element_type=jnp.float32
            ) * scale
            t = lax.broadcasted_iota(jnp.int32, (rows, rows), 0)
            u = lax.broadcasted_iota(jnp.int32, (rows, rows), 1)
            if b == 3:
                visible = u <= t
            else:
                visible = jnp.broadcast_to(me - 3 + b >= 0, (rows, rows))
            parts.append(jnp.where(visible, s, -jnp.inf))
        masked = jnp.concatenate(parts, axis=1)
        peak = jnp.max(masked, axis=1, keepdims=True)
        w = jnp.exp(masked - peak)
        totals[h] = jnp.sum(w, axis=1, keepdims=True)
        weights[h] = w.astype(jnp.bfloat16)
        return carry

    lax.fori_loop(0, heads, score_head, 0)

    def accumulate(block, v_src, first):
        def one_head(h, carry):
            cols = pl.ds(pl.multiple_of(h * HEAD_DIM, HEAD_DIM), HEAD_DIM)
            w = weights[h, :, pl.ds(block * rows, rows)]
            part = jnp.dot(w, v_src[:, cols], preferred_element_type=jnp.float32)
            if first:
                acc[:, cols] = part
            else:
                acc[:, cols] = acc[:, cols] + part
            return carry

        lax.fori_loop(0, heads, one_head, 0)

    accumulate(3, vstage, True)
    start_relay(v_relay_near, v_relay_far, v_incoming)
    accumulate(1, vslots.at[1], False)

    @pl.when(me >= 1)
    def _():
        v_incoming(2).wait_recv()

    accumulate(2, vslots.at[2], False)

    @pl.when(me >= 3)
    def _():
        v_incoming(0).wait_recv()

    accumulate(0, vslots.at[0], False)

    def finish(h, carry):
        cols = pl.ds(pl.multiple_of(h * HEAD_DIM, HEAD_DIM), HEAD_DIM)
        out_ref[:, cols] = (acc[:, cols] / totals[h]).astype(out_ref.dtype)
        return carry

    lax.fori_loop(0, heads, finish, 0)

    @pl.when(me + 1 < count)
    def _():
        edge.wait_send()

    finish_sends(k_far, k_near, k_relay_near, k_relay_far)
    finish_sends(v_far, v_near, v_relay_near, v_relay_far)


def fused_call(keys, feats, short_filter, long_filter, query):
    count = lax.axis_size("ctx")
    rows, width = keys.shape
    taps = long_filter.shape[0]
    heads = width // HEAD_DIM
    edge_rows = rows // 2 + 16
    vmem = pl.BlockSpec(memory_space=pltpu.VMEM)
    return pl.pallas_call(
        functools.partial(fused_kernel, count),
        out_shape=(
            jax.ShapeDtypeStruct((rows, width), jnp.bfloat16),
            jax.ShapeDtypeStruct((rows, width), jnp.bfloat16),
        ),
        in_specs=[vmem] * 5,
        out_specs=(vmem, vmem),
        scratch_shapes=[
            pltpu.VMEM((edge_rows, width), jnp.bfloat16),
            pltpu.VMEM((edge_rows, width), jnp.bfloat16),
            pltpu.VMEM((edge_rows, width), jnp.bfloat16),
            pltpu.VMEM((3, rows, width), keys.dtype),
            pltpu.VMEM((3, rows, width), jnp.bfloat16),
            pltpu.VMEM((rows, width), jnp.bfloat16),
            pltpu.VMEM((rows, width), jnp.bfloat16),
            pltpu.VMEM((3, rows + 8, width), jnp.float32),
            pltpu.VMEM((rows, width), jnp.float32),
            pltpu.VMEM((rows + taps, width), jnp.float32),
            pltpu.VMEM((8, rows + taps, 128), jnp.float32),
            pltpu.VMEM((heads, rows, WINDOW_BLOCKS * rows), jnp.bfloat16),
            pltpu.VMEM((heads, rows, 1), jnp.float32),
            pltpu.VMEM((rows, width), jnp.float32),
            pltpu.SemaphoreType.DMA((9,)),
            pltpu.SemaphoreType.DMA((7,)),
            pltpu.SemaphoreType.DMA((2,)),
        ],
        compiler_params=pltpu.CompilerParams(
            collective_id=0, has_side_effects=True, vmem_limit_bytes=60 * 1024 * 1024
        ),
    )(keys, feats, short_filter, long_filter, query)


def round_kernel(gated_ref, attended_ref, hm_out, out_ref):
    hm_out[...] = gated_ref[...]
    out_ref[...] = attended_ref[...]


def round_outputs(gated, attended):
    vmem = pl.BlockSpec(memory_space=pltpu.VMEM)
    return pl.pallas_call(
        round_kernel,
        out_shape=(
            jax.ShapeDtypeStruct(gated.shape, jnp.bfloat16),
            jax.ShapeDtypeStruct(attended.shape, jnp.bfloat16),
        ),
        in_specs=[vmem] * 2,
        out_specs=(vmem, vmem),
    )(gated, attended)


def body(hyena_features, short_filter, long_filter, att_query, att_key):
    gated, attended = fused_call(att_key, hyena_features, short_filter, long_filter, att_query)
    return round_outputs(gated, attended)


def solution(mesh):
    return jax.shard_map(
        body,
        mesh=mesh,
        in_specs=(
            P(None, ("dp", "ctx"), "tp"),
            P(None, None, "tp"),
            P(None, "tp"),
            P(("dp", "ctx"), "tp"),
            P(("dp", "ctx"), "tp"),
        ),
        out_specs=(P(("dp", "ctx"), "tp"), P(("dp", "ctx"), "tp")),
        check_vma=False,
    )
```

```python
import functools
import math

import jax
import jax.numpy as jnp
from jax import lax
from jax.experimental import pallas as pl
from jax.experimental.pallas import tpu as pltpu
from jax.sharding import PartitionSpec as P

MESH = pl.DeviceIdType.MESH

HEAD_DIM = 128
WINDOW_BLOCKS = 4


def fused_kernel(
    count, k_ref, feats_ref, sf_ref, lf_ref, q_ref,
    hm_out, out_ref,
    edge_stage, edge_send, edge_slot, kslots, vslots, vsrc, vstage, raw, qmix, ext, shifted,
    weights, totals, acc, send_sems, recv_sems, copy_sem,
):
    me = lax.axis_index("ctx")
    odd = lax.rem(me, 2) == 1
    even = jnp.logical_not(odd)
    rows, width = k_ref.shape
    taps = lf_ref.shape[0]
    heads = width // HEAD_DIM
    scale = 1.0 / math.sqrt(HEAD_DIM)

    @pl.when(me < 3)
    def _():
        for slot, first in ((0, 3), (1, 2), (2, 1)):
            @pl.when(me < first)
            def _():
                kslots[slot] = jnp.zeros((rows, width), kslots.dtype)
                vslots[slot] = jnp.zeros((rows, width), vslots.dtype)

    @pl.when(me == 0)
    def _():
        edge_slot[...] = jnp.zeros(edge_slot.shape, edge_slot.dtype)

    barrier = pltpu.get_barrier_semaphore()
    for step in (-2, -1, 1, 2):
        peer = me + step

        @pl.when((peer >= 0) & (peer < count))
        def _():
            pl.semaphore_signal(barrier, inc=1, device_id={"ctx": peer}, device_id_type=MESH)

    neighbours = (
        (me >= 2).astype(jnp.int32) + (me >= 1).astype(jnp.int32)
        + (me + 1 < count).astype(jnp.int32) + (me + 2 < count).astype(jnp.int32)
    )
    pl.semaphore_wait(barrier, neighbours)

    def route(slots, src, base_send, base_recv):
        def send(source, slot, peer, sem):
            return pltpu.make_async_remote_copy(
                src_ref=source, dst_ref=slots.at[slot], send_sem=send_sems.at[base_send + sem],
                recv_sem=recv_sems.at[base_recv + slot], device_id={"ctx": peer},
                device_id_type=MESH,
            )

        def incoming(slot):
            return pltpu.make_async_remote_copy(
                src_ref=src, dst_ref=slots.at[slot], send_sem=send_sems.at[base_send],
                recv_sem=recv_sems.at[base_recv + slot], device_id={"ctx": me},
                device_id_type=MESH,
            )

        far = send(src, 1, me + 2, 0)
        near = send(src, 2, me + 1, 1)
        relay_near = send(slots.at[1], 2, me - 1, 2)
        relay_far = send(slots.at[1], 0, me + 1, 3)
        return far, near, relay_near, relay_far, incoming

    def start_first(far, near):
        @pl.when(me + 2 < count)
        def _():
            far.start()

        @pl.when(even)
        def _():
            near.start()

    def start_relay(relay_near, relay_far, incoming):
        @pl.when(me >= 2)
        def _():
            incoming(1).wait_recv()

            @pl.when(odd)
            def _():
                relay_near.start()

            @pl.when(jnp.logical_or(even, me + 1 < count))
            def _():
                relay_far.start()

    def finish_sends(far, near, relay_near, relay_far):
        @pl.when(me + 2 < count)
        def _():
            far.wait_send()

        @pl.when(even)
        def _():
            near.wait_send()

        @pl.when((me >= 2) & odd)
        def _():
            relay_near.wait_send()

        @pl.when((me >= 2) & jnp.logical_or(even, me + 1 < count))
        def _():
            relay_far.wait_send()

    front = 8
    half = rows // 2
    for which in range(3):
        raw[which, pl.ds(0, front), :] = jnp.zeros((front, width), jnp.float32)
        raw[which, pl.ds(front, rows), :] = feats_ref[which].astype(jnp.float32)

    def mix(which, start, length):
        w = sf_ref[which]
        x = raw.at[which]
        return (
            w[0:1] * x[pl.ds(front + start, length), :]
            + w[1:2] * x[pl.ds(front + start - 1, length), :]
        ) + w[2:3] * x[pl.ds(front + start - 2, length), :]

    edge_stage[pl.ds(0, half), :] = (mix(1, half, half) * mix(2, half, half)).astype(
        edge_stage.dtype
    )
    line = lax.broadcasted_iota(jnp.int32, (16, width), 0)
    packed = jnp.zeros((16, width), jnp.float32)
    for which in range(3):
        last = feats_ref[which, pl.ds(rows - 16, 16), :].astype(jnp.float32)
        for r in range(2):
            packed = jnp.where(line == 2 * which + r, last[14 + r : 15 + r], packed)
    edge_stage[pl.ds(half, 16), :] = packed.astype(edge_stage.dtype)
    staged = pltpu.make_async_copy(edge_stage, edge_send, copy_sem.at[1])
    staged.start()
    staged.wait()

    edge = pltpu.make_async_remote_copy(
        src_ref=edge_send, dst_ref=edge_slot, send_sem=send_sems.at[8],
        recv_sem=recv_sems.at[6], device_id={"ctx": me + 1}, device_id_type=MESH,
    )
    edge_in = pltpu.make_async_remote_copy(
        src_ref=edge_send, dst_ref=edge_slot, send_sem=send_sems.at[8],
        recv_sem=recv_sems.at[6], device_id={"ctx": me}, device_id_type=MESH,
    )

    @pl.when(me + 1 < count)
    def _():
        edge.start()

    k_far, k_near, k_relay_near, k_relay_far, k_incoming = route(kslots, k_ref, 0, 0)
    start_first(k_far, k_near)

    @pl.when(me >= 1)
    def _():
        edge_in.wait_recv()

    older = edge_slot[pl.ds(half, 16), :].astype(jnp.float32)
    line = lax.broadcasted_iota(jnp.int32, (front, width), 0)
    for which in range(3):
        tile = jnp.zeros((front, width), jnp.float32)
        for r in range(2):
            tile = jnp.where(line == front - 2 + r, older[2 * which + r : 2 * which + r + 1], tile)
        raw[which, pl.ds(0, front), :] = tile

    qmix[...] = mix(0, 0, rows)
    ext[pl.ds(0, taps), :] = edge_slot[pl.ds(0, taps), :].astype(jnp.float32)
    ext[pl.ds(taps, rows), :] = (mix(1, 0, rows) * mix(2, 0, rows)).astype(
        jnp.bfloat16
    ).astype(jnp.float32)

    def chunk(c, carry):
        cols = pl.ds(pl.multiple_of(c * 128, 128), 128)
        for b in range(8):
            shifted[b, pl.ds(8, rows + taps - 8), :] = ext[pl.ds(8 - b, rows + taps - 8), cols]
        total = jnp.zeros((rows, 128), jnp.float32)
        for a in range(taps // 8):
            for b in range(8):
                j = 8 * a + b
                total = total + lf_ref[pl.ds(j, 1), cols] * shifted[b, pl.ds(taps - 8 * a, rows), :]
        gated = (qmix[:, cols] * total).astype(vsrc.dtype)
        hm_out[:, cols] = gated
        vsrc[:, cols] = gated
        local = pltpu.make_async_copy(vsrc.at[:, cols], vstage.at[:, cols], copy_sem.at[0])
        local.start()
        local.wait()

        @pl.when(me + 2 < count)
        def _():
            pltpu.make_async_remote_copy(
                src_ref=vstage.at[:, cols], dst_ref=vslots.at[1, :, cols],
                send_sem=send_sems.at[4], recv_sem=recv_sems.at[4], device_id={"ctx": me + 2},
                device_id_type=MESH,
            ).start()

        @pl.when(even)
        def _():
            pltpu.make_async_remote_copy(
                src_ref=vstage.at[:, cols], dst_ref=vslots.at[2, :, cols],
                send_sem=send_sems.at[5], recv_sem=recv_sems.at[5], device_id={"ctx": me + 1},
                device_id_type=MESH,
            ).start()

        return carry

    v_far, v_near, v_relay_near, v_relay_far, v_incoming = route(vslots, vstage, 4, 3)
    lax.fori_loop(0, width // 128, chunk, 0)

    start_relay(k_relay_near, k_relay_far, k_incoming)

    @pl.when(me >= 1)
    def _():
        k_incoming(2).wait_recv()

    @pl.when(me >= 3)
    def _():
        k_incoming(0).wait_recv()

    def score_head(h, carry):
        cols = pl.ds(pl.multiple_of(h * HEAD_DIM, HEAD_DIM), HEAD_DIM)
        q = q_ref[:, cols]
        parts = []
        for b, keys in enumerate((kslots.at[0], kslots.at[1], kslots.at[2], k_ref)):
            s = lax.dot_general(
                q, keys[:, cols], (((1,), (1,)), ((), ())), preferred_element_type=jnp.float32
            ) * scale
            t = lax.broadcasted_iota(jnp.int32, (rows, rows), 0)
            u = lax.broadcasted_iota(jnp.int32, (rows, rows), 1)
            if b == 3:
                visible = u <= t
            else:
                visible = jnp.broadcast_to(me - 3 + b >= 0, (rows, rows))
            parts.append(jnp.where(visible, s, -jnp.inf))
        masked = jnp.concatenate(parts, axis=1)
        peak = jnp.max(masked, axis=1, keepdims=True)
        w = jnp.exp(masked - peak)
        totals[h] = jnp.sum(w, axis=1, keepdims=True)
        weights[h] = w.astype(jnp.bfloat16)
        return carry

    lax.fori_loop(0, heads, score_head, 0)

    def accumulate(block, v_src, first):
        def one_head(h, carry):
            cols = pl.ds(pl.multiple_of(h * HEAD_DIM, HEAD_DIM), HEAD_DIM)
            w = weights[h, :, pl.ds(block * rows, rows)]
            part = jnp.dot(w, v_src[:, cols], preferred_element_type=jnp.float32)
            if first:
                acc[:, cols] = part
            else:
                acc[:, cols] = acc[:, cols] + part
            return carry

        lax.fori_loop(0, heads, one_head, 0)

    accumulate(3, vstage, True)
    start_relay(v_relay_near, v_relay_far, v_incoming)
    accumulate(1, vslots.at[1], False)

    @pl.when(me >= 1)
    def _():
        v_incoming(2).wait_recv()

    accumulate(2, vslots.at[2], False)

    @pl.when(me >= 3)
    def _():
        v_incoming(0).wait_recv()

    accumulate(0, vslots.at[0], False)

    def finish(h, carry):
        cols = pl.ds(pl.multiple_of(h * HEAD_DIM, HEAD_DIM), HEAD_DIM)
        out_ref[:, cols] = (acc[:, cols] / totals[h]).astype(out_ref.dtype)
        return carry

    lax.fori_loop(0, heads, finish, 0)

    @pl.when(me + 1 < count)
    def _():
        edge.wait_send()

    finish_sends(k_far, k_near, k_relay_near, k_relay_far)
    finish_sends(v_far, v_near, v_relay_near, v_relay_far)


def fused_call(keys, feats, short_filter, long_filter, query):
    count = lax.axis_size("ctx")
    rows, width = keys.shape
    taps = long_filter.shape[0]
    heads = width // HEAD_DIM
    edge_rows = rows // 2 + 16
    vmem = pl.BlockSpec(memory_space=pltpu.VMEM)
    return pl.pallas_call(
        functools.partial(fused_kernel, count),
        out_shape=(
            jax.ShapeDtypeStruct((rows, width), jnp.bfloat16),
            jax.ShapeDtypeStruct((rows, width), jnp.bfloat16),
        ),
        in_specs=[vmem] * 5,
        out_specs=(vmem, vmem),
        scratch_shapes=[
            pltpu.VMEM((edge_rows, width), jnp.bfloat16),
            pltpu.VMEM((edge_rows, width), jnp.bfloat16),
            pltpu.VMEM((edge_rows, width), jnp.bfloat16),
            pltpu.VMEM((3, rows, width), keys.dtype),
            pltpu.VMEM((3, rows, width), jnp.bfloat16),
            pltpu.VMEM((rows, width), jnp.bfloat16),
            pltpu.VMEM((rows, width), jnp.bfloat16),
            pltpu.VMEM((3, rows + 8, width), jnp.float32),
            pltpu.VMEM((rows, width), jnp.float32),
            pltpu.VMEM((rows + taps, width), jnp.float32),
            pltpu.VMEM((8, rows + taps, 128), jnp.float32),
            pltpu.VMEM((heads, rows, WINDOW_BLOCKS * rows), jnp.bfloat16),
            pltpu.VMEM((heads, rows, 1), jnp.float32),
            pltpu.VMEM((rows, width), jnp.float32),
            pltpu.SemaphoreType.DMA((9,)),
            pltpu.SemaphoreType.DMA((7,)),
            pltpu.SemaphoreType.DMA((2,)),
        ],
        compiler_params=pltpu.CompilerParams(
            collective_id=0, has_side_effects=True, vmem_limit_bytes=60 * 1024 * 1024
        ),
    )(keys, feats, short_filter, long_filter, query)


def round_kernel(gated_ref, attended_ref, hm_out, out_ref):
    hm_out[...] = gated_ref[...]
    out_ref[...] = attended_ref[...]


def round_outputs(gated, attended):
    vmem = pl.BlockSpec(memory_space=pltpu.VMEM)
    return pl.pallas_call(
        round_kernel,
        out_shape=(
            jax.ShapeDtypeStruct(gated.shape, jnp.bfloat16),
            jax.ShapeDtypeStruct(attended.shape, jnp.bfloat16),
        ),
        in_specs=[vmem] * 2,
        out_specs=(vmem, vmem),
    )(gated, attended)


def body(hyena_features, short_filter, long_filter, att_query, att_key):
    gated, attended = fused_call(att_key, hyena_features, short_filter, long_filter, att_query)
    return round_outputs(gated, attended)


def solution(mesh):
    return jax.shard_map(
        body,
        mesh=mesh,
        in_specs=(
            P(None, ("dp", "ctx"), "tp"),
            P(None, None, "tp"),
            P(None, "tp"),
            P(("dp", "ctx"), "tp"),
            P(("dp", "ctx"), "tp"),
        ),
        out_specs=(P(("dp", "ctx"), "tp"), P(("dp", "ctx"), "tp")),
        check_vma=False,
    )
```

```python
import functools
import math

import jax
import jax.numpy as jnp
from jax import lax
from jax.experimental import pallas as pl
from jax.experimental.pallas import tpu as pltpu
from jax.sharding import PartitionSpec as P

MESH = pl.DeviceIdType.MESH

HEAD_DIM = 128
WINDOW_BLOCKS = 4


def fused_kernel(
    count, k_ref, feats_ref, sf_ref, lf_ref, q_ref,
    hm_out, out_ref,
    edge_stage, edge_send, edge_slot, kslots, vslots, vsrc, vstage, raw, qmix, ext, shifted,
    weights, totals, acc, peaks, qslot, pbuf, psend, pslot, sbuf, ssend, sslot,
    send_sems, recv_sems, copy_sem,
):
    me = lax.axis_index("ctx")
    odd = lax.rem(me, 2) == 1
    even = jnp.logical_not(odd)
    asks = even & (me >= 4)
    answers = odd & (me >= 3) & (me + 1 < count)
    rows, width = k_ref.shape
    taps = lf_ref.shape[0]
    heads = width // HEAD_DIM
    scale = 1.0 / math.sqrt(HEAD_DIM)

    @pl.when(me < 3)
    def _():
        for slot, first in ((0, 3), (1, 2), (2, 1)):
            @pl.when(me < first)
            def _():
                kslots[slot] = jnp.zeros((rows, width), kslots.dtype)
                vslots[slot] = jnp.zeros((rows, width), vslots.dtype)

    @pl.when(me == 0)
    def _():
        edge_slot[...] = jnp.zeros(edge_slot.shape, edge_slot.dtype)

    @pl.when(asks)
    def _():
        kslots[0] = jnp.zeros((rows, width), kslots.dtype)
        vslots[0] = jnp.zeros((rows, width), vslots.dtype)

    barrier = pltpu.get_barrier_semaphore()
    for step in (-2, -1, 1, 2):
        peer = me + step

        @pl.when((peer >= 0) & (peer < count))
        def _():
            pl.semaphore_signal(barrier, inc=1, device_id={"ctx": peer}, device_id_type=MESH)

    neighbours = (
        (me >= 2).astype(jnp.int32) + (me >= 1).astype(jnp.int32)
        + (me + 1 < count).astype(jnp.int32) + (me + 2 < count).astype(jnp.int32)
    )
    pl.semaphore_wait(barrier, neighbours)

    def route(slots, src, base_send, base_recv):
        def send(source, slot, peer, sem):
            return pltpu.make_async_remote_copy(
                src_ref=source, dst_ref=slots.at[slot], send_sem=send_sems.at[base_send + sem],
                recv_sem=recv_sems.at[base_recv + slot], device_id={"ctx": peer},
                device_id_type=MESH,
            )

        def incoming(slot):
            return pltpu.make_async_remote_copy(
                src_ref=src, dst_ref=slots.at[slot], send_sem=send_sems.at[base_send],
                recv_sem=recv_sems.at[base_recv + slot], device_id={"ctx": me},
                device_id_type=MESH,
            )

        far = send(src, 1, me + 2, 0)
        near = send(src, 2, me + 1, 1)
        relay_near = send(slots.at[1], 2, me - 1, 2)
        relay_far = send(slots.at[1], 0, me + 1, 3)
        return far, near, relay_near, relay_far, incoming

    def start_first(far, near):
        @pl.when(me + 2 < count)
        def _():
            far.start()

        @pl.when(even)
        def _():
            near.start()

    def start_relay(relay_near, relay_far, incoming):
        @pl.when(me >= 2)
        def _():
            incoming(1).wait_recv()

            @pl.when(odd)
            def _():
                relay_near.start()

            @pl.when(even)
            def _():
                relay_far.start()

    def finish_sends(far, near, relay_near, relay_far):
        @pl.when(me + 2 < count)
        def _():
            far.wait_send()

        @pl.when(even)
        def _():
            near.wait_send()

        @pl.when((me >= 2) & odd)
        def _():
            relay_near.wait_send()

        @pl.when((me >= 2) & even)
        def _():
            relay_far.wait_send()

    front = 8
    half = rows // 2
    for which in range(3):
        raw[which, pl.ds(0, front), :] = jnp.zeros((front, width), jnp.float32)
        raw[which, pl.ds(front, rows), :] = feats_ref[which].astype(jnp.float32)

    def mix(which, start, length):
        w = sf_ref[which]
        x = raw.at[which]
        return (
            w[0:1] * x[pl.ds(front + start, length), :]
            + w[1:2] * x[pl.ds(front + start - 1, length), :]
        ) + w[2:3] * x[pl.ds(front + start - 2, length), :]

    edge_stage[pl.ds(0, half), :] = (mix(1, half, half) * mix(2, half, half)).astype(
        edge_stage.dtype
    )
    for which in range(3):
        edge_stage[pl.ds(half + 16 * which, 16), :] = feats_ref[which, pl.ds(rows - 16, 16), :]
    staged = pltpu.make_async_copy(edge_stage, edge_send, copy_sem.at[1])
    staged.start()
    staged.wait()

    edge = pltpu.make_async_remote_copy(
        src_ref=edge_send, dst_ref=edge_slot, send_sem=send_sems.at[8],
        recv_sem=recv_sems.at[6], device_id={"ctx": me + 1}, device_id_type=MESH,
    )
    edge_in = pltpu.make_async_remote_copy(
        src_ref=edge_send, dst_ref=edge_slot, send_sem=send_sems.at[8],
        recv_sem=recv_sems.at[6], device_id={"ctx": me}, device_id_type=MESH,
    )

    @pl.when(me + 1 < count)
    def _():
        edge.start()

    k_far, k_near, k_relay_near, k_relay_far, k_incoming = route(kslots, k_ref, 0, 0)
    start_first(k_far, k_near)

    def remote(src, dst, send, recv, peer):
        return pltpu.make_async_remote_copy(
            src_ref=src, dst_ref=dst, send_sem=send_sems.at[send], recv_sem=recv_sems.at[recv],
            device_id={"ctx": peer}, device_id_type=MESH,
        )

    q_out = remote(q_ref, qslot, 9, 7, me - 1)
    q_in = remote(q_ref, qslot, 9, 7, me)
    p_out = remote(psend, pslot, 10, 8, me + 1)
    p_in = remote(psend, pslot, 10, 8, me)
    s_out = remote(ssend, sslot, 11, 9, me + 1)
    s_in = remote(ssend, sslot, 11, 9, me)

    @pl.when(asks)
    def _():
        q_out.start()

    @pl.when(me >= 1)
    def _():
        edge_in.wait_recv()

    for which in range(3):
        older = edge_slot[pl.ds(half + 16 * which, 16), :].astype(jnp.float32)
        raw[which, pl.ds(0, front), :] = older[16 - front :]

    qmix[...] = mix(0, 0, rows)
    ext[pl.ds(0, taps), :] = edge_slot[pl.ds(0, taps), :].astype(jnp.float32)
    ext[pl.ds(taps, rows), :] = (mix(1, 0, rows) * mix(2, 0, rows)).astype(
        jnp.bfloat16
    ).astype(jnp.float32)

    def chunk(c, carry):
        cols = pl.ds(pl.multiple_of(c * 128, 128), 128)
        for b in range(8):
            shifted[b, pl.ds(8, rows + taps - 8), :] = ext[pl.ds(8 - b, rows + taps - 8), cols]
        total = jnp.zeros((rows, 128), jnp.float32)
        for a in range(taps // 8):
            for b in range(8):
                j = 8 * a + b
                total = total + lf_ref[pl.ds(j, 1), cols] * shifted[b, pl.ds(taps - 8 * a, rows), :]
        gated = qmix[:, cols] * total
        hm_out[:, cols] = gated
        vsrc[:, cols] = gated.astype(vsrc.dtype)
        return carry

    lax.fori_loop(0, width // 128, chunk, 0)

    local = pltpu.make_async_copy(vsrc, vstage, copy_sem.at[0])
    local.start()
    local.wait()

    v_far, v_near, v_relay_near, v_relay_far, v_incoming = route(vslots, vstage, 4, 3)
    start_first(v_far, v_near)
    start_relay(k_relay_near, k_relay_far, k_incoming)

    @pl.when(me >= 1)
    def _():
        k_incoming(2).wait_recv()

    @pl.when((me >= 3) & odd)
    def _():
        k_incoming(0).wait_recv()

    def score_head(h, carry):
        cols = pl.ds(pl.multiple_of(h * HEAD_DIM, HEAD_DIM), HEAD_DIM)
        q = q_ref[:, cols]
        parts = []
        for b, keys in enumerate((kslots.at[0], kslots.at[1], kslots.at[2], k_ref)):
            s = lax.dot_general(
                q, keys[:, cols], (((1,), (1,)), ((), ())), preferred_element_type=jnp.float32
            ) * scale
            t = lax.broadcasted_iota(jnp.int32, (rows, rows), 0)
            u = lax.broadcasted_iota(jnp.int32, (rows, rows), 1)
            if b == 3:
                visible = u <= t
            else:
                seen = me - 3 + b >= 0
                if b == 0:
                    seen = seen & jnp.logical_not(asks)
                visible = jnp.broadcast_to(seen, (rows, rows))
            parts.append(jnp.where(visible, s, -jnp.inf))
        masked = jnp.concatenate(parts, axis=1)
        peak = jnp.max(masked, axis=1, keepdims=True)
        w = jnp.exp(masked - peak)
        totals[h] = jnp.sum(w, axis=1, keepdims=True)
        peaks[h] = peak
        weights[h] = w.astype(jnp.bfloat16)
        return carry

    lax.fori_loop(0, heads, score_head, 0)

    def accumulate(block, v_src, first):
        def one_head(h, carry):
            cols = pl.ds(pl.multiple_of(h * HEAD_DIM, HEAD_DIM), HEAD_DIM)
            w = weights[h, :, pl.ds(block * rows, rows)]
            part = jnp.dot(w, v_src[:, cols], preferred_element_type=jnp.float32)
            if first:
                acc[:, cols] = part
            else:
                acc[:, cols] = acc[:, cols] + part
            return carry

        lax.fori_loop(0, heads, one_head, 0)

    accumulate(3, vstage, True)
    start_relay(v_relay_near, v_relay_far, v_incoming)

    @pl.when(answers)
    def _():
        q_in.wait_recv()
        lane = lax.broadcasted_iota(jnp.int32, (rows, 128), 1)
        sbuf[...] = jnp.zeros((rows, 128), jnp.float32)

        def partial_head(h, carry):
            cols = pl.ds(pl.multiple_of(h * HEAD_DIM, HEAD_DIM), HEAD_DIM)
            s = lax.dot_general(
                qslot[:, cols], kslots[1, :, cols], (((1,), (1,)), ((), ())),
                preferred_element_type=jnp.float32,
            ) * scale
            top = jnp.max(s, axis=1, keepdims=True)
            w = jnp.exp(s - top)
            part = jnp.dot(
                w.astype(jnp.bfloat16), vslots[1, :, cols], preferred_element_type=jnp.float32
            )
            pbuf[:, cols] = part.astype(pbuf.dtype)
            stats = jnp.where(lane == h, top, sbuf[...])
            sbuf[...] = jnp.where(lane == heads + h, jnp.sum(w, axis=1, keepdims=True), stats)
            return carry

        lax.fori_loop(0, heads, partial_head, 0)
        staged_p = pltpu.make_async_copy(pbuf, psend, copy_sem.at[0])
        staged_s = pltpu.make_async_copy(sbuf, ssend, copy_sem.at[1])
        staged_p.start()
        staged_s.start()
        staged_p.wait()
        staged_s.wait()
        p_out.start()
        s_out.start()
    accumulate(1, vslots.at[1], False)

    @pl.when(me >= 1)
    def _():
        v_incoming(2).wait_recv()

    accumulate(2, vslots.at[2], False)

    @pl.when((me >= 3) & odd)
    def _():
        v_incoming(0).wait_recv()

    accumulate(0, vslots.at[0], False)

    def finish(h, carry):
        cols = pl.ds(pl.multiple_of(h * HEAD_DIM, HEAD_DIM), HEAD_DIM)
        out_ref[:, cols] = acc[:, cols] / totals[h]
        return carry

    @pl.when(jnp.logical_not(asks))
    def _():
        lax.fori_loop(0, heads, finish, 0)

    @pl.when(asks)
    def _():
        p_in.wait_recv()
        s_in.wait_recv()
        lane = lax.broadcasted_iota(jnp.int32, (rows, 128), 1)

        def combine(h, carry):
            cols = pl.ds(pl.multiple_of(h * HEAD_DIM, HEAD_DIM), HEAD_DIM)
            stats = sslot[...]
            top = jnp.max(jnp.where(lane == h, stats, -jnp.inf), axis=1, keepdims=True)
            rest = jnp.sum(jnp.where(lane == heads + h, stats, 0.0), axis=1, keepdims=True)
            mine = peaks[h]
            both = jnp.maximum(mine, top)
            a = jnp.exp(mine - both)
            b = jnp.exp(top - both)
            out_ref[:, cols] = (acc[:, cols] * a + pslot[:, cols].astype(jnp.float32) * b) / (
                totals[h] * a + rest * b
            )
            return carry

        lax.fori_loop(0, heads, combine, 0)

    @pl.when(asks)
    def _():
        q_out.wait_send()

    @pl.when(answers)
    def _():
        p_out.wait_send()
        s_out.wait_send()

    @pl.when(me + 1 < count)
    def _():
        edge.wait_send()

    finish_sends(k_far, k_near, k_relay_near, k_relay_far)
    finish_sends(v_far, v_near, v_relay_near, v_relay_far)


def fused_call(keys, feats, short_filter, long_filter, query):
    count = lax.axis_size("ctx")
    rows, width = keys.shape
    taps = long_filter.shape[0]
    heads = width // HEAD_DIM
    edge_rows = rows // 2 + 48
    vmem = pl.BlockSpec(memory_space=pltpu.VMEM)
    return pl.pallas_call(
        functools.partial(fused_kernel, count),
        out_shape=(
            jax.ShapeDtypeStruct((rows, width), jnp.float32),
            jax.ShapeDtypeStruct((rows, width), jnp.float32),
        ),
        in_specs=[vmem] * 5,
        out_specs=(vmem, vmem),
        scratch_shapes=[
            pltpu.VMEM((edge_rows, width), jnp.bfloat16),
            pltpu.VMEM((edge_rows, width), jnp.bfloat16),
            pltpu.VMEM((edge_rows, width), jnp.bfloat16),
            pltpu.VMEM((3, rows, width), keys.dtype),
            pltpu.VMEM((3, rows, width), jnp.bfloat16),
            pltpu.VMEM((rows, width), jnp.bfloat16),
            pltpu.VMEM((rows, width), jnp.bfloat16),
            pltpu.VMEM((3, rows + 8, width), jnp.float32),
            pltpu.VMEM((rows, width), jnp.float32),
            pltpu.VMEM((rows + taps, width), jnp.float32),
            pltpu.VMEM((8, rows + taps, 128), jnp.float32),
            pltpu.VMEM((heads, rows, WINDOW_BLOCKS * rows), jnp.bfloat16),
            pltpu.VMEM((heads, rows, 1), jnp.float32),
            pltpu.VMEM((rows, width), jnp.float32),
            pltpu.VMEM((heads, rows, 1), jnp.float32),
            pltpu.VMEM((rows, width), jnp.bfloat16),
            pltpu.VMEM((rows, width), jnp.bfloat16),
            pltpu.VMEM((rows, width), jnp.bfloat16),
            pltpu.VMEM((rows, width), jnp.bfloat16),
            pltpu.VMEM((rows, 128), jnp.float32),
            pltpu.VMEM((rows, 128), jnp.float32),
            pltpu.VMEM((rows, 128), jnp.float32),
            pltpu.SemaphoreType.DMA((12,)),
            pltpu.SemaphoreType.DMA((10,)),
            pltpu.SemaphoreType.DMA((2,)),
        ],
        compiler_params=pltpu.CompilerParams(
            collective_id=0, has_side_effects=True, vmem_limit_bytes=60 * 1024 * 1024
        ),
    )(keys, feats, short_filter, long_filter, query)


def round_kernel(gated_ref, attended_ref, hm_out, out_ref):
    hm_out[...] = gated_ref[...].astype(hm_out.dtype)
    out_ref[...] = attended_ref[...].astype(out_ref.dtype)


def round_outputs(gated, attended):
    vmem = pl.BlockSpec(memory_space=pltpu.VMEM)
    return pl.pallas_call(
        round_kernel,
        out_shape=(
            jax.ShapeDtypeStruct(gated.shape, jnp.bfloat16),
            jax.ShapeDtypeStruct(attended.shape, jnp.bfloat16),
        ),
        in_specs=[vmem] * 2,
        out_specs=(vmem, vmem),
    )(gated, attended)


def body(hyena_features, short_filter, long_filter, att_query, att_key):
    gated, attended = fused_call(att_key, hyena_features, short_filter, long_filter, att_query)
    return round_outputs(gated, attended)


def solution(mesh):
    return jax.shard_map(
        body,
        mesh=mesh,
        in_specs=(
            P(None, ("dp", "ctx"), "tp"),
            P(None, None, "tp"),
            P(None, "tp"),
            P(("dp", "ctx"), "tp"),
            P(("dp", "ctx"), "tp"),
        ),
        out_specs=(P(("dp", "ctx"), "tp"), P(("dp", "ctx"), "tp")),
        check_vma=False,
    )
```

```python
import functools
import math

import jax
import jax.numpy as jnp
from jax import lax
from jax.experimental import pallas as pl
from jax.experimental.pallas import tpu as pltpu
from jax.sharding import PartitionSpec as P

MESH = pl.DeviceIdType.MESH

HEAD_DIM = 128
WINDOW_BLOCKS = 4


def fused_kernel(
    count, k_ref, feats_ref, sf_ref, lf_ref, q_ref,
    hm_out, out_ref,
    edge_stage, edge_send, edge_slot, kslots, vslots, vsrc, vstage, raw, qmix, ext, shifted,
    weights, totals, acc, send_sems, recv_sems, copy_sem,
):
    me = lax.axis_index("ctx")
    odd = lax.rem(me, 2) == 1
    even = jnp.logical_not(odd)
    rows, width = k_ref.shape
    taps = lf_ref.shape[0]
    heads = width // HEAD_DIM
    scale = 1.0 / math.sqrt(HEAD_DIM)

    @pl.when(me < 3)
    def _():
        for slot, first in ((0, 3), (1, 2), (2, 1)):
            @pl.when(me < first)
            def _():
                kslots[slot] = jnp.zeros((rows, width), kslots.dtype)
                vslots[slot] = jnp.zeros((rows, width), vslots.dtype)

    @pl.when(me == 0)
    def _():
        edge_slot[...] = jnp.zeros(edge_slot.shape, edge_slot.dtype)

    barrier = pltpu.get_barrier_semaphore()
    for step in (-2, -1, 1, 2):
        peer = me + step

        @pl.when((peer >= 0) & (peer < count))
        def _():
            pl.semaphore_signal(barrier, inc=1, device_id={"ctx": peer}, device_id_type=MESH)

    neighbours = (
        (me >= 2).astype(jnp.int32) + (me >= 1).astype(jnp.int32)
        + (me + 1 < count).astype(jnp.int32) + (me + 2 < count).astype(jnp.int32)
    )
    pl.semaphore_wait(barrier, neighbours)

    def route(slots, src, base_send, base_recv, second):
        def send(source, slot, peer, sem):
            return pltpu.make_async_remote_copy(
                src_ref=source, dst_ref=slots.at[slot], send_sem=send_sems.at[base_send + sem],
                recv_sem=recv_sems.at[base_recv + slot], device_id={"ctx": peer},
                device_id_type=MESH,
            )

        def incoming(slot):
            return pltpu.make_async_remote_copy(
                src_ref=src, dst_ref=slots.at[slot], send_sem=send_sems.at[base_send],
                recv_sem=recv_sems.at[base_recv + slot], device_id={"ctx": me},
                device_id_type=MESH,
            )

        half = rows // 2

        def piece(source, target, send_index, recv_index, peer, start):
            return pltpu.make_async_remote_copy(
                src_ref=source.at[pl.ds(start, half)], dst_ref=target.at[pl.ds(start, half)],
                send_sem=send_sems.at[send_index], recv_sem=recv_sems.at[recv_index],
                device_id={"ctx": peer}, device_id_type=MESH,
            )

        far = send(src, 1, me + 2, 0)
        far_parts = [
            piece(src, slots.at[1], base_send, base_recv + 1, me + 2, 0),
            piece(src, slots.at[1], base_send, second, me + 2, half),
        ]
        arrived = [
            piece(src, slots.at[1], base_send, base_recv + 1, me, 0),
            piece(src, slots.at[1], base_send, second, me, half),
        ]
        near = send(src, 2, me + 1, 1)
        relay_near = send(slots.at[1], 2, me - 1, 2)
        relay_far = send(slots.at[1], 0, me + 1, 3)
        relay_parts = [
            (
                piece(slots.at[1], slots.at[2], base_send + 2, base_recv + 2, me - 1, start),
                piece(slots.at[1], slots.at[0], base_send + 3, base_recv + 0, me + 1, start),
            )
            for start in (0, half)
        ]
        return (far, far_parts, arrived, relay_parts), near, relay_near, relay_far, incoming

    def start_first(far, near):
        @pl.when(me + 2 < count)
        def _():
            for part in far[1]:
                part.start()

        @pl.when(even)
        def _():
            near.start()

    def start_relay(far, relay_near, relay_far, incoming):
        @pl.when(me >= 2)
        def _():
            for arrived, (part_near, part_far) in zip(far[2], far[3]):
                arrived.wait_recv()

                @pl.when(odd)
                def _():
                    part_near.start()

                @pl.when(jnp.logical_or(even, me + 1 < count))
                def _():
                    part_far.start()

    def finish_sends(far, near, relay_near, relay_far):
        @pl.when(me + 2 < count)
        def _():
            far[0].wait_send()

        @pl.when(even)
        def _():
            near.wait_send()

        @pl.when((me >= 2) & odd)
        def _():
            relay_near.wait_send()

        @pl.when((me >= 2) & jnp.logical_or(even, me + 1 < count))
        def _():
            relay_far.wait_send()

    front = 8
    half = rows // 2
    for which in range(3):
        raw[which, pl.ds(0, front), :] = jnp.zeros((front, width), jnp.float32)
        raw[which, pl.ds(front, rows), :] = feats_ref[which].astype(jnp.float32)

    def mix(which, start, length):
        w = sf_ref[which]
        x = raw.at[which]
        return (
            w[0:1] * x[pl.ds(front + start, length), :]
            + w[1:2] * x[pl.ds(front + start - 1, length), :]
        ) + w[2:3] * x[pl.ds(front + start - 2, length), :]

    edge_stage[pl.ds(0, half), :] = (mix(1, half, half) * mix(2, half, half)).astype(
        edge_stage.dtype
    )
    for which in range(3):
        edge_stage[pl.ds(half + 16 * which, 16), :] = feats_ref[which, pl.ds(rows - 16, 16), :]
    staged = pltpu.make_async_copy(edge_stage, edge_send, copy_sem.at[1])
    staged.start()
    staged.wait()

    edge = pltpu.make_async_remote_copy(
        src_ref=edge_send, dst_ref=edge_slot, send_sem=send_sems.at[8],
        recv_sem=recv_sems.at[6], device_id={"ctx": me + 1}, device_id_type=MESH,
    )
    edge_in = pltpu.make_async_remote_copy(
        src_ref=edge_send, dst_ref=edge_slot, send_sem=send_sems.at[8],
        recv_sem=recv_sems.at[6], device_id={"ctx": me}, device_id_type=MESH,
    )

    @pl.when(me + 1 < count)
    def _():
        edge.start()

    k_far, k_near, k_relay_near, k_relay_far, k_incoming = route(kslots, k_ref, 0, 0, 7)
    start_first(k_far, k_near)

    @pl.when(me >= 1)
    def _():
        edge_in.wait_recv()

    for which in range(3):
        older = edge_slot[pl.ds(half + 16 * which, 16), :].astype(jnp.float32)
        raw[which, pl.ds(0, front), :] = older[16 - front :]

    qmix[...] = mix(0, 0, rows)
    ext[pl.ds(0, taps), :] = edge_slot[pl.ds(0, taps), :].astype(jnp.float32)
    ext[pl.ds(taps, rows), :] = (mix(1, 0, rows) * mix(2, 0, rows)).astype(
        jnp.bfloat16
    ).astype(jnp.float32)

    def chunk(c, carry):
        cols = pl.ds(pl.multiple_of(c * 128, 128), 128)
        for b in range(8):
            shifted[b, pl.ds(8, rows + taps - 8), :] = ext[pl.ds(8 - b, rows + taps - 8), cols]
        total = jnp.zeros((rows, 128), jnp.float32)
        for a in range(taps // 8):
            for b in range(8):
                j = 8 * a + b
                total = total + lf_ref[pl.ds(j, 1), cols] * shifted[b, pl.ds(taps - 8 * a, rows), :]
        gated = qmix[:, cols] * total
        hm_out[:, cols] = gated
        vsrc[:, cols] = gated.astype(vsrc.dtype)
        return carry

    lax.fori_loop(0, width // 128, chunk, 0)

    local = pltpu.make_async_copy(vsrc, vstage, copy_sem.at[0])
    local.start()
    local.wait()

    v_far, v_near, v_relay_near, v_relay_far, v_incoming = route(vslots, vstage, 4, 3, 8)
    start_first(v_far, v_near)
    start_relay(k_far, k_relay_near, k_relay_far, k_incoming)

    @pl.when(me >= 1)
    def _():
        k_incoming(2).wait_recv()

    @pl.when(me >= 3)
    def _():
        k_incoming(0).wait_recv()

    def score_head(h, carry):
        cols = pl.ds(pl.multiple_of(h * HEAD_DIM, HEAD_DIM), HEAD_DIM)
        q = q_ref[:, cols]
        parts = []
        for b, keys in enumerate((kslots.at[0], kslots.at[1], kslots.at[2], k_ref)):
            s = lax.dot_general(
                q, keys[:, cols], (((1,), (1,)), ((), ())), preferred_element_type=jnp.float32
            ) * scale
            t = lax.broadcasted_iota(jnp.int32, (rows, rows), 0)
            u = lax.broadcasted_iota(jnp.int32, (rows, rows), 1)
            if b == 3:
                visible = u <= t
            else:
                visible = jnp.broadcast_to(me - 3 + b >= 0, (rows, rows))
            parts.append(jnp.where(visible, s, -jnp.inf))
        masked = jnp.concatenate(parts, axis=1)
        peak = jnp.max(masked, axis=1, keepdims=True)
        w = jnp.exp(masked - peak)
        totals[h] = jnp.sum(w, axis=1, keepdims=True)
        weights[h] = w.astype(jnp.bfloat16)
        return carry

    lax.fori_loop(0, heads, score_head, 0)

    def accumulate(block, v_src, first):
        def one_head(h, carry):
            cols = pl.ds(pl.multiple_of(h * HEAD_DIM, HEAD_DIM), HEAD_DIM)
            w = weights[h, :, pl.ds(block * rows, rows)]
            part = jnp.dot(w, v_src[:, cols], preferred_element_type=jnp.float32)
            if first:
                acc[:, cols] = part
            else:
                acc[:, cols] = acc[:, cols] + part
            return carry

        lax.fori_loop(0, heads, one_head, 0)

    accumulate(3, vstage, True)
    start_relay(v_far, v_relay_near, v_relay_far, v_incoming)
    accumulate(1, vslots.at[1], False)

    @pl.when(me >= 1)
    def _():
        v_incoming(2).wait_recv()

    accumulate(2, vslots.at[2], False)

    @pl.when(me >= 3)
    def _():
        v_incoming(0).wait_recv()

    accumulate(0, vslots.at[0], False)

    def finish(h, carry):
        cols = pl.ds(pl.multiple_of(h * HEAD_DIM, HEAD_DIM), HEAD_DIM)
        out_ref[:, cols] = acc[:, cols] / totals[h]
        return carry

    lax.fori_loop(0, heads, finish, 0)

    @pl.when(me + 1 < count)
    def _():
        edge.wait_send()

    finish_sends(k_far, k_near, k_relay_near, k_relay_far)
    finish_sends(v_far, v_near, v_relay_near, v_relay_far)


def fused_call(keys, feats, short_filter, long_filter, query):
    count = lax.axis_size("ctx")
    rows, width = keys.shape
    taps = long_filter.shape[0]
    heads = width // HEAD_DIM
    edge_rows = rows // 2 + 48
    vmem = pl.BlockSpec(memory_space=pltpu.VMEM)
    return pl.pallas_call(
        functools.partial(fused_kernel, count),
        out_shape=(
            jax.ShapeDtypeStruct((rows, width), jnp.float32),
            jax.ShapeDtypeStruct((rows, width), jnp.float32),
        ),
        in_specs=[vmem] * 5,
        out_specs=(vmem, vmem),
        scratch_shapes=[
            pltpu.VMEM((edge_rows, width), jnp.bfloat16),
            pltpu.VMEM((edge_rows, width), jnp.bfloat16),
            pltpu.VMEM((edge_rows, width), jnp.bfloat16),
            pltpu.VMEM((3, rows, width), keys.dtype),
            pltpu.VMEM((3, rows, width), jnp.bfloat16),
            pltpu.VMEM((rows, width), jnp.bfloat16),
            pltpu.VMEM((rows, width), jnp.bfloat16),
            pltpu.VMEM((3, rows + 8, width), jnp.float32),
            pltpu.VMEM((rows, width), jnp.float32),
            pltpu.VMEM((rows + taps, width), jnp.float32),
            pltpu.VMEM((8, rows + taps, 128), jnp.float32),
            pltpu.VMEM((heads, rows, WINDOW_BLOCKS * rows), jnp.bfloat16),
            pltpu.VMEM((heads, rows, 1), jnp.float32),
            pltpu.VMEM((rows, width), jnp.float32),
            pltpu.SemaphoreType.DMA((9,)),
            pltpu.SemaphoreType.DMA((9,)),
            pltpu.SemaphoreType.DMA((2,)),
        ],
        compiler_params=pltpu.CompilerParams(
            collective_id=0, has_side_effects=True, vmem_limit_bytes=60 * 1024 * 1024
        ),
    )(keys, feats, short_filter, long_filter, query)


def round_kernel(gated_ref, attended_ref, hm_out, out_ref):
    hm_out[...] = gated_ref[...].astype(hm_out.dtype)
    out_ref[...] = attended_ref[...].astype(out_ref.dtype)


def round_outputs(gated, attended):
    vmem = pl.BlockSpec(memory_space=pltpu.VMEM)
    return pl.pallas_call(
        round_kernel,
        out_shape=(
            jax.ShapeDtypeStruct(gated.shape, jnp.bfloat16),
            jax.ShapeDtypeStruct(attended.shape, jnp.bfloat16),
        ),
        in_specs=[vmem] * 2,
        out_specs=(vmem, vmem),
    )(gated, attended)


def body(hyena_features, short_filter, long_filter, att_query, att_key):
    gated, attended = fused_call(att_key, hyena_features, short_filter, long_filter, att_query)
    return round_outputs(gated, attended)


def solution(mesh):
    return jax.shard_map(
        body,
        mesh=mesh,
        in_specs=(
            P(None, ("dp", "ctx"), "tp"),
            P(None, None, "tp"),
            P(None, "tp"),
            P(("dp", "ctx"), "tp"),
            P(("dp", "ctx"), "tp"),
        ),
        out_specs=(P(("dp", "ctx"), "tp"), P(("dp", "ctx"), "tp")),
        check_vma=False,
    )
```

```python
import functools
import math

import jax
import jax.numpy as jnp
from jax import lax
from jax.experimental import pallas as pl
from jax.experimental.pallas import tpu as pltpu
from jax.sharding import PartitionSpec as P

MESH = pl.DeviceIdType.MESH

HEAD_DIM = 128
WINDOW_BLOCKS = 4


def fused_kernel(
    count, k_ref, feats_ref, sf_ref, lf_ref, q_ref,
    hm_out, out_ref,
    edge_stage, edge_send, edge_slot, kslots, vslots, vsrc, vstage, raw, qmix, ext, shifted,
    weights, totals, acc, send_sems, recv_sems, copy_sem,
):
    me = lax.axis_index("ctx")
    odd = lax.rem(me, 2) == 1
    even = jnp.logical_not(odd)
    rows, width = k_ref.shape
    taps = lf_ref.shape[0]
    heads = width // HEAD_DIM
    scale = 1.0 / math.sqrt(HEAD_DIM)

    @pl.when(me < 3)
    def _():
        for slot, first in ((0, 3), (1, 2), (2, 1)):
            @pl.when(me < first)
            def _():
                kslots[slot] = jnp.zeros((rows, width), kslots.dtype)
                vslots[slot] = jnp.zeros((rows, width), vslots.dtype)

    @pl.when(me == 0)
    def _():
        edge_slot[...] = jnp.zeros(edge_slot.shape, edge_slot.dtype)

    barrier = pltpu.get_barrier_semaphore()
    for step in (-2, -1, 1, 2):
        peer = me + step

        @pl.when((peer >= 0) & (peer < count))
        def _():
            pl.semaphore_signal(barrier, inc=1, device_id={"ctx": peer}, device_id_type=MESH)

    neighbours = (
        (me >= 2).astype(jnp.int32) + (me >= 1).astype(jnp.int32)
        + (me + 1 < count).astype(jnp.int32) + (me + 2 < count).astype(jnp.int32)
    )
    pl.semaphore_wait(barrier, neighbours)

    def route(slots, src, base_send, base_recv, second):
        def send(source, slot, peer, sem):
            return pltpu.make_async_remote_copy(
                src_ref=source, dst_ref=slots.at[slot], send_sem=send_sems.at[base_send + sem],
                recv_sem=recv_sems.at[base_recv + slot], device_id={"ctx": peer},
                device_id_type=MESH,
            )

        def incoming(slot):
            return pltpu.make_async_remote_copy(
                src_ref=src, dst_ref=slots.at[slot], send_sem=send_sems.at[base_send],
                recv_sem=recv_sems.at[base_recv + slot], device_id={"ctx": me},
                device_id_type=MESH,
            )

        pieces = 4
        half = rows // pieces
        starts = [half * i for i in range(pieces)]
        landing = [base_recv + 1] + list(second)

        def piece(source, target, send_index, recv_index, peer, start):
            return pltpu.make_async_remote_copy(
                src_ref=source.at[pl.ds(start, half)], dst_ref=target.at[pl.ds(start, half)],
                send_sem=send_sems.at[send_index], recv_sem=recv_sems.at[recv_index],
                device_id={"ctx": peer}, device_id_type=MESH,
            )

        far = send(src, 1, me + 2, 0)
        far_parts = [
            piece(src, slots.at[1], base_send, sem, me + 2, start)
            for sem, start in zip(landing, starts)
        ]
        arrived = [
            piece(src, slots.at[1], base_send, sem, me, start)
            for sem, start in zip(landing, starts)
        ]
        near = send(src, 2, me + 1, 1)
        relay_near = send(slots.at[1], 2, me - 1, 2)
        relay_far = send(slots.at[1], 0, me + 1, 3)
        relay_parts = [
            (
                piece(slots.at[1], slots.at[2], base_send + 2, base_recv + 2, me - 1, start),
                piece(slots.at[1], slots.at[0], base_send + 3, base_recv + 0, me + 1, start),
            )
            for start in starts
        ]
        return (far, far_parts, arrived, relay_parts), near, relay_near, relay_far, incoming

    def start_first(far, near):
        @pl.when(me + 2 < count)
        def _():
            for part in far[1]:
                part.start()

        @pl.when(even)
        def _():
            near.start()

    def start_relay(far, relay_near, relay_far, incoming):
        @pl.when(me >= 2)
        def _():
            for arrived, (part_near, part_far) in zip(far[2], far[3]):
                arrived.wait_recv()

                @pl.when(odd)
                def _():
                    part_near.start()

                @pl.when(jnp.logical_or(even, me + 1 < count))
                def _():
                    part_far.start()

    def finish_sends(far, near, relay_near, relay_far):
        @pl.when(me + 2 < count)
        def _():
            far[0].wait_send()

        @pl.when(even)
        def _():
            near.wait_send()

        @pl.when((me >= 2) & odd)
        def _():
            relay_near.wait_send()

        @pl.when((me >= 2) & jnp.logical_or(even, me + 1 < count))
        def _():
            relay_far.wait_send()

    front = 8
    half = rows // 2
    for which in range(3):
        raw[which, pl.ds(0, front), :] = jnp.zeros((front, width), jnp.float32)
        raw[which, pl.ds(front, rows), :] = feats_ref[which].astype(jnp.float32)

    def mix(which, start, length):
        w = sf_ref[which]
        x = raw.at[which]
        return (
            w[0:1] * x[pl.ds(front + start, length), :]
            + w[1:2] * x[pl.ds(front + start - 1, length), :]
        ) + w[2:3] * x[pl.ds(front + start - 2, length), :]

    edge_stage[pl.ds(0, half), :] = (mix(1, half, half) * mix(2, half, half)).astype(
        edge_stage.dtype
    )
    for which in range(3):
        edge_stage[pl.ds(half + 16 * which, 16), :] = feats_ref[which, pl.ds(rows - 16, 16), :]
    staged = pltpu.make_async_copy(edge_stage, edge_send, copy_sem.at[1])
    staged.start()
    staged.wait()

    edge = pltpu.make_async_remote_copy(
        src_ref=edge_send, dst_ref=edge_slot, send_sem=send_sems.at[8],
        recv_sem=recv_sems.at[6], device_id={"ctx": me + 1}, device_id_type=MESH,
    )
    edge_in = pltpu.make_async_remote_copy(
        src_ref=edge_send, dst_ref=edge_slot, send_sem=send_sems.at[8],
        recv_sem=recv_sems.at[6], device_id={"ctx": me}, device_id_type=MESH,
    )

    @pl.when(me + 1 < count)
    def _():
        edge.start()

    k_far, k_near, k_relay_near, k_relay_far, k_incoming = route(kslots, k_ref, 0, 0, (7, 8, 9))
    start_first(k_far, k_near)

    @pl.when(me >= 1)
    def _():
        edge_in.wait_recv()

    for which in range(3):
        older = edge_slot[pl.ds(half + 16 * which, 16), :].astype(jnp.float32)
        raw[which, pl.ds(0, front), :] = older[16 - front :]

    qmix[...] = mix(0, 0, rows)
    ext[pl.ds(0, taps), :] = edge_slot[pl.ds(0, taps), :].astype(jnp.float32)
    ext[pl.ds(taps, rows), :] = (mix(1, 0, rows) * mix(2, 0, rows)).astype(
        jnp.bfloat16
    ).astype(jnp.float32)

    def chunk(c, carry):
        cols = pl.ds(pl.multiple_of(c * 128, 128), 128)
        for b in range(8):
            shifted[b, pl.ds(8, rows + taps - 8), :] = ext[pl.ds(8 - b, rows + taps - 8), cols]
        total = jnp.zeros((rows, 128), jnp.float32)
        for a in range(taps // 8):
            for b in range(8):
                j = 8 * a + b
                total = total + lf_ref[pl.ds(j, 1), cols] * shifted[b, pl.ds(taps - 8 * a, rows), :]
        gated = qmix[:, cols] * total
        hm_out[:, cols] = gated
        vsrc[:, cols] = gated.astype(vsrc.dtype)
        return carry

    lax.fori_loop(0, width // 128, chunk, 0)

    local = pltpu.make_async_copy(vsrc, vstage, copy_sem.at[0])
    local.start()
    local.wait()

    v_far, v_near, v_relay_near, v_relay_far, v_incoming = route(vslots, vstage, 4, 3, (10, 11, 12))
    start_first(v_far, v_near)
    start_relay(k_far, k_relay_near, k_relay_far, k_incoming)

    @pl.when(me >= 1)
    def _():
        k_incoming(2).wait_recv()

    @pl.when(me >= 3)
    def _():
        k_incoming(0).wait_recv()

    def score_head(h, carry):
        cols = pl.ds(pl.multiple_of(h * HEAD_DIM, HEAD_DIM), HEAD_DIM)
        q = q_ref[:, cols]
        parts = []
        for b, keys in enumerate((kslots.at[0], kslots.at[1], kslots.at[2], k_ref)):
            s = lax.dot_general(
                q, keys[:, cols], (((1,), (1,)), ((), ())), preferred_element_type=jnp.float32
            ) * scale
            t = lax.broadcasted_iota(jnp.int32, (rows, rows), 0)
            u = lax.broadcasted_iota(jnp.int32, (rows, rows), 1)
            if b == 3:
                visible = u <= t
            else:
                visible = jnp.broadcast_to(me - 3 + b >= 0, (rows, rows))
            parts.append(jnp.where(visible, s, -jnp.inf))
        masked = jnp.concatenate(parts, axis=1)
        peak = jnp.max(masked, axis=1, keepdims=True)
        w = jnp.exp(masked - peak)
        totals[h] = jnp.sum(w, axis=1, keepdims=True)
        weights[h] = w.astype(jnp.bfloat16)
        return carry

    lax.fori_loop(0, heads, score_head, 0)

    def accumulate(block, v_src, first):
        def one_head(h, carry):
            cols = pl.ds(pl.multiple_of(h * HEAD_DIM, HEAD_DIM), HEAD_DIM)
            w = weights[h, :, pl.ds(block * rows, rows)]
            part = jnp.dot(w, v_src[:, cols], preferred_element_type=jnp.float32)
            if first:
                acc[:, cols] = part
            else:
                acc[:, cols] = acc[:, cols] + part
            return carry

        lax.fori_loop(0, heads, one_head, 0)

    accumulate(3, vstage, True)
    start_relay(v_far, v_relay_near, v_relay_far, v_incoming)
    accumulate(1, vslots.at[1], False)

    @pl.when(me >= 1)
    def _():
        v_incoming(2).wait_recv()

    accumulate(2, vslots.at[2], False)

    @pl.when(me >= 3)
    def _():
        v_incoming(0).wait_recv()

    accumulate(0, vslots.at[0], False)

    def finish(h, carry):
        cols = pl.ds(pl.multiple_of(h * HEAD_DIM, HEAD_DIM), HEAD_DIM)
        out_ref[:, cols] = acc[:, cols] / totals[h]
        return carry

    lax.fori_loop(0, heads, finish, 0)

    @pl.when(me + 1 < count)
    def _():
        edge.wait_send()

    finish_sends(k_far, k_near, k_relay_near, k_relay_far)
    finish_sends(v_far, v_near, v_relay_near, v_relay_far)


def fused_call(keys, feats, short_filter, long_filter, query):
    count = lax.axis_size("ctx")
    rows, width = keys.shape
    taps = long_filter.shape[0]
    heads = width // HEAD_DIM
    edge_rows = rows // 2 + 48
    vmem = pl.BlockSpec(memory_space=pltpu.VMEM)
    return pl.pallas_call(
        functools.partial(fused_kernel, count),
        out_shape=(
            jax.ShapeDtypeStruct((rows, width), jnp.float32),
            jax.ShapeDtypeStruct((rows, width), jnp.float32),
        ),
        in_specs=[vmem] * 5,
        out_specs=(vmem, vmem),
        scratch_shapes=[
            pltpu.VMEM((edge_rows, width), jnp.bfloat16),
            pltpu.VMEM((edge_rows, width), jnp.bfloat16),
            pltpu.VMEM((edge_rows, width), jnp.bfloat16),
            pltpu.VMEM((3, rows, width), keys.dtype),
            pltpu.VMEM((3, rows, width), jnp.bfloat16),
            pltpu.VMEM((rows, width), jnp.bfloat16),
            pltpu.VMEM((rows, width), jnp.bfloat16),
            pltpu.VMEM((3, rows + 8, width), jnp.float32),
            pltpu.VMEM((rows, width), jnp.float32),
            pltpu.VMEM((rows + taps, width), jnp.float32),
            pltpu.VMEM((8, rows + taps, 128), jnp.float32),
            pltpu.VMEM((heads, rows, WINDOW_BLOCKS * rows), jnp.bfloat16),
            pltpu.VMEM((heads, rows, 1), jnp.float32),
            pltpu.VMEM((rows, width), jnp.float32),
            pltpu.SemaphoreType.DMA((9,)),
            pltpu.SemaphoreType.DMA((13,)),
            pltpu.SemaphoreType.DMA((2,)),
        ],
        compiler_params=pltpu.CompilerParams(
            collective_id=0, has_side_effects=True, vmem_limit_bytes=60 * 1024 * 1024
        ),
    )(keys, feats, short_filter, long_filter, query)


def round_kernel(gated_ref, attended_ref, hm_out, out_ref):
    hm_out[...] = gated_ref[...].astype(hm_out.dtype)
    out_ref[...] = attended_ref[...].astype(out_ref.dtype)


def round_outputs(gated, attended):
    vmem = pl.BlockSpec(memory_space=pltpu.VMEM)
    return pl.pallas_call(
        round_kernel,
        out_shape=(
            jax.ShapeDtypeStruct(gated.shape, jnp.bfloat16),
            jax.ShapeDtypeStruct(attended.shape, jnp.bfloat16),
        ),
        in_specs=[vmem] * 2,
        out_specs=(vmem, vmem),
    )(gated, attended)


def body(hyena_features, short_filter, long_filter, att_query, att_key):
    gated, attended = fused_call(att_key, hyena_features, short_filter, long_filter, att_query)
    return round_outputs(gated, attended)


def solution(mesh):
    return jax.shard_map(
        body,
        mesh=mesh,
        in_specs=(
            P(None, ("dp", "ctx"), "tp"),
            P(None, None, "tp"),
            P(None, "tp"),
            P(("dp", "ctx"), "tp"),
            P(("dp", "ctx"), "tp"),
        ),
        out_specs=(P(("dp", "ctx"), "tp"), P(("dp", "ctx"), "tp")),
        check_vma=False,
    )
```

```python
import functools
import math

import jax
import jax.numpy as jnp
from jax import lax
from jax.experimental import pallas as pl
from jax.experimental.pallas import tpu as pltpu
from jax.sharding import PartitionSpec as P

MESH = pl.DeviceIdType.MESH

HEAD_DIM = 128
WINDOW_BLOCKS = 4


def fused_kernel(
    count, k_ref, feats_ref, sf_ref, lf_ref, q_ref,
    hm_out, out_ref,
    edge_stage, edge_send, edge_slot, kslots, vslots, vsrc, vstage, raw, qmix, ext, shifted,
    weights, totals, acc, send_sems, recv_sems, copy_sem,
):
    me = lax.axis_index("ctx")
    odd = lax.rem(me, 2) == 1
    even = jnp.logical_not(odd)
    rows, width = k_ref.shape
    taps = lf_ref.shape[0]
    heads = width // HEAD_DIM
    scale = 1.0 / math.sqrt(HEAD_DIM)

    @pl.when(me < 3)
    def _():
        for slot, first in ((0, 3), (1, 2), (2, 1)):
            @pl.when(me < first)
            def _():
                kslots[slot] = jnp.zeros((rows, width), kslots.dtype)
                vslots[slot] = jnp.zeros((rows, width), vslots.dtype)

    @pl.when(me == 0)
    def _():
        edge_slot[...] = jnp.zeros(edge_slot.shape, edge_slot.dtype)

    barrier = pltpu.get_barrier_semaphore()
    for step in (-2, -1, 1, 2):
        peer = me + step

        @pl.when((peer >= 0) & (peer < count))
        def _():
            pl.semaphore_signal(barrier, inc=1, device_id={"ctx": peer}, device_id_type=MESH)

    neighbours = (
        (me >= 2).astype(jnp.int32) + (me >= 1).astype(jnp.int32)
        + (me + 1 < count).astype(jnp.int32) + (me + 2 < count).astype(jnp.int32)
    )
    pl.semaphore_wait(barrier, neighbours)

    def route(slots, src, base_send, base_recv, second):
        def send(source, slot, peer, sem):
            return pltpu.make_async_remote_copy(
                src_ref=source, dst_ref=slots.at[slot], send_sem=send_sems.at[base_send + sem],
                recv_sem=recv_sems.at[base_recv + slot], device_id={"ctx": peer},
                device_id_type=MESH,
            )

        def incoming(slot):
            return pltpu.make_async_remote_copy(
                src_ref=src, dst_ref=slots.at[slot], send_sem=send_sems.at[base_send],
                recv_sem=recv_sems.at[base_recv + slot], device_id={"ctx": me},
                device_id_type=MESH,
            )

        half = rows // 2

        def piece(source, target, send_index, recv_index, peer, start):
            return pltpu.make_async_remote_copy(
                src_ref=source.at[pl.ds(start, half)], dst_ref=target.at[pl.ds(start, half)],
                send_sem=send_sems.at[send_index], recv_sem=recv_sems.at[recv_index],
                device_id={"ctx": peer}, device_id_type=MESH,
            )

        far = send(src, 1, me + 2, 0)
        far_parts = [
            piece(src, slots.at[1], base_send, base_recv + 1, me + 2, 0),
            piece(src, slots.at[1], base_send, second, me + 2, half),
        ]
        arrived = [
            piece(src, slots.at[1], base_send, base_recv + 1, me, 0),
            piece(src, slots.at[1], base_send, second, me, half),
        ]
        near = send(src, 2, me + 1, 1)
        relay_near = send(slots.at[1], 2, me - 1, 2)
        relay_far = send(slots.at[1], 0, me + 1, 3)
        relay_parts = [
            (
                piece(slots.at[1], slots.at[2], base_send + 2, base_recv + 2, me - 1, start),
                piece(slots.at[1], slots.at[0], base_send + 3, base_recv + 0, me + 1, start),
            )
            for start in (0, half)
        ]
        return (far, far_parts, arrived, relay_parts), near, relay_near, relay_far, incoming

    def start_first(far, near):
        @pl.when(me + 2 < count)
        def _():
            for part in far[1]:
                part.start()

        @pl.when(even)
        def _():
            near.start()

    def start_relay(far, relay_near, relay_far, incoming):
        @pl.when(me >= 2)
        def _():
            for arrived, (part_near, part_far) in zip(far[2], far[3]):
                arrived.wait_recv()

                @pl.when(odd)
                def _():
                    part_near.start()

                @pl.when(jnp.logical_or(even, me + 1 < count))
                def _():
                    part_far.start()

    def finish_sends(far, near, relay_near, relay_far):
        @pl.when(me + 2 < count)
        def _():
            far[0].wait_send()

        @pl.when(even)
        def _():
            near.wait_send()

        @pl.when((me >= 2) & odd)
        def _():
            relay_near.wait_send()

        @pl.when((me >= 2) & jnp.logical_or(even, me + 1 < count))
        def _():
            relay_far.wait_send()

    front = 8
    half = rows // 2
    for which in range(3):
        raw[which, pl.ds(0, front), :] = jnp.zeros((front, width), jnp.float32)
        raw[which, pl.ds(front, rows), :] = feats_ref[which].astype(jnp.float32)

    def mix(which, start, length):
        w = sf_ref[which]
        x = raw.at[which]
        return (
            w[0:1] * x[pl.ds(front + start, length), :]
            + w[1:2] * x[pl.ds(front + start - 1, length), :]
        ) + w[2:3] * x[pl.ds(front + start - 2, length), :]

    edge_stage[pl.ds(0, half), :] = (mix(1, half, half) * mix(2, half, half)).astype(
        edge_stage.dtype
    )
    for which in range(3):
        edge_stage[pl.ds(half + 16 * which, 16), :] = feats_ref[which, pl.ds(rows - 16, 16), :]
    staged = pltpu.make_async_copy(edge_stage, edge_send, copy_sem.at[1])
    staged.start()
    staged.wait()

    edge = pltpu.make_async_remote_copy(
        src_ref=edge_send, dst_ref=edge_slot, send_sem=send_sems.at[8],
        recv_sem=recv_sems.at[6], device_id={"ctx": me + 1}, device_id_type=MESH,
    )
    edge_in = pltpu.make_async_remote_copy(
        src_ref=edge_send, dst_ref=edge_slot, send_sem=send_sems.at[8],
        recv_sem=recv_sems.at[6], device_id={"ctx": me}, device_id_type=MESH,
    )

    @pl.when(me + 1 < count)
    def _():
        edge.start()

    k_far, k_near, k_relay_near, k_relay_far, k_incoming = route(kslots, k_ref, 0, 0, 7)
    start_first(k_far, k_near)

    @pl.when(me >= 1)
    def _():
        edge_in.wait_recv()

    for which in range(3):
        older = edge_slot[pl.ds(half + 16 * which, 16), :].astype(jnp.float32)
        raw[which, pl.ds(0, front), :] = older[16 - front :]

    qmix[...] = mix(0, 0, rows)
    ext[pl.ds(0, taps), :] = edge_slot[pl.ds(0, taps), :].astype(jnp.float32)
    ext[pl.ds(taps, rows), :] = (mix(1, 0, rows) * mix(2, 0, rows)).astype(
        jnp.bfloat16
    ).astype(jnp.float32)

    def chunk(c, carry):
        cols = pl.ds(pl.multiple_of(c * 128, 128), 128)
        for b in range(8):
            shifted[b, pl.ds(8, rows + taps - 8), :] = ext[pl.ds(8 - b, rows + taps - 8), cols]
        total = jnp.zeros((rows, 128), jnp.float32)
        for a in range(taps // 8):
            for b in range(8):
                j = 8 * a + b
                total = total + lf_ref[pl.ds(j, 1), cols] * shifted[b, pl.ds(taps - 8 * a, rows), :]
        gated = (qmix[:, cols] * total).astype(vsrc.dtype)
        hm_out[:, cols] = gated
        vsrc[:, cols] = gated
        return carry

    lax.fori_loop(0, width // 128, chunk, 0)

    local = pltpu.make_async_copy(vsrc, vstage, copy_sem.at[0])
    local.start()
    local.wait()

    v_far, v_near, v_relay_near, v_relay_far, v_incoming = route(vslots, vstage, 4, 3, 8)
    start_first(v_far, v_near)
    start_relay(k_far, k_relay_near, k_relay_far, k_incoming)

    @pl.when(me >= 1)
    def _():
        k_incoming(2).wait_recv()

    @pl.when(me >= 3)
    def _():
        k_incoming(0).wait_recv()

    def score_head(h, carry):
        cols = pl.ds(pl.multiple_of(h * HEAD_DIM, HEAD_DIM), HEAD_DIM)
        q = q_ref[:, cols]
        parts = []
        for b, keys in enumerate((kslots.at[0], kslots.at[1], kslots.at[2], k_ref)):
            s = lax.dot_general(
                q, keys[:, cols], (((1,), (1,)), ((), ())), preferred_element_type=jnp.float32
            ) * scale
            t = lax.broadcasted_iota(jnp.int32, (rows, rows), 0)
            u = lax.broadcasted_iota(jnp.int32, (rows, rows), 1)
            if b == 3:
                visible = u <= t
            else:
                visible = jnp.broadcast_to(me - 3 + b >= 0, (rows, rows))
            parts.append(jnp.where(visible, s, -jnp.inf))
        masked = jnp.concatenate(parts, axis=1)
        peak = jnp.max(masked, axis=1, keepdims=True)
        w = jnp.exp(masked - peak)
        totals[h] = jnp.sum(w, axis=1, keepdims=True)
        weights[h] = w.astype(jnp.bfloat16)
        return carry

    lax.fori_loop(0, heads, score_head, 0)

    def accumulate(block, v_src, first):
        def one_head(h, carry):
            cols = pl.ds(pl.multiple_of(h * HEAD_DIM, HEAD_DIM), HEAD_DIM)
            w = weights[h, :, pl.ds(block * rows, rows)]
            part = jnp.dot(w, v_src[:, cols], preferred_element_type=jnp.float32)
            if first:
                acc[:, cols] = part
            else:
                acc[:, cols] = acc[:, cols] + part
            return carry

        lax.fori_loop(0, heads, one_head, 0)

    accumulate(3, vstage, True)
    start_relay(v_far, v_relay_near, v_relay_far, v_incoming)
    accumulate(1, vslots.at[1], False)

    @pl.when(me >= 1)
    def _():
        v_incoming(2).wait_recv()

    accumulate(2, vslots.at[2], False)

    @pl.when(me >= 3)
    def _():
        v_incoming(0).wait_recv()

    accumulate(0, vslots.at[0], False)

    def finish(h, carry):
        cols = pl.ds(pl.multiple_of(h * HEAD_DIM, HEAD_DIM), HEAD_DIM)
        out_ref[:, cols] = (acc[:, cols] / totals[h]).astype(out_ref.dtype)
        return carry

    lax.fori_loop(0, heads, finish, 0)

    @pl.when(me + 1 < count)
    def _():
        edge.wait_send()

    finish_sends(k_far, k_near, k_relay_near, k_relay_far)
    finish_sends(v_far, v_near, v_relay_near, v_relay_far)


def fused_call(keys, feats, short_filter, long_filter, query):
    count = lax.axis_size("ctx")
    rows, width = keys.shape
    taps = long_filter.shape[0]
    heads = width // HEAD_DIM
    edge_rows = rows // 2 + 48
    vmem = pl.BlockSpec(memory_space=pltpu.VMEM)
    return pl.pallas_call(
        functools.partial(fused_kernel, count),
        out_shape=(
            jax.ShapeDtypeStruct((rows, width), jnp.bfloat16),
            jax.ShapeDtypeStruct((rows, width), jnp.bfloat16),
        ),
        in_specs=[vmem] * 5,
        out_specs=(vmem, vmem),
        scratch_shapes=[
            pltpu.VMEM((edge_rows, width), jnp.bfloat16),
            pltpu.VMEM((edge_rows, width), jnp.bfloat16),
            pltpu.VMEM((edge_rows, width), jnp.bfloat16),
            pltpu.VMEM((3, rows, width), keys.dtype),
            pltpu.VMEM((3, rows, width), jnp.bfloat16),
            pltpu.VMEM((rows, width), jnp.bfloat16),
            pltpu.VMEM((rows, width), jnp.bfloat16),
            pltpu.VMEM((3, rows + 8, width), jnp.float32),
            pltpu.VMEM((rows, width), jnp.float32),
            pltpu.VMEM((rows + taps, width), jnp.float32),
            pltpu.VMEM((8, rows + taps, 128), jnp.float32),
            pltpu.VMEM((heads, rows, WINDOW_BLOCKS * rows), jnp.bfloat16),
            pltpu.VMEM((heads, rows, 1), jnp.float32),
            pltpu.VMEM((rows, width), jnp.float32),
            pltpu.SemaphoreType.DMA((9,)),
            pltpu.SemaphoreType.DMA((9,)),
            pltpu.SemaphoreType.DMA((2,)),
        ],
        compiler_params=pltpu.CompilerParams(
            collective_id=0, has_side_effects=True, vmem_limit_bytes=60 * 1024 * 1024
        ),
    )(keys, feats, short_filter, long_filter, query)


def round_kernel(gated_ref, attended_ref, hm_out, out_ref):
    hm_out[...] = gated_ref[...]
    out_ref[...] = attended_ref[...]


def round_outputs(gated, attended):
    vmem = pl.BlockSpec(memory_space=pltpu.VMEM)
    return pl.pallas_call(
        round_kernel,
        out_shape=(
            jax.ShapeDtypeStruct(gated.shape, jnp.bfloat16),
            jax.ShapeDtypeStruct(attended.shape, jnp.bfloat16),
        ),
        in_specs=[vmem] * 2,
        out_specs=(vmem, vmem),
    )(gated, attended)


def body(hyena_features, short_filter, long_filter, att_query, att_key):
    gated, attended = fused_call(att_key, hyena_features, short_filter, long_filter, att_query)
    return round_outputs(gated, attended)


def solution(mesh):
    return jax.shard_map(
        body,
        mesh=mesh,
        in_specs=(
            P(None, ("dp", "ctx"), "tp"),
            P(None, None, "tp"),
            P(None, "tp"),
            P(("dp", "ctx"), "tp"),
            P(("dp", "ctx"), "tp"),
        ),
        out_specs=(P(("dp", "ctx"), "tp"), P(("dp", "ctx"), "tp")),
        check_vma=False,
    )
```

```python
import functools
import math

import jax
import jax.numpy as jnp
from jax import lax
from jax.experimental import pallas as pl
from jax.experimental.pallas import tpu as pltpu
from jax.sharding import PartitionSpec as P

MESH = pl.DeviceIdType.MESH

HEAD_DIM = 128
WINDOW_BLOCKS = 4


def fused_kernel(
    count, k_ref, feats_ref, sf_ref, lf_ref, q_ref,
    hm_out, out_ref,
    edge_stage, edge_send, edge_slot, kslots, vslots, vsrc, vstage, raw, qmix, ext, shifted,
    weights, totals, acc, send_sems, recv_sems, copy_sem,
):
    me = lax.axis_index("ctx")
    odd = lax.rem(me, 2) == 1
    even = jnp.logical_not(odd)
    rows, width = k_ref.shape
    taps = lf_ref.shape[0]
    heads = width // HEAD_DIM
    scale = 1.0 / math.sqrt(HEAD_DIM)

    @pl.when(me < 3)
    def _():
        for slot, first in ((0, 3), (1, 2), (2, 1)):
            @pl.when(me < first)
            def _():
                kslots[slot] = jnp.zeros((rows, width), kslots.dtype)
                vslots[slot] = jnp.zeros((rows, width), vslots.dtype)

    @pl.when(me == 0)
    def _():
        edge_slot[...] = jnp.zeros(edge_slot.shape, edge_slot.dtype)

    barrier = pltpu.get_barrier_semaphore()
    for step in (-2, -1, 1, 2):
        peer = me + step

        @pl.when((peer >= 0) & (peer < count))
        def _():
            pl.semaphore_signal(barrier, inc=1, device_id={"ctx": peer}, device_id_type=MESH)

    neighbours = (
        (me >= 2).astype(jnp.int32) + (me >= 1).astype(jnp.int32)
        + (me + 1 < count).astype(jnp.int32) + (me + 2 < count).astype(jnp.int32)
    )
    pl.semaphore_wait(barrier, neighbours)

    def route(slots, src, base_send, base_recv, second):
        def send(source, slot, peer, sem):
            return pltpu.make_async_remote_copy(
                src_ref=source, dst_ref=slots.at[slot], send_sem=send_sems.at[base_send + sem],
                recv_sem=recv_sems.at[base_recv + slot], device_id={"ctx": peer},
                device_id_type=MESH,
            )

        def incoming(slot):
            return pltpu.make_async_remote_copy(
                src_ref=src, dst_ref=slots.at[slot], send_sem=send_sems.at[base_send],
                recv_sem=recv_sems.at[base_recv + slot], device_id={"ctx": me},
                device_id_type=MESH,
            )

        half = rows // 2

        def piece(source, target, send_index, recv_index, peer, start):
            return pltpu.make_async_remote_copy(
                src_ref=source.at[pl.ds(start, half)], dst_ref=target.at[pl.ds(start, half)],
                send_sem=send_sems.at[send_index], recv_sem=recv_sems.at[recv_index],
                device_id={"ctx": peer}, device_id_type=MESH,
            )

        far = send(src, 1, me + 2, 0)
        far_parts = [
            piece(src, slots.at[1], base_send, base_recv + 1, me + 2, 0),
            piece(src, slots.at[1], base_send, second, me + 2, half),
        ]
        arrived = [
            piece(src, slots.at[1], base_send, base_recv + 1, me, 0),
            piece(src, slots.at[1], base_send, second, me, half),
        ]
        near = send(src, 2, me + 1, 1)
        relay_near = send(slots.at[1], 2, me - 1, 2)
        relay_far = send(slots.at[1], 0, me + 1, 3)
        relay_parts = [
            (
                piece(slots.at[1], slots.at[2], base_send + 2, base_recv + 2, me - 1, start),
                piece(slots.at[1], slots.at[0], base_send + 3, base_recv + 0, me + 1, start),
            )
            for start in (0, half)
        ]
        return (far, far_parts, arrived, relay_parts), near, relay_near, relay_far, incoming

    def start_first(far, near):
        @pl.when(me + 2 < count)
        def _():
            for part in far[1]:
                part.start()

        @pl.when(even)
        def _():
            near.start()

    def start_relay(far, relay_near, relay_far, incoming):
        @pl.when(me >= 2)
        def _():
            for arrived, (part_near, part_far) in zip(far[2], far[3]):
                arrived.wait_recv()

                @pl.when(odd)
                def _():
                    part_near.start()

                @pl.when(jnp.logical_or(even, me + 1 < count))
                def _():
                    part_far.start()

    def finish_sends(far, near, relay_near, relay_far):
        @pl.when(me + 2 < count)
        def _():
            far[0].wait_send()

        @pl.when(even)
        def _():
            near.wait_send()

        @pl.when((me >= 2) & odd)
        def _():
            relay_near.wait_send()

        @pl.when((me >= 2) & jnp.logical_or(even, me + 1 < count))
        def _():
            relay_far.wait_send()

    front = 8
    half = rows // 2
    for which in range(3):
        raw[which, pl.ds(0, front), :] = jnp.zeros((front, width), jnp.float32)
        raw[which, pl.ds(front, rows), :] = feats_ref[which].astype(jnp.float32)

    def mix(which, start, length):
        w = sf_ref[which]
        x = raw.at[which]
        return (
            w[0:1] * x[pl.ds(front + start, length), :]
            + w[1:2] * x[pl.ds(front + start - 1, length), :]
        ) + w[2:3] * x[pl.ds(front + start - 2, length), :]

    edge_stage[pl.ds(0, half), :] = (mix(1, half, half) * mix(2, half, half)).astype(
        edge_stage.dtype
    )
    line = lax.broadcasted_iota(jnp.int32, (16, width), 0)
    packed = jnp.zeros((16, width), jnp.float32)
    for which in range(3):
        last = feats_ref[which, pl.ds(rows - 16, 16), :].astype(jnp.float32)
        for r in range(2):
            packed = jnp.where(line == 2 * which + r, last[14 + r : 15 + r], packed)
    edge_stage[pl.ds(half, 16), :] = packed.astype(edge_stage.dtype)
    staged = pltpu.make_async_copy(edge_stage, edge_send, copy_sem.at[1])
    staged.start()
    staged.wait()

    edge = pltpu.make_async_remote_copy(
        src_ref=edge_send, dst_ref=edge_slot, send_sem=send_sems.at[8],
        recv_sem=recv_sems.at[6], device_id={"ctx": me + 1}, device_id_type=MESH,
    )
    edge_in = pltpu.make_async_remote_copy(
        src_ref=edge_send, dst_ref=edge_slot, send_sem=send_sems.at[8],
        recv_sem=recv_sems.at[6], device_id={"ctx": me}, device_id_type=MESH,
    )

    @pl.when(me + 1 < count)
    def _():
        edge.start()

    k_far, k_near, k_relay_near, k_relay_far, k_incoming = route(kslots, k_ref, 0, 0, 7)
    start_first(k_far, k_near)

    @pl.when(me >= 1)
    def _():
        edge_in.wait_recv()

    older = edge_slot[pl.ds(half, 16), :].astype(jnp.float32)
    line = lax.broadcasted_iota(jnp.int32, (front, width), 0)
    for which in range(3):
        tile = jnp.zeros((front, width), jnp.float32)
        for r in range(2):
            tile = jnp.where(line == front - 2 + r, older[2 * which + r : 2 * which + r + 1], tile)
        raw[which, pl.ds(0, front), :] = tile

    qmix[...] = mix(0, 0, rows)
    ext[pl.ds(0, taps), :] = edge_slot[pl.ds(0, taps), :].astype(jnp.float32)
    ext[pl.ds(taps, rows), :] = (mix(1, 0, rows) * mix(2, 0, rows)).astype(
        jnp.bfloat16
    ).astype(jnp.float32)

    def chunk(c, carry):
        cols = pl.ds(pl.multiple_of(c * 128, 128), 128)
        for b in range(8):
            shifted[b, pl.ds(8, rows + taps - 8), :] = ext[pl.ds(8 - b, rows + taps - 8), cols]
        total = jnp.zeros((rows, 128), jnp.float32)
        for a in range(taps // 8):
            for b in range(8):
                j = 8 * a + b
                total = total + lf_ref[pl.ds(j, 1), cols] * shifted[b, pl.ds(taps - 8 * a, rows), :]
        gated = (qmix[:, cols] * total).astype(vsrc.dtype)
        hm_out[:, cols] = gated
        vsrc[:, cols] = gated
        return carry

    lax.fori_loop(0, width // 128, chunk, 0)

    local = pltpu.make_async_copy(vsrc, vstage, copy_sem.at[0])
    local.start()
    local.wait()

    v_far, v_near, v_relay_near, v_relay_far, v_incoming = route(vslots, vstage, 4, 3, 8)
    start_first(v_far, v_near)
    start_relay(k_far, k_relay_near, k_relay_far, k_incoming)

    @pl.when(me >= 1)
    def _():
        k_incoming(2).wait_recv()

    @pl.when(me >= 3)
    def _():
        k_incoming(0).wait_recv()

    def score_head(h, carry):
        cols = pl.ds(pl.multiple_of(h * HEAD_DIM, HEAD_DIM), HEAD_DIM)
        q = q_ref[:, cols]
        parts = []
        for b, keys in enumerate((kslots.at[0], kslots.at[1], kslots.at[2], k_ref)):
            s = lax.dot_general(
                q, keys[:, cols], (((1,), (1,)), ((), ())), preferred_element_type=jnp.float32
            ) * scale
            t = lax.broadcasted_iota(jnp.int32, (rows, rows), 0)
            u = lax.broadcasted_iota(jnp.int32, (rows, rows), 1)
            if b == 3:
                visible = u <= t
            else:
                visible = jnp.broadcast_to(me - 3 + b >= 0, (rows, rows))
            parts.append(jnp.where(visible, s, -jnp.inf))
        masked = jnp.concatenate(parts, axis=1)
        peak = jnp.max(masked, axis=1, keepdims=True)
        w = jnp.exp(masked - peak)
        totals[h] = jnp.sum(w, axis=1, keepdims=True)
        weights[h] = w.astype(jnp.bfloat16)
        return carry

    lax.fori_loop(0, heads, score_head, 0)

    def accumulate(block, v_src, first):
        def one_head(h, carry):
            cols = pl.ds(pl.multiple_of(h * HEAD_DIM, HEAD_DIM), HEAD_DIM)
            w = weights[h, :, pl.ds(block * rows, rows)]
            part = jnp.dot(w, v_src[:, cols], preferred_element_type=jnp.float32)
            if first:
                acc[:, cols] = part
            else:
                acc[:, cols] = acc[:, cols] + part
            return carry

        lax.fori_loop(0, heads, one_head, 0)

    accumulate(3, vstage, True)
    start_relay(v_far, v_relay_near, v_relay_far, v_incoming)
    accumulate(1, vslots.at[1], False)

    @pl.when(me >= 1)
    def _():
        v_incoming(2).wait_recv()

    accumulate(2, vslots.at[2], False)

    @pl.when(me >= 3)
    def _():
        v_incoming(0).wait_recv()

    accumulate(0, vslots.at[0], False)

    def finish(h, carry):
        cols = pl.ds(pl.multiple_of(h * HEAD_DIM, HEAD_DIM), HEAD_DIM)
        out_ref[:, cols] = (acc[:, cols] / totals[h]).astype(out_ref.dtype)
        return carry

    lax.fori_loop(0, heads, finish, 0)

    @pl.when(me + 1 < count)
    def _():
        edge.wait_send()

    finish_sends(k_far, k_near, k_relay_near, k_relay_far)
    finish_sends(v_far, v_near, v_relay_near, v_relay_far)


def fused_call(keys, feats, short_filter, long_filter, query):
    count = lax.axis_size("ctx")
    rows, width = keys.shape
    taps = long_filter.shape[0]
    heads = width // HEAD_DIM
    edge_rows = rows // 2 + 16
    vmem = pl.BlockSpec(memory_space=pltpu.VMEM)
    return pl.pallas_call(
        functools.partial(fused_kernel, count),
        out_shape=(
            jax.ShapeDtypeStruct((rows, width), jnp.bfloat16),
            jax.ShapeDtypeStruct((rows, width), jnp.bfloat16),
        ),
        in_specs=[vmem] * 5,
        out_specs=(vmem, vmem),
        scratch_shapes=[
            pltpu.VMEM((edge_rows, width), jnp.bfloat16),
            pltpu.VMEM((edge_rows, width), jnp.bfloat16),
            pltpu.VMEM((edge_rows, width), jnp.bfloat16),
            pltpu.VMEM((3, rows, width), keys.dtype),
            pltpu.VMEM((3, rows, width), jnp.bfloat16),
            pltpu.VMEM((rows, width), jnp.bfloat16),
            pltpu.VMEM((rows, width), jnp.bfloat16),
            pltpu.VMEM((3, rows + 8, width), jnp.float32),
            pltpu.VMEM((rows, width), jnp.float32),
            pltpu.VMEM((rows + taps, width), jnp.float32),
            pltpu.VMEM((8, rows + taps, 128), jnp.float32),
            pltpu.VMEM((heads, rows, WINDOW_BLOCKS * rows), jnp.bfloat16),
            pltpu.VMEM((heads, rows, 1), jnp.float32),
            pltpu.VMEM((rows, width), jnp.float32),
            pltpu.SemaphoreType.DMA((9,)),
            pltpu.SemaphoreType.DMA((9,)),
            pltpu.SemaphoreType.DMA((2,)),
        ],
        compiler_params=pltpu.CompilerParams(
            collective_id=0, has_side_effects=True, vmem_limit_bytes=60 * 1024 * 1024
        ),
    )(keys, feats, short_filter, long_filter, query)


def round_kernel(gated_ref, attended_ref, hm_out, out_ref):
    hm_out[...] = gated_ref[...]
    out_ref[...] = attended_ref[...]


def round_outputs(gated, attended):
    vmem = pl.BlockSpec(memory_space=pltpu.VMEM)
    return pl.pallas_call(
        round_kernel,
        out_shape=(
            jax.ShapeDtypeStruct(gated.shape, jnp.bfloat16),
            jax.ShapeDtypeStruct(attended.shape, jnp.bfloat16),
        ),
        in_specs=[vmem] * 2,
        out_specs=(vmem, vmem),
    )(gated, attended)


def body(hyena_features, short_filter, long_filter, att_query, att_key):
    gated, attended = fused_call(att_key, hyena_features, short_filter, long_filter, att_query)
    return round_outputs(gated, attended)


def solution(mesh):
    return jax.shard_map(
        body,
        mesh=mesh,
        in_specs=(
            P(None, ("dp", "ctx"), "tp"),
            P(None, None, "tp"),
            P(None, "tp"),
            P(("dp", "ctx"), "tp"),
            P(("dp", "ctx"), "tp"),
        ),
        out_specs=(P(("dp", "ctx"), "tp"), P(("dp", "ctx"), "tp")),
        check_vma=False,
    )
```
